32 devices in a mesh: batch: 2 (over y), seq: 16 (over z, x, core).
Axes of the slice: x: 2, y: 2, z: 4, core: 2. Of those that a mesh axis runs over, the one named last changes fastest.
Arguments:
- block_input: bfloat16 [2, 2048, 1536], P('batch', 'seq'), may hold values from -6 to 6
- positions: int32 [2, 2048], P('batch', 'seq'), may hold values from 0 to 3070, as said below
- needle: int32 [2, 2048], P('batch', 'seq'), may hold values 0 or 1
- cotangent: bfloat16 [2, 2048, 1536], P('batch', 'seq'), may hold values from -6 to 6
- norm_gain1: float32 [1536], replicated, may hold values from 0.25 to 1.75
- w_query: bfloat16 [1536, 1536], P('seq'), may hold values from -0.21875 to 0.21875
- w_key: bfloat16 [1536, 1536], P('seq'), may hold values from -0.21875 to 0.21875
- w_value: bfloat16 [1536, 1536], P('seq'), may hold values from -0.15625 to 0.15625
- lam_q1: float32 [12, 64], replicated, may hold values from -0.6 to 0.6
- lam_k1: float32 [12, 64], replicated, may hold values from -0.6 to 0.6
- lam_q2: float32 [12, 64], replicated, may hold values from -0.6 to 0.6
- lam_k2: float32 [12, 64], replicated, may hold values from -0.6 to 0.6
- sub_gain: float32 [128], replicated, may hold values from 0.25 to 1.75
- w_out: bfloat16 [1536, 1536], P('seq'), may hold values from -0.375 to 0.375
- norm_gain2: float32 [1536], replicated, may hold values from 0.25 to 1.75
- w_gate: bfloat16 [1536, 4096], P('seq'), may hold values from -0.15625 to 0.15625
- w_up: bfloat16 [1536, 4096], P('seq'), may hold values from -0.15625 to 0.15625
- w_down: bfloat16 [1536, 4096], P('seq'), may hold values from -0.125 to 0.125
Outputs:
- output: bfloat16 [2, 2048, 1536], P('batch', 'seq')
- input_grad: float32 [2, 2048, 1536], P('batch', 'seq')
- gain1_grad: float32 [1536], replicated
- query_grad: float32 [1536, 1536], P('seq')
- key_grad: float32 [1536, 1536], P('seq')
- value_grad: float32 [1536, 1536], P('seq')
- lam_q1_grad: float32 [12, 64], replicated
- lam_k1_grad: float32 [12, 64], replicated
- lam_q2_grad: float32 [12, 64], replicated
- lam_k2_grad: float32 [12, 64], replicated
- sub_gain_grad: float32 [128], replicated
- out_grad: float32 [1536, 1536], P('seq')
- gain2_grad: float32 [1536], replicated
- gate_grad: float32 [1536, 4096], P('seq')
- up_grad: float32 [1536, 4096], P('seq')
- down_grad: float32 [1536, 4096], P('seq')
- lam_mean: float32 [], replicated
- lam_grad_norm: float32 [], replicated
The draws below stay inside these ranges and needn't reach their ends.
Inputs may be any that keep to these rules, and one draw needn't show every extreme that they name: Along each sequence the positions start at 0 and rise by 1 or 2 from token to token, by 2 at exactly (2047) // 2 of the steps, so that every sequence ends at the maximum.
All inputs are finite; a program needn't handle non-finite values. No bound on the sum of `needle` on one device may be relied on, other than what follows from the above.
Results may differ from the reference program's by a relative error of at most 0.02.
Values may be sent and summed in bfloat16 or wider, within the bound.
A program may use at most 448 MiB of HBM per device.

```python
import math
import jax
import jax.numpy as jnp
from jax import lax

D = 1536
H = 12
HD = 64
VD = 128
FF = 4096
SEQS = 2
LENGTH = 2048


def one_row(row_key):
    order = jax.random.permutation(row_key, LENGTH - 1)
    steps = (1 + (order < (LENGTH - 1) // 2).astype(jnp.int32)).astype(jnp.int32)
    return jnp.concatenate([jnp.zeros((1,), jnp.int32), jnp.cumsum(steps).astype(jnp.int32)])


def draw_positions(key, part):
    row_keys = jax.random.split(jax.random.fold_in(key, 17), SEQS)
    return jax.vmap(one_row)(row_keys).astype(jnp.int32)


def with_ends(drawn, key, least, largest):
    longest = drawn.shape.index(max(drawn.shape))
    spots = []
    for shift in (0, 1):
        where = [jax.random.randint(jax.random.fold_in(key, axis), (), 0, length) for axis, length in enumerate(drawn.shape)]
        where[longest] = (where[longest] + shift) % drawn.shape[longest]
        spots.append(tuple(where))
    return drawn.at[spots[0]].set(least).at[spots[1]].set(largest)


def block_scale(own_key, shape, shards, low, high):
    loudness = 1.0
    for position, blocks in shards:
        draws = jax.random.uniform(jax.random.fold_in(jax.random.fold_in(own_key, 6), position), (blocks,), jnp.float32, low / len(shards), high / len(shards))
        loudness = loudness * jnp.repeat(jnp.exp(draws), shape[position] // blocks).reshape((-1,) + (1,) * (len(shape) - 1 - position))
    return loudness


def scatter_about(rng, dims, scale, most, cuts=(), kind=jnp.bfloat16):
    drawn = scale * jax.random.normal(rng, dims, jnp.float32)
    if cuts:
        drawn = drawn * block_scale(rng, dims, cuts, -0.22, 0.18)
    return jnp.clip(drawn, -most, most).astype(kind)


def setup_inputs(seed: int = 0) -> dict:
    arg_keys = jax.random.split(jax.random.key(seed), 19)
    return {
        "block_input": scatter_about(arg_keys[0], (SEQS, LENGTH, D), 1.0, 6.0, ((0, 2), (1, 16))),
        "positions": draw_positions(jax.random.fold_in(arg_keys[18], 71), 0),
        "needle": with_ends((jax.random.randint(arg_keys[2], (SEQS, LENGTH), 0, 2) < 1).astype(jnp.int32), jax.random.fold_in(arg_keys[2], 1), 0, 1),
        "cotangent": scatter_about(arg_keys[3], (SEQS, LENGTH, D), 1.0, 6.0, ((0, 2), (1, 16))),
        "norm_gain1": jnp.clip(1.0 + 0.15 * jax.random.normal(arg_keys[4], (D,), jnp.float32), 0.25, 1.75),
        "w_query": scatter_about(arg_keys[5], (D, D), (D // 2) ** -0.5, 0.21875, ((0, 16),)),
        "w_key": scatter_about(arg_keys[6], (D, D), (D // 2) ** -0.5, 0.21875, ((0, 16),)),
        "w_value": scatter_about(arg_keys[7], (D, D), D ** -0.5, 0.15625, ((0, 16),)),
        "lam_q1": scatter_about(arg_keys[8], (H, HD), 0.15, 0.6, (), jnp.float32),
        "lam_k1": scatter_about(arg_keys[9], (H, HD), 0.15, 0.6, (), jnp.float32),
        "lam_q2": scatter_about(arg_keys[10], (H, HD), 0.15, 0.6, (), jnp.float32),
        "lam_k2": scatter_about(arg_keys[11], (H, HD), 0.15, 0.6, (), jnp.float32),
        "sub_gain": jnp.clip(1.0 + 0.15 * jax.random.normal(arg_keys[12], (VD,), jnp.float32), 0.25, 1.75),
        "w_out": scatter_about(arg_keys[13], (D, D), (D // 6) ** -0.5, 0.375, ((0, 16),)),
        "norm_gain2": jnp.clip(1.0 + 0.15 * jax.random.normal(arg_keys[14], (D,), jnp.float32), 0.25, 1.75),
        "w_gate": scatter_about(arg_keys[15], (D, FF), D ** -0.5, 0.15625, ((0, 16),)),
        "w_up": scatter_about(arg_keys[16], (D, FF), D ** -0.5, 0.15625, ((0, 16),)),
        "w_down": scatter_about(arg_keys[17], (D, FF), (FF // 2) ** -0.5, 0.125, ((0, 16),)),
    }


@jax.custom_vjp
def low(v):
    return lax.optimization_barrier(v.astype(jnp.bfloat16)).astype(jnp.float32)

@jax.custom_vjp
def low_back(v):
    return v

def low_keep(v):
    return (low(v), None)

def low_pass(kept, grad):
    return (grad,)

def back_keep(v):
    return (v, None)

def back_low(kept, grad):
    return (low(grad),)
low.defvjp(low_keep, low_pass)
low_back.defvjp(back_keep, back_low)
lam_init = 0.619
norm_eps = 1e-05
precise = lax.Precision.HIGHEST

def rms_norm(value, gain):
    factor = lax.rsqrt(lax.optimization_barrier(jnp.mean(value * value, axis=-1, keepdims=True)) + norm_eps)
    return value * factor * gain

def rotate(value, angles):
    middle = value.shape[-1] // 2
    first_half = value[..., :middle]
    second_half = value[..., middle:]
    cosine = jnp.cos(angles)[:, None, None, :]
    sine = jnp.sin(angles)[:, None, None, :]
    return jnp.concatenate([first_half * cosine - second_half * sine, second_half * cosine + first_half * sine], axis=-1)

def lambdas(lam_q1, lam_k1, lam_q2, lam_k2):
    return jnp.exp(lax.optimization_barrier(jnp.sum(lam_q1 * lam_k1, axis=-1))) - jnp.exp(lax.optimization_barrier(jnp.sum(lam_q2 * lam_k2, axis=-1))) + lam_init

def sequence_forward(params, tokens, angles):
    gain_one, w_q, w_k, w_v, lq_one, lk_one, lq_two, lk_two, gain_sub, w_o, gain_two, w_g, w_u, w_d = params
    length = tokens.shape[0]
    normed = low(rms_norm(tokens, gain_one))
    query = low_back(jnp.dot(normed, w_q, precision=precise))
    keyed = low_back(jnp.dot(normed, w_k, precision=precise))
    values = low_back(low(jnp.dot(normed, w_v, precision=precise)))
    query = low(rotate(query.reshape(length, H, 2, HD), angles))
    keyed = low(rotate(keyed.reshape(length, H, 2, HD), angles))
    values = values.reshape(length, H, VD)
    lam_vals = lambdas(lq_one, lk_one, lq_two, lk_two)
    block_rows = math.gcd(length, 512)
    key_ids = jnp.arange(length, dtype=jnp.int32)

    def attend(start_row):
        query_block = lax.dynamic_slice_in_dim(query, start_row, block_rows, 0)
        query_ids = start_row + jnp.arange(block_rows, dtype=jnp.int32)
        allowed = key_ids[None, :] <= query_ids[:, None]
        map_outs = []
        for map_index in range(2):
            scores = jnp.einsum('qhd,khd->hqk', query_block[:, :, map_index], keyed[:, :, map_index], precision=precise)
            scores = low_back(scores * HD ** (-0.5))
            scores = jnp.where(allowed[None], scores, -1e+30)
            weights = low(jax.nn.softmax(scores, axis=-1))
            map_outs.append(jnp.einsum('hqk,khe->qhe', weights, values, precision=precise))
        mixed = low_back(map_outs[0] - lam_vals[None, :, None] * map_outs[1])
        return rms_norm(mixed, gain_sub) * (1.0 - lam_init)
    starts = (jnp.arange(length // block_rows, dtype=jnp.int32) * block_rows).astype(jnp.int32)
    attended = lax.map(jax.checkpoint(attend), starts)
    attended = low(attended.reshape(length, H * VD))
    resid = tokens + low_back(jnp.dot(attended, w_o, precision=precise))
    normed_two = low(rms_norm(resid, gain_two))
    gate = low_back(jnp.dot(normed_two, w_g, precision=precise))
    upper = low_back(jnp.dot(normed_two, w_u, precision=precise))
    inner = low(jax.nn.silu(gate) * upper)
    return resid + low_back(jnp.dot(inner, w_d.T, precision=precise))

def reference(block_input, positions, needle, cotangent, norm_gain1, w_query, w_key, w_value, lam_q1, lam_k1, lam_q2, lam_k2, sub_gain, w_out, norm_gain2, w_gate, w_up, w_down):
    params = tuple((param.astype(jnp.float32) for param in (norm_gain1, w_query, w_key, w_value, lam_q1, lam_k1, lam_q2, lam_k2, sub_gain, w_out, norm_gain2, w_gate, w_up, w_down)))
    inv_freq = jnp.exp(-math.log(10000.0) * jnp.arange(HD // 2, dtype=jnp.float32) / (HD // 2))

    def one_sequence(totals, inputs):
        tokens, places, needle_row, cotangent_row = inputs
        angles = places.astype(jnp.float32)[:, None] * inv_freq[None, :]
        result, pullback = jax.vjp(lambda param_set, token_set: sequence_forward(param_set, token_set, angles), params, tokens.astype(jnp.float32))
        param_grads, token_grad = pullback(cotangent_row.astype(jnp.float32) * needle_row.astype(jnp.float32)[:, None])
        totals = jax.tree.map(jnp.add, totals, param_grads)
        return (totals, (result.astype(jnp.bfloat16), token_grad))
    zero_grads = jax.tree.map(jnp.zeros_like, params)
    totals, (outputs, input_grads) = lax.scan(one_sequence, zero_grads, (block_input, positions, needle, cotangent))
    lam_vals = lambdas(params[4], params[5], params[6], params[7])
    squares = jnp.sum(totals[4] ** 2) + jnp.sum(totals[5] ** 2) + jnp.sum(totals[6] ** 2) + jnp.sum(totals[7] ** 2)
    return (outputs, input_grads, totals[0], totals[1], totals[2], totals[3], totals[4], totals[5], totals[6], totals[7], totals[8], totals[9], totals[10], totals[11], totals[12], totals[13], jnp.mean(lam_vals), jnp.sqrt(squares))
```

```python
import functools
import math

import jax
import jax.numpy as jnp
from jax import lax
from jax.experimental import pallas as pl
from jax.experimental.pallas import tpu as pltpu
from jax.sharding import PartitionSpec as P

lam_init = 0.619
norm_eps = 1e-05
log2e = math.log2(math.e)
neg_large = -1e30
f32 = jnp.float32
bf16 = jnp.bfloat16


def lambdas(lam_q1, lam_k1, lam_q2, lam_k2):
    return (
        jnp.exp(jnp.sum(lam_q1 * lam_k1, axis=-1))
        - jnp.exp(jnp.sum(lam_q2 * lam_k2, axis=-1))
        + lam_init
    )


def dims(left_axis, right_axis):
    return (((left_axis,), (right_axis,)), ((), ()))


def dot(left, right, left_axis=1, right_axis=0):
    return lax.dot_general(left, right, dims(left_axis, right_axis), preferred_element_type=f32)


def rotated(value, cosine, sine, inverse=False):
    parts = []
    step = cosine.shape[0]
    sign = -1.0 if inverse else 1.0
    for start in range(0, value.shape[0], 2 * step):
        first = value[start : start + step]
        second = value[start + step : start + 2 * step]
        parts.append(first * cosine - sign * (second * sine))
        parts.append(second * cosine + sign * (first * sine))
    return jnp.concatenate(parts, axis=0)


def forward_kernel(
    block, lam_ref, qkv_ref, cos_ref, sin_ref, gain_ref,
    q_ref, k_ref, v_ref, kt_ref, o1_ref, o2_ref, lse_ref, att_ref,
    qt_ref, vt_ref,
):
    step = pl.program_id(0)
    width = v_ref.shape[1]
    half = width // 2
    length = q_ref.shape[0]
    scale = half ** -0.5 * log2e

    @pl.when(step == 0)
    def _():
        def prepare(index, carry):
            cols = pl.ds(pl.multiple_of(index * block, block), block)
            cosine, sine = cos_ref[:, cols], sin_ref[:, cols]
            query = rotated(qkv_ref[0:width, cols], cosine, sine)
            key = rotated(qkv_ref[width : 2 * width, cols], cosine, sine)
            value = qkv_ref[2 * width : 3 * width, cols]
            qt_ref[:, cols] = query.astype(bf16)
            kt_ref[:, cols] = key.astype(bf16)
            vt_ref[:, cols] = value.astype(bf16)
            q_ref[cols, :] = query.T.astype(bf16)
            k_ref[cols, :] = key.T.astype(bf16)
            v_ref[cols, :] = value.T.astype(bf16)
            return carry

        lax.fori_loop(0, length // block, prepare, 0)

    own = pl.ds(pl.multiple_of(step * block, block), block)
    queries = qt_ref[:, own]
    key_ids = lax.broadcasted_iota(jnp.int32, (block, block), 0)
    query_ids = lax.broadcasted_iota(jnp.int32, (block, block), 1)

    def visit(index, state, diagonal):
        rows = pl.ds(pl.multiple_of(index * block, block), block)
        values = vt_ref[:, rows]
        out = []
        for part in range(2):
            top, total, acc = state[part]
            lo, hi = part * half, (part + 1) * half
            scores = dot(k_ref[rows, lo:hi], queries[lo:hi]) * scale
            if diagonal:
                scores = jnp.where(key_ids <= query_ids, scores, neg_large)
            new_top = jnp.maximum(top, jnp.max(scores, axis=0, keepdims=True))
            weights = jnp.exp2(scores - new_top)
            fade = jnp.exp2(top - new_top)
            total = total * fade + jnp.sum(weights, axis=0, keepdims=True)
            acc = acc * fade + dot(values, weights.astype(bf16))
            out.append((new_top, total, acc))
        return tuple(out)

    start = tuple(
        (
            jnp.full((1, block), neg_large, f32),
            jnp.zeros((1, block), f32),
            jnp.zeros((width, block), f32),
        )
        for _ in range(2)
    )
    state = lax.fori_loop(0, step, lambda index, now: visit(index, now, False), start)
    state = visit(step, state, True)
    outs = []
    for part, ref in ((0, o1_ref), (1, o2_ref)):
        top, total, acc = state[part]
        result = acc / total
        ref[:, own] = result
        lse_ref[pl.ds(part, 1), own] = top + jnp.log2(total)
        outs.append(result)
    mixed = outs[0] - lam_ref[0] * outs[1]
    factor = lax.rsqrt(jnp.mean(mixed * mixed, axis=0, keepdims=True) + norm_eps)
    attended = mixed * factor * gain_ref[...] * (1.0 - lam_init)
    att_ref[own, :] = attended.T.astype(bf16)


def forward_attention(lam, qkv, cosine, sine, gain, block):
    width = qkv.shape[0] // 3
    length = qkv.shape[1]
    full = lambda shape: pl.BlockSpec(shape, lambda i: (0,) * len(shape))
    outs = [
        ((length, width), bf16),
        ((length, width), bf16),
        ((length, width), bf16),
        ((width, length), bf16),
        ((width, length), f32),
        ((width, length), f32),
        ((8, length), f32),
        ((length, width), bf16),
    ]
    return pl.pallas_call(
        functools.partial(forward_kernel, block),
        grid=(length // block,),
        in_specs=[
            pl.BlockSpec(memory_space=pltpu.SMEM),
            full(qkv.shape),
            full(cosine.shape),
            full(sine.shape),
            full(gain.shape),
        ],
        out_specs=[full(shape) for shape, _ in outs],
        out_shape=[jax.ShapeDtypeStruct(shape, kind) for shape, kind in outs],
        scratch_shapes=[pltpu.VMEM((width, length), bf16), pltpu.VMEM((width, length), bf16)],
        compiler_params=pltpu.CompilerParams(
            dimension_semantics=("arbitrary",), vmem_limit_bytes=60 * 2**20
        ),
        name="attention_forward",
    )(lam, qkv, cosine, sine, gain)


def backward_kernel(
    block, lam_ref, q_ref, k_ref, v_ref, kt_ref, o1_ref, o2_ref, lse_ref, datt_ref,
    cos_ref, sin_ref, gain_ref,
    dqkv_ref, dgain_ref, dlam_ref,
    dmix_ref, dmixt_ref, delta_ref, dqt_ref,
):
    step = pl.program_id(0)
    blocks = pl.num_programs(0)
    width = v_ref.shape[1]
    half = width // 2
    length = q_ref.shape[0]
    scale = half ** -0.5
    lam = lam_ref[0]

    @pl.when(step == 0)
    def _():
        dgain_ref[...] = jnp.zeros_like(dgain_ref)
        dlam_ref[...] = jnp.zeros_like(dlam_ref)
        dqt_ref[...] = jnp.zeros_like(dqt_ref)

        def prepare(index, carry):
            cols = pl.ds(pl.multiple_of(index * block, block), block)
            first, second = o1_ref[:, cols], o2_ref[:, cols]
            mixed = first - lam * second
            factor = lax.rsqrt(jnp.mean(mixed * mixed, axis=0, keepdims=True) + norm_eps)
            upstream = datt_ref[cols, :].astype(f32).T * (1.0 - lam_init)
            dgain_ref[...] += jnp.sum(upstream * mixed * factor, axis=1, keepdims=True)
            scaled = upstream * gain_ref[...]
            dmixed = factor * scaled - mixed * (factor * factor * factor) * jnp.mean(
                scaled * mixed, axis=0, keepdims=True
            )
            low = dmixed.astype(bf16)
            back = low.astype(f32)
            dmixt_ref[:, cols] = low
            dmix_ref[cols, :] = back.T.astype(bf16)
            along_second = jnp.sum(back * second, axis=0, keepdims=True)
            delta_ref[0:1, cols] = jnp.sum(back * first, axis=0, keepdims=True)
            delta_ref[1:2, cols] = -lam * along_second
            dlam_ref[...] -= jnp.sum(along_second, axis=1, keepdims=True)
            return carry

        lax.fori_loop(0, length // block, prepare, 0)

    own = pl.ds(pl.multiple_of(step * block, block), block)
    key_ids = lax.broadcasted_iota(jnp.int32, (block, block), 0)
    query_ids = lax.broadcasted_iota(jnp.int32, (block, block), 1)
    keys = k_ref[own, :]
    keys_t = kt_ref[:, own]
    values = v_ref[own, :]

    def visit(index, state, diagonal):
        dkeys, dvalues = state
        cols = pl.ds(pl.multiple_of(index * block, block), block)
        queries = q_ref[cols, :]
        dmix = dmix_ref[cols, :]
        dprob = dot(values, dmixt_ref[:, cols])
        new_keys = []
        blend = None
        for part in range(2):
            lo, hi = part * half, (part + 1) * half
            scores = dot(keys[:, lo:hi], queries[:, lo:hi], 1, 1) * (scale * log2e)
            weights = jnp.exp2(scores - lse_ref[pl.ds(part, 1), cols])
            if diagonal:
                weights = jnp.where(key_ids <= query_ids, weights, 0.0)
            delta = delta_ref[part : part + 1, cols]
            if part == 0:
                blend = weights
                dscore = (weights * (dprob - delta)).astype(bf16)
            else:
                blend = blend - lam * weights
                dscore = (weights * (-lam * dprob - delta)).astype(bf16)
            new_keys.append(dkeys[part] + dot(dscore, queries[:, lo:hi]))
            dqt_ref[lo:hi, cols] += dot(keys_t[lo:hi], dscore)
        dvalues = dvalues + dot(blend.astype(bf16), dmix)
        return tuple(new_keys), dvalues

    start = (
        (jnp.zeros((block, half), f32), jnp.zeros((block, half), f32)),
        jnp.zeros((block, width), f32),
    )
    state = visit(step, start, True)
    dkeys, dvalues = lax.fori_loop(
        step + 1, blocks, lambda index, now: visit(index, now, False), state
    )
    both = jnp.concatenate(dkeys, axis=1).T * scale
    dqkv_ref[own, width : 2 * width] = (
        rotated(both, cos_ref[:, own], sin_ref[:, own], True).T.astype(bf16)
    )
    dqkv_ref[own, 2 * width : 3 * width] = dvalues.astype(bf16)

    dqkv_ref[own, 0:width] = (
        rotated(dqt_ref[:, own] * scale, cos_ref[:, own], sin_ref[:, own], True).T.astype(bf16)
    )


def backward_attention(lam, q, k, v, kt, o1, o2, lse, datt, cosine, sine, gain, block):
    length, width = q.shape
    full = lambda shape: pl.BlockSpec(shape, lambda i: (0,) * len(shape))
    arrays = (q, k, v, kt, o1, o2, lse, datt, cosine, sine, gain)
    outs = [((length, 3 * width), bf16), ((width, 1), f32), ((1, 1), f32)]
    return pl.pallas_call(
        functools.partial(backward_kernel, block),
        grid=(length // block,),
        in_specs=[pl.BlockSpec(memory_space=pltpu.SMEM)] + [full(a.shape) for a in arrays],
        out_specs=[full(shape) for shape, _ in outs],
        out_shape=[jax.ShapeDtypeStruct(shape, kind) for shape, kind in outs],
        scratch_shapes=[
            pltpu.VMEM((length, width), bf16),
            pltpu.VMEM((width, length), bf16),
            pltpu.VMEM((8, length), f32),
            pltpu.VMEM((width, length), f32),
        ],
        compiler_params=pltpu.CompilerParams(
            dimension_semantics=("arbitrary",), vmem_limit_bytes=60 * 2**20
        ),
        name="attention_backward",
    )(lam, *arrays)


def gather_rows(value):
    return lax.all_gather(value, "seq", axis=0, tiled=True)


def scatter_sum(value):
    return lax.psum_scatter(value, "seq", scatter_dimension=0, tiled=True)


def exchange(value):
    return lax.all_to_all(value, "seq", split_axis=0, concat_axis=0, tiled=True)


def rms_parts(value):
    return lax.rsqrt(jnp.mean(value * value, axis=-1, keepdims=True) + norm_eps)


def rms_back(value, factor, gain, upstream):
    scaled = upstream * gain
    mean = jnp.mean(scaled * value, axis=-1, keepdims=True)
    grad = factor * scaled - value * (factor * factor * factor) * mean
    return grad, jnp.sum(upstream * value * factor, axis=0)


def body(
    devices, block_input, positions, needle, cotangent, norm_gain1, w_query, w_key, w_value,
    lam_q1, lam_k1, lam_q2, lam_k2, sub_gain, w_out, norm_gain2, w_gate, w_up, w_down,
):
    rows, width = block_input.shape[1:]
    heads, half = lam_q1.shape
    head_width = sub_gain.shape[0]
    hidden = w_gate.shape[1]
    depth = w_query.shape[0]
    length = rows * devices
    columns = hidden // devices
    if heads > devices or hidden % devices:
        raise ValueError("unsupported mesh")
    head_of = [d * heads // devices for d in range(devices)]
    owner_of = [max(d for d in range(devices) if head_of[d] == h) for h in range(heads)]
    me = lax.axis_index("seq")
    my_head = me * heads // devices
    active = ((me + 1) * heads // devices > my_head).astype(f32)

    tokens = block_input[0].astype(f32)
    factor1 = rms_parts(tokens)
    normed = (tokens * factor1 * norm_gain1).astype(bf16)
    normed_all = gather_rows(normed)
    places = gather_rows(positions[0])

    by_head = jnp.stack([w.reshape(depth, heads, head_width) for w in (w_query, w_key, w_value)], 2)
    by_head = by_head.reshape(depth, heads, 3 * head_width).transpose(1, 0, 2)
    w_head = exchange(by_head[jnp.array(head_of)]).reshape(width, 3 * head_width)

    w_o = gather_rows(w_out)
    grad_out = cotangent[0].astype(f32) * needle[0].astype(f32)[:, None]
    grad_low = grad_out.astype(bf16)
    grad_all = gather_rows(grad_low)

    ffn = jnp.stack([w.reshape(depth, devices, columns) for w in (w_gate, w_up, w_down)], 2)
    ffn = ffn.reshape(depth, devices, 3 * columns).transpose(1, 0, 2)
    w_ffn = exchange(ffn).reshape(width, 3 * columns)

    inv_freq = jnp.exp(-math.log(10000.0) * jnp.arange(half // 2, dtype=f32) / (half // 2))
    angles = inv_freq[:, None] * places.astype(f32)[None, :]
    cosine, sine = jnp.cos(angles), jnp.sin(angles)
    lam_vals, lam_pull = jax.vjp(lambdas, lam_q1, lam_k1, lam_q2, lam_k2)
    lam_mine = lax.dynamic_slice_in_dim(lam_vals, my_head, 1, 0)
    gain_col = sub_gain[:, None]
    block = math.gcd(length, 512)

    qkv = dot(w_head, normed_all, 0, 1)
    q, k, v, kt, o1, o2, lse, att = forward_attention(
        lam_mine, qkv, cosine, sine, gain_col, block
    )
    att_rows = exchange(att.reshape(devices, rows, head_width))
    attended = jnp.concatenate([att_rows[d] for d in owner_of], axis=1)
    resid = tokens + dot(attended, w_o)
    factor2 = rms_parts(resid)
    normed_two = (resid * factor2 * norm_gain2).astype(bf16)
    two_all = gather_rows(normed_two)

    both = dot(two_all, w_ffn[:, : 2 * columns])
    gate, upper = both[:, :columns], both[:, columns:]
    grad_inner = dot(grad_all, w_ffn[:, 2 * columns :])
    sigma = jax.nn.sigmoid(gate)
    silu = gate * sigma
    inner = (silu * upper).astype(bf16)
    gate_low = (grad_inner * upper * sigma * (1.0 + gate * (1.0 - sigma))).astype(bf16)
    upper_low = (grad_inner * silu).astype(bf16)
    gates_low = jnp.concatenate([gate_low, upper_low], axis=1)
    grad_two = scatter_sum(dot(gates_low, w_ffn[:, : 2 * columns], 1, 1).astype(bf16)).astype(f32)
    ffn_out = scatter_sum(dot(inner, w_ffn[:, 2 * columns :], 1, 1).astype(bf16)).astype(f32)
    output = (resid + ffn_out).astype(bf16)[None]

    grad_resid_two, gain_two = rms_back(resid, factor2, norm_gain2, grad_two)
    grad_resid = grad_out + grad_resid_two
    resid_low = grad_resid.astype(bf16)
    grad_att = dot(resid_low, w_o, 1, 1).astype(bf16)
    pieces = jnp.stack(
        [grad_att[:, h * head_width : (h + 1) * head_width] for h in head_of], axis=0
    )
    datt = exchange(pieces).reshape(length, head_width)

    dqkv, dgain, dlam = backward_attention(
        lam_mine, q, k, v, kt, o1, o2, lse, datt, cosine, sine, gain_col, block
    )
    partial = (dot(dqkv, w_head, 1, 1) * active).astype(bf16)
    grad_normed = scatter_sum(partial).astype(f32)
    grad_tokens, gain_one = rms_back(tokens, factor1, norm_gain1, grad_normed)
    input_grad = (grad_resid + grad_tokens)[None]

    def settle(value):
        other = lax.ppermute(value, "batch", [(0, 1), (1, 0)])
        return value.astype(f32) + other.astype(f32)

    ffn_grads = jnp.concatenate(
        [dot(two_all, gates_low, 0, 0), dot(grad_all, inner, 0, 0)], axis=1
    ).astype(bf16)
    ffn_grads = settle(exchange(ffn_grads.reshape(devices, depth, 3 * columns)))
    ffn_grads = ffn_grads.reshape(devices, depth, 3, columns).transpose(2, 1, 0, 3)
    ffn_grads = ffn_grads.reshape(3, depth, hidden)

    head_grads = dot(normed_all, dqkv, 0, 0).astype(bf16)
    head_grads = settle(exchange(head_grads.reshape(devices, depth, 3 * head_width)))
    head_grads = jnp.stack([head_grads[d] for d in owner_of], axis=1)
    head_grads = head_grads.reshape(depth, heads, 3, head_width).transpose(2, 0, 1, 3)
    head_grads = head_grads.reshape(3, depth, width)

    out_grads = dot(attended, resid_low, 0, 0).astype(bf16)
    out_grads = settle(scatter_sum(out_grads))

    hot = jax.nn.one_hot(my_head, heads, dtype=f32) * active
    small = lax.psum(
        (gain_one, gain_two, dgain[:, 0] * active, hot * dlam[0, 0]), ("batch", "seq")
    )
    lam_grads = lam_pull(small[3])
    squares = sum(jnp.sum(g * g) for g in lam_grads)
    return (
        output, input_grad, small[0], head_grads[0], head_grads[1], head_grads[2],
        lam_grads[0], lam_grads[1], lam_grads[2], lam_grads[3], small[2], out_grads, small[1],
        ffn_grads[0], ffn_grads[1], ffn_grads[2], jnp.mean(lam_vals), jnp.sqrt(squares),
    )


def solution(mesh):
    rows = P("seq", None)
    in_specs = (
        P("batch", "seq", None), P("batch", "seq"), P("batch", "seq"), P("batch", "seq", None),
        P(), rows, rows, rows, P(), P(), P(), P(), P(), rows, P(), rows, rows, rows,
    )
    out_specs = (
        P("batch", "seq", None), P("batch", "seq", None), P(), rows, rows, rows,
        P(), P(), P(), P(), P(), rows, P(), rows, rows, rows, P(), P(),
    )
    return jax.shard_map(
        functools.partial(body, mesh.shape["seq"]),
        mesh=mesh, in_specs=in_specs, out_specs=out_specs, check_vma=False,
    )
```

```python
import functools
import math

import jax
import jax.numpy as jnp
from jax import lax
from jax.experimental import pallas as pl
from jax.experimental.pallas import tpu as pltpu
from jax.sharding import PartitionSpec as P

lam_init = 0.619
norm_eps = 1e-05
log2e = math.log2(math.e)
neg_large = -1e30
f32 = jnp.float32
bf16 = jnp.bfloat16


def lambdas(lam_q1, lam_k1, lam_q2, lam_k2):
    return (
        jnp.exp(jnp.sum(lam_q1 * lam_k1, axis=-1))
        - jnp.exp(jnp.sum(lam_q2 * lam_k2, axis=-1))
        + lam_init
    )


def dims(left_axis, right_axis):
    return (((left_axis,), (right_axis,)), ((), ()))


def dot(left, right, left_axis=1, right_axis=0):
    return lax.dot_general(left, right, dims(left_axis, right_axis), preferred_element_type=f32)


def rotated(value, cosine, sine, inverse=False):
    parts = []
    step = cosine.shape[0]
    sign = -1.0 if inverse else 1.0
    for start in range(0, value.shape[0], 2 * step):
        first = value[start : start + step]
        second = value[start + step : start + 2 * step]
        parts.append(first * cosine - sign * (second * sine))
        parts.append(second * cosine + sign * (first * sine))
    return jnp.concatenate(parts, axis=0)


def forward_kernel(
    block, lam_ref, qkv_ref, cos_ref, sin_ref, gain_ref,
    q_ref, k_ref, v_ref, kt_ref, o1_ref, o2_ref, lse_ref, att_ref,
    qt_ref, vt_ref,
):
    step = pl.program_id(0)
    width = v_ref.shape[1]
    half = width // 2
    length = q_ref.shape[0]
    scale = half ** -0.5 * log2e

    @pl.when(step == 0)
    def _():
        def prepare(index, carry):
            cols = pl.ds(pl.multiple_of(index * block, block), block)
            cosine, sine = cos_ref[:, cols], sin_ref[:, cols]
            query = rotated(qkv_ref[0:width, cols], cosine, sine)
            key = rotated(qkv_ref[width : 2 * width, cols], cosine, sine)
            value = qkv_ref[2 * width : 3 * width, cols]
            qt_ref[:, cols] = query.astype(bf16)
            kt_ref[:, cols] = key.astype(bf16)
            vt_ref[:, cols] = value.astype(bf16)
            q_ref[cols, :] = query.T.astype(bf16)
            k_ref[cols, :] = key.T.astype(bf16)
            v_ref[cols, :] = value.T.astype(bf16)
            return carry

        lax.fori_loop(0, length // block, prepare, 0)

    own = pl.ds(pl.multiple_of(step * block, block), block)
    queries = qt_ref[:, own]
    key_ids = lax.broadcasted_iota(jnp.int32, (block, block), 0)
    query_ids = lax.broadcasted_iota(jnp.int32, (block, block), 1)

    def visit(index, state, diagonal):
        rows = pl.ds(pl.multiple_of(index * block, block), block)
        values = vt_ref[:, rows]
        out = []
        for part in range(2):
            top, total, acc = state[part]
            lo, hi = part * half, (part + 1) * half
            scores = dot(k_ref[rows, lo:hi], queries[lo:hi]) * scale
            if diagonal:
                scores = jnp.where(key_ids <= query_ids, scores, neg_large)
            new_top = jnp.maximum(top, jnp.max(scores, axis=0, keepdims=True))
            weights = jnp.exp2(scores - new_top)
            fade = jnp.exp2(top - new_top)
            total = total * fade + jnp.sum(weights, axis=0, keepdims=True)
            acc = acc * fade + dot(values, weights.astype(bf16))
            out.append((new_top, total, acc))
        return tuple(out)

    start = tuple(
        (
            jnp.full((1, block), neg_large, f32),
            jnp.zeros((1, block), f32),
            jnp.zeros((width, block), f32),
        )
        for _ in range(2)
    )
    state = lax.fori_loop(0, step, lambda index, now: visit(index, now, False), start)
    state = visit(step, state, True)
    outs = []
    for part, ref in ((0, o1_ref), (1, o2_ref)):
        top, total, acc = state[part]
        result = acc / total
        ref[:, own] = result
        lse_ref[pl.ds(part, 1), own] = top + jnp.log2(total)
        outs.append(result)
    mixed = outs[0] - lam_ref[0] * outs[1]
    factor = lax.rsqrt(jnp.mean(mixed * mixed, axis=0, keepdims=True) + norm_eps)
    attended = mixed * factor * gain_ref[...] * (1.0 - lam_init)
    att_ref[own, :] = attended.T.astype(bf16)


def forward_attention(lam, qkv, cosine, sine, gain, block):
    width = qkv.shape[0] // 3
    length = qkv.shape[1]
    full = lambda shape: pl.BlockSpec(shape, lambda i: (0,) * len(shape))
    outs = [
        ((length, width), bf16),
        ((length, width), bf16),
        ((length, width), bf16),
        ((width, length), bf16),
        ((width, length), f32),
        ((width, length), f32),
        ((8, length), f32),
        ((length, width), bf16),
    ]
    return pl.pallas_call(
        functools.partial(forward_kernel, block),
        grid=(length // block,),
        in_specs=[
            pl.BlockSpec(memory_space=pltpu.SMEM),
            full(qkv.shape),
            full(cosine.shape),
            full(sine.shape),
            full(gain.shape),
        ],
        out_specs=[full(shape) for shape, _ in outs],
        out_shape=[jax.ShapeDtypeStruct(shape, kind) for shape, kind in outs],
        scratch_shapes=[pltpu.VMEM((width, length), bf16), pltpu.VMEM((width, length), bf16)],
        compiler_params=pltpu.CompilerParams(
            dimension_semantics=("arbitrary",), vmem_limit_bytes=60 * 2**20
        ),
        name="attention_forward",
    )(lam, qkv, cosine, sine, gain)


def backward_kernel(
    block, lam_ref, q_ref, k_ref, v_ref, kt_ref, o1_ref, o2_ref, lse_ref, datt_ref,
    cos_ref, sin_ref, gain_ref,
    dqkv_ref, dgain_ref, dlam_ref,
    dmix_ref, dmixt_ref, delta_ref, dqt_ref,
):
    step = pl.program_id(0)
    blocks = pl.num_programs(0)
    width = v_ref.shape[1]
    half = width // 2
    length = q_ref.shape[0]
    scale = half ** -0.5
    lam = lam_ref[0]

    @pl.when(step == 0)
    def _():
        dgain_ref[...] = jnp.zeros_like(dgain_ref)
        dlam_ref[...] = jnp.zeros_like(dlam_ref)
        dqt_ref[...] = jnp.zeros_like(dqt_ref)

        def prepare(index, carry):
            cols = pl.ds(pl.multiple_of(index * block, block), block)
            first, second = o1_ref[:, cols], o2_ref[:, cols]
            mixed = first - lam * second
            factor = lax.rsqrt(jnp.mean(mixed * mixed, axis=0, keepdims=True) + norm_eps)
            upstream = datt_ref[cols, :].astype(f32).T * (1.0 - lam_init)
            dgain_ref[...] += jnp.sum(upstream * mixed * factor, axis=1, keepdims=True)
            scaled = upstream * gain_ref[...]
            dmixed = factor * scaled - mixed * (factor * factor * factor) * jnp.mean(
                scaled * mixed, axis=0, keepdims=True
            )
            low = dmixed.astype(bf16)
            back = low.astype(f32)
            dmixt_ref[:, cols] = low
            dmix_ref[cols, :] = back.T.astype(bf16)
            along_second = jnp.sum(back * second, axis=0, keepdims=True)
            delta_ref[0:1, cols] = jnp.sum(back * first, axis=0, keepdims=True)
            delta_ref[1:2, cols] = -lam * along_second
            dlam_ref[...] -= jnp.sum(along_second, axis=1, keepdims=True)
            return carry

        lax.fori_loop(0, length // block, prepare, 0)

    own = pl.ds(pl.multiple_of(step * block, block), block)
    key_ids = lax.broadcasted_iota(jnp.int32, (block, block), 0)
    query_ids = lax.broadcasted_iota(jnp.int32, (block, block), 1)
    keys = k_ref[own, :]
    keys_t = kt_ref[:, own]
    values = v_ref[own, :]

    def visit(index, state, diagonal):
        dkeys, dvalues = state
        cols = pl.ds(pl.multiple_of(index * block, block), block)
        queries = q_ref[cols, :]
        dmix = dmix_ref[cols, :]
        dprob = dot(values, dmixt_ref[:, cols])
        new_keys = []
        blend = None
        for part in range(2):
            lo, hi = part * half, (part + 1) * half
            scores = dot(keys[:, lo:hi], queries[:, lo:hi], 1, 1) * (scale * log2e)
            weights = jnp.exp2(scores - lse_ref[pl.ds(part, 1), cols])
            if diagonal:
                weights = jnp.where(key_ids <= query_ids, weights, 0.0)
            delta = delta_ref[part : part + 1, cols]
            if part == 0:
                blend = weights
                dscore = (weights * (dprob - delta)).astype(bf16)
            else:
                blend = blend - lam * weights
                dscore = (weights * (-lam * dprob - delta)).astype(bf16)
            new_keys.append(dkeys[part] + dot(dscore, queries[:, lo:hi]))
            dqt_ref[lo:hi, cols] += dot(keys_t[lo:hi], dscore)
        dvalues = dvalues + dot(blend.astype(bf16), dmix)
        return tuple(new_keys), dvalues

    start = (
        (jnp.zeros((block, half), f32), jnp.zeros((block, half), f32)),
        jnp.zeros((block, width), f32),
    )
    state = visit(step, start, True)
    dkeys, dvalues = lax.fori_loop(
        step + 1, blocks, lambda index, now: visit(index, now, False), state
    )
    both = jnp.concatenate(dkeys, axis=1).T * (scale * lam_ref[1])
    dqkv_ref[own, width : 2 * width] = (
        rotated(both, cos_ref[:, own], sin_ref[:, own], True).T.astype(bf16)
    )
    dqkv_ref[own, 2 * width : 3 * width] = (dvalues * lam_ref[1]).astype(bf16)

    dqkv_ref[own, 0:width] = (
        rotated(dqt_ref[:, own] * (scale * lam_ref[1]), cos_ref[:, own], sin_ref[:, own], True).T.astype(bf16)
    )


def backward_attention(lam, q, k, v, kt, o1, o2, lse, datt, cosine, sine, gain, block):
    length, width = q.shape
    full = lambda shape: pl.BlockSpec(shape, lambda i: (0,) * len(shape))
    arrays = (q, k, v, kt, o1, o2, lse, datt, cosine, sine, gain)
    outs = [((length, 3 * width), bf16), ((width, 1), f32), ((1, 1), f32)]
    return pl.pallas_call(
        functools.partial(backward_kernel, block),
        grid=(length // block,),
        in_specs=[pl.BlockSpec(memory_space=pltpu.SMEM)] + [full(a.shape) for a in arrays],
        out_specs=[full(shape) for shape, _ in outs],
        out_shape=[jax.ShapeDtypeStruct(shape, kind) for shape, kind in outs],
        scratch_shapes=[
            pltpu.VMEM((length, width), bf16),
            pltpu.VMEM((width, length), bf16),
            pltpu.VMEM((8, length), f32),
            pltpu.VMEM((width, length), f32),
        ],
        compiler_params=pltpu.CompilerParams(
            dimension_semantics=("arbitrary",), vmem_limit_bytes=60 * 2**20
        ),
        name="attention_backward",
    )(lam, *arrays)


MESH = pl.DeviceIdType.MESH
ANY = pl.BlockSpec(memory_space=pl.ANY)
VMEM = pl.BlockSpec(memory_space=pltpu.VMEM)
DMA = pltpu.SemaphoreType.DMA
group = 16


def place():
    me = lax.axis_index("seq")
    return me, me // 4, (me // 2) % 2, me % 2


def remote(src, dst, send_sem, recv_sem, target):
    return pltpu.make_async_remote_copy(
        src_ref=src, dst_ref=dst, send_sem=send_sem, recv_sem=recv_sem,
        device_id={"seq": target}, device_id_type=MESH,
    )


def greet():
    me, z, _, _ = place()
    barrier = pltpu.get_barrier_semaphore()

    def tell(target):
        pl.semaphore_signal(barrier, inc=1, device_id={"seq": target}, device_id_type=MESH)

    tell(me ^ 1)
    tell(me ^ 2)
    pl.when(z > 0)(lambda: tell(me - 4))
    pl.when(z < 3)(lambda: tell(me + 4))
    pl.semaphore_wait(barrier, 2 + (z > 0).astype(jnp.int32) + (z < 3).astype(jnp.int32))


def gather_kernel(parts, *refs):
    count = len(parts)
    ins, outs = refs[:count], refs[count : 2 * count]
    local_sem, recv_sem, up_sem, down_sem, side_sem, core_sem = refs[2 * count :]
    me, z, x, c = place()
    greet()

    def view(a, block, part):
        rows = ins[a].shape[0]
        sub = rows // parts[a]
        return outs[a].at[pl.ds(pl.multiple_of(block * rows + part * sub, sub), sub)]

    def copy(a, part, block, target, sems, own=False):
        sub = ins[a].shape[0] // parts[a]
        src = ins[a].at[pl.ds(part * sub, sub)] if own else view(a, block, part)
        return remote(
            src, view(a, block, part), sems.at[a, part, block], recv_sem.at[a, part, block], target
        )

    def local(a):
        rows = ins[a].shape[0]
        place_here = outs[a].at[pl.ds(pl.multiple_of(me * rows, rows), rows)]
        return pltpu.make_async_copy(ins[a], place_here, local_sem.at[a])

    every = [(a, p) for a in range(count) for p in range(parts[a])]
    for a, p in every:
        copy(a, p, me, me ^ 2, side_sem, True).start()
        pl.when(z < 3)(lambda: copy(a, p, me, me + 4, up_sem, True).start())
        pl.when(z > 0)(lambda: copy(a, p, me, me - 4, down_sem, True).start())
        copy(a, p, me, me ^ 1, core_sem, True).start()
    for a in range(count):
        local(a).start()

    def from_line(a, p, s):
        def pass_on(block):
            copy(a, p, block, me ^ 2, side_sem).start()
            copy(a, p, block, me ^ 1, core_sem).start()

        @pl.when(z >= s)
        def _():
            block = me - 4 * s
            copy(a, p, block, me, side_sem).wait_recv()
            pl.when(z < 3)(lambda: copy(a, p, block, me + 4, up_sem).start())
            pass_on(block)

        @pl.when(z + s <= 3)
        def _():
            block = me + 4 * s
            copy(a, p, block, me, side_sem).wait_recv()
            pl.when(z > 0)(lambda: copy(a, p, block, me - 4, down_sem).start())
            pass_on(block)

    def from_side(a, p, s):
        def take(block):
            copy(a, p, block, me, side_sem).wait_recv()
            copy(a, p, block, me ^ 1, core_sem).start()

        if s == 0:
            take(me ^ 2)
        else:
            pl.when(z >= s)(lambda: take((me ^ 2) - 4 * s))
            pl.when(z + s <= 3)(lambda: take((me ^ 2) + 4 * s))

    for s in range(1, 4):
        for a, p in every:
            from_line(a, p, s)
        for a, p in every:
            from_side(a, p, s - 1)
    for a, p in every:
        from_side(a, p, 3)

    def finish(i, carry):
        pair = 4 * (i // 2) + 2 * (i % 2)
        for a, p in every:
            copy(a, p, pair + 1 - c, me, core_sem).wait_recv()
            copy(a, p, pair + c, me, core_sem).wait_send()
        return carry

    lax.fori_loop(0, 8, finish, 0)

    def sent(i, carry):
        block = 4 * i + 2 * x + c
        for a, p in every:
            copy(a, p, block, me, side_sem).wait_send()
            pl.when((i <= z) & (z < 3))(lambda: copy(a, p, block, me, up_sem).wait_send())
            pl.when((i >= z) & (z > 0))(lambda: copy(a, p, block, me, down_sem).wait_send())
        return carry

    lax.fori_loop(0, 4, sent, 0)
    for a in range(count):
        local(a).wait()


def gather(arrays, parts, collective_id):
    devices = lax.axis_size("seq")
    if devices != group:
        return [lax.all_gather(a, "seq", axis=0, tiled=True) for a in arrays]
    count = len(arrays)
    sem = DMA((count, max(parts), group))
    return pl.pallas_call(
        functools.partial(gather_kernel, parts),
        in_specs=[ANY] * count,
        out_specs=[ANY] * count,
        out_shape=[jax.ShapeDtypeStruct((group * a.shape[0],) + a.shape[1:], a.dtype) for a in arrays],
        scratch_shapes=[DMA((count,)), sem, sem, sem, sem, sem],
        compiler_params=pltpu.CompilerParams(collective_id=collective_id, has_side_effects=True),
        name=f"gather{collective_id}",
    )(*arrays)


def scatter_kernel(
    lhs_ref, rhs_ref, out_ref, own, core_in, side_in, up_in, down_in,
    core_s, core_r, side_s, side_r, up_s, up_r, down_s, down_r,
):
    me, z, x, c = place()
    rows, width = out_ref.shape
    greet()
    mine, across = 2 * x + c, 2 * (1 - x) + c

    def order(g):
        if g == 3:
            return z
        first = jnp.where(3 - g > z, 3 - g, 2 - g)
        second = jnp.where(g < z, g, g + 1)
        return jnp.where(z < 2, first, second)

    def core_copy(t, i):
        return remote(
            own.at[t, 2 * i + 1 - c], core_in.at[t, i], core_s.at[t, i], core_r.at[t, i], me ^ 1
        )

    def side_copy(t):
        return remote(own.at[t, across], side_in.at[t], side_s.at[t], side_r.at[t], me ^ 2)

    def up_copy(t):
        return remote(own.at[t, mine], up_in.at[t], up_s.at[t], up_r.at[t], me + 4)

    def down_copy(t):
        return remote(own.at[t, mine], down_in.at[t], down_s.at[t], down_r.at[t], me - 4)

    def multiply(t):
        left = lhs_ref[pl.ds(pl.multiple_of(t * 4 * rows, 4 * rows), 4 * rows), :]
        own[t] = dot(left, rhs_ref[...], 1, 1).astype(bf16).reshape(4, rows, width)
        core_copy(t, 0).start()
        core_copy(t, 1).start()

    def add(t, block, extra):
        own[t, block] = (own[t, block].astype(f32) + extra.astype(f32)).astype(bf16)

    def merge_core(t):
        core_copy(t, 0).wait()
        core_copy(t, 1).wait()
        add(t, across, core_in[t, 1 - x])
        side_copy(t).start()
        add(t, mine, core_in[t, x])

    def along(t):
        side_copy(t).wait()
        add(t, mine, side_in[t])

        @pl.when(t > z)
        def _():
            @pl.when(z > 0)
            def _():
                up_copy(t).wait_recv()
                add(t, mine, up_in[t])

            up_copy(t).start()

        @pl.when(t < z)
        def _():
            @pl.when(z < 3)
            def _():
                down_copy(t).wait_recv()
                add(t, mine, down_in[t])

            down_copy(t).start()

    steps = [order(g) for g in range(4)]
    multiply(steps[0])
    multiply(steps[1])
    merge_core(steps[0])
    multiply(steps[2])
    merge_core(steps[1])
    multiply(steps[3])
    merge_core(steps[2])
    along(steps[0])
    merge_core(steps[3])
    along(steps[1])
    along(steps[2])
    side_copy(z).wait()
    out_ref[...] = own[z, mine].astype(f32) + side_in[z].astype(f32)

    @pl.when(z > 0)
    def _():
        up_copy(z).wait_recv()
        out_ref[...] += up_in[z].astype(f32)

    @pl.when(z < 3)
    def _():
        down_copy(z).wait_recv()
        out_ref[...] += down_in[z].astype(f32)

    def sent(i, carry):
        pl.when(i > z)(lambda: up_copy(i).wait_send())
        pl.when(i < z)(lambda: down_copy(i).wait_send())
        return carry

    lax.fori_loop(0, 4, sent, 0)


def scatter(lhs, rhs, collective_id):
    devices = lax.axis_size("seq")
    if devices != group:
        partial = dot(lhs, rhs, 1, 1).astype(bf16)
        return lax.psum_scatter(partial, "seq", scatter_dimension=0, tiled=True).astype(f32)
    rows, width = lhs.shape[0] // group, rhs.shape[0]
    block = pltpu.VMEM((4, rows, width), bf16)
    return pl.pallas_call(
        scatter_kernel,
        in_specs=[VMEM, VMEM],
        out_specs=VMEM,
        out_shape=jax.ShapeDtypeStruct((rows, width), f32),
        scratch_shapes=[
            pltpu.VMEM((4, 4, rows, width), bf16), pltpu.VMEM((4, 2, rows, width), bf16),
            block, block, block, DMA((4, 2)), DMA((4, 2)),
            DMA((4,)), DMA((4,)), DMA((4,)), DMA((4,)), DMA((4,)), DMA((4,)),
        ],
        compiler_params=pltpu.CompilerParams(
            collective_id=collective_id, has_side_effects=True, vmem_limit_bytes=56 * 2**20
        ),
        name=f"scatter{collective_id}",
    )(lhs, rhs)


def exchange(value):
    return lax.all_to_all(value, "seq", split_axis=0, concat_axis=0, tiled=True)


def rms_parts(value):
    return lax.rsqrt(jnp.mean(value * value, axis=-1, keepdims=True) + norm_eps)


def rms_back(value, factor, gain, upstream):
    scaled = upstream * gain
    mean = jnp.mean(scaled * value, axis=-1, keepdims=True)
    grad = factor * scaled - value * (factor * factor * factor) * mean
    return grad, jnp.sum(upstream * value * factor, axis=0)


def body(
    devices, block_input, positions, needle, cotangent, norm_gain1, w_query, w_key, w_value,
    lam_q1, lam_k1, lam_q2, lam_k2, sub_gain, w_out, norm_gain2, w_gate, w_up, w_down,
):
    rows, width = block_input.shape[1:]
    heads, half = lam_q1.shape
    head_width = sub_gain.shape[0]
    hidden = w_gate.shape[1]
    depth = w_query.shape[0]
    length = rows * devices
    columns = hidden // devices
    if heads > devices or hidden % devices:
        raise ValueError("unsupported mesh")
    head_of = [d * heads // devices for d in range(devices)]
    owner_of = [max(d for d in range(devices) if head_of[d] == h) for h in range(heads)]
    me = lax.axis_index("seq")
    my_head = me * heads // devices
    active = ((me + 1) * heads // devices > my_head).astype(f32)

    tokens = block_input[0].astype(f32)
    factor1 = rms_parts(tokens)
    normed = (tokens * factor1 * norm_gain1).astype(bf16)
    here = jnp.broadcast_to(positions[0], (1, 8, rows))
    normed_all, places = gather([normed, here], (2, 1), 0)
    places = places[:, 0].reshape(length)

    by_head = jnp.stack([w.reshape(depth, heads, head_width) for w in (w_query, w_key, w_value)], 2)
    by_head = by_head.reshape(depth, heads, 3 * head_width).transpose(1, 0, 2)
    w_head = exchange(by_head[jnp.array(head_of)]).reshape(width, 3 * head_width)

    w_o, = gather([w_out], (1,), 1)
    grad_out = cotangent[0].astype(f32) * needle[0].astype(f32)[:, None]
    grad_low = grad_out.astype(bf16)

    ffn = jnp.stack([w.reshape(depth, devices, columns) for w in (w_gate, w_up, w_down)], 2)
    ffn = ffn.reshape(depth, devices, 3 * columns).transpose(1, 0, 2)
    w_ffn = exchange(ffn).reshape(width, 3 * columns)

    inv_freq = jnp.exp(-math.log(10000.0) * jnp.arange(half // 2, dtype=f32) / (half // 2))
    angles = inv_freq[:, None] * places.astype(f32)[None, :]
    cosine, sine = jnp.cos(angles), jnp.sin(angles)
    lam_vals, lam_pull = jax.vjp(lambdas, lam_q1, lam_k1, lam_q2, lam_k2)
    lam_mine = jnp.stack([lax.dynamic_index_in_dim(lam_vals, my_head, 0, False), active])
    gain_col = sub_gain[:, None]
    block = math.gcd(length, 512)

    qkv = dot(w_head, normed_all, 0, 1)
    q, k, v, kt, o1, o2, lse, att = forward_attention(
        lam_mine, qkv, cosine, sine, gain_col, block
    )
    att_rows = exchange(att.reshape(devices, rows, head_width))
    attended = jnp.concatenate([att_rows[d] for d in owner_of], axis=1)
    resid = tokens + dot(attended, w_o)
    factor2 = rms_parts(resid)
    normed_two = (resid * factor2 * norm_gain2).astype(bf16)
    two_all, grad_all = gather([normed_two, grad_low], (2, 2), 2)

    both = dot(two_all, w_ffn[:, : 2 * columns])
    gate, upper = both[:, :columns], both[:, columns:]
    grad_inner = dot(grad_all, w_ffn[:, 2 * columns :])
    sigma = jax.nn.sigmoid(gate)
    silu = gate * sigma
    inner = (silu * upper).astype(bf16)
    gate_low = (grad_inner * upper * sigma * (1.0 + gate * (1.0 - sigma))).astype(bf16)
    upper_low = (grad_inner * silu).astype(bf16)
    gates_low = jnp.concatenate([gate_low, upper_low], axis=1)
    grad_two = scatter(gates_low, w_ffn[:, : 2 * columns], 3)
    ffn_out = scatter(inner, w_ffn[:, 2 * columns :], 4)
    output = (resid + ffn_out).astype(bf16)[None]

    grad_resid_two, gain_two = rms_back(resid, factor2, norm_gain2, grad_two)
    grad_resid = grad_out + grad_resid_two
    resid_low = grad_resid.astype(bf16)
    grad_att = dot(resid_low, w_o, 1, 1).astype(bf16)
    pieces = jnp.stack(
        [grad_att[:, h * head_width : (h + 1) * head_width] for h in head_of], axis=0
    )
    datt = exchange(pieces).reshape(length, head_width)

    dqkv, dgain, dlam = backward_attention(
        lam_mine, q, k, v, kt, o1, o2, lse, datt, cosine, sine, gain_col, block
    )
    grad_normed = scatter(dqkv, w_head, 5)
    grad_tokens, gain_one = rms_back(tokens, factor1, norm_gain1, grad_normed)
    input_grad = (grad_resid + grad_tokens)[None]

    def settle(value):
        other = lax.ppermute(value, "batch", [(0, 1), (1, 0)])
        return value.astype(f32) + other.astype(f32)

    ffn_grads = jnp.concatenate(
        [dot(two_all, gates_low, 0, 0), dot(grad_all, inner, 0, 0)], axis=1
    ).astype(bf16)
    ffn_grads = settle(exchange(ffn_grads.reshape(devices, depth, 3 * columns)))
    ffn_grads = ffn_grads.reshape(devices, depth, 3, columns).transpose(2, 1, 0, 3)
    ffn_grads = ffn_grads.reshape(3, depth, hidden)

    head_grads = dot(normed_all, dqkv, 0, 0).astype(bf16)
    head_grads = settle(exchange(head_grads.reshape(devices, depth, 3 * head_width)))
    head_grads = jnp.stack([head_grads[d] for d in owner_of], axis=1)
    head_grads = head_grads.reshape(depth, heads, 3, head_width).transpose(2, 0, 1, 3)
    head_grads = head_grads.reshape(3, depth, width)

    out_grads = settle(scatter(attended.T, resid_low.T, 6).astype(bf16))

    hot = jax.nn.one_hot(my_head, heads, dtype=f32) * active
    small = lax.psum(
        (gain_one, gain_two, dgain[:, 0] * active, hot * dlam[0, 0]), ("batch", "seq")
    )
    lam_grads = lam_pull(small[3])
    squares = sum(jnp.sum(g * g) for g in lam_grads)
    return (
        output, input_grad, small[0], head_grads[0], head_grads[1], head_grads[2],
        lam_grads[0], lam_grads[1], lam_grads[2], lam_grads[3], small[2], out_grads, small[1],
        ffn_grads[0], ffn_grads[1], ffn_grads[2], jnp.mean(lam_vals), jnp.sqrt(squares),
    )


def solution(mesh):
    rows = P("seq", None)
    in_specs = (
        P("batch", "seq", None), P("batch", "seq"), P("batch", "seq"), P("batch", "seq", None),
        P(), rows, rows, rows, P(), P(), P(), P(), P(), rows, P(), rows, rows, rows,
    )
    out_specs = (
        P("batch", "seq", None), P("batch", "seq", None), P(), rows, rows, rows,
        P(), P(), P(), P(), P(), rows, P(), rows, rows, rows, P(), P(),
    )
    return jax.shard_map(
        functools.partial(body, mesh.shape["seq"]),
        mesh=mesh, in_specs=in_specs, out_specs=out_specs, check_vma=False,
    )
```

```python
import functools
import math

import jax
import jax.numpy as jnp
from jax import lax
from jax.experimental import pallas as pl
from jax.experimental.pallas import tpu as pltpu
from jax.sharding import PartitionSpec as P

lam_init = 0.619
norm_eps = 1e-05
log2e = math.log2(math.e)
neg_large = -1e30
f32 = jnp.float32
bf16 = jnp.bfloat16


def lambdas(lam_q1, lam_k1, lam_q2, lam_k2):
    return (
        jnp.exp(jnp.sum(lam_q1 * lam_k1, axis=-1))
        - jnp.exp(jnp.sum(lam_q2 * lam_k2, axis=-1))
        + lam_init
    )


def dims(left_axis, right_axis):
    return (((left_axis,), (right_axis,)), ((), ()))


def dot(left, right, left_axis=1, right_axis=0):
    return lax.dot_general(left, right, dims(left_axis, right_axis), preferred_element_type=f32)


MESH = pl.DeviceIdType.MESH
ANY = pl.BlockSpec(memory_space=pl.ANY)
VMEM = pl.BlockSpec(memory_space=pltpu.VMEM)
SMEM = pl.BlockSpec(memory_space=pltpu.SMEM)
DMA = pltpu.SemaphoreType.DMA
group = 16
busy = pl.CostEstimate(flops=4 * 10**10, bytes_accessed=10**7, transcendentals=0)
sides = (8, 4, 2)


def place():
    seq = lax.axis_index("seq")
    return lax.axis_index("batch") * 8 + seq % 8, seq // 8


def device(number, cube=None):
    return {"batch": number // 8, "seq": (place()[1] if cube is None else cube) * 8 + number % 8}


def partner():
    return {"batch": lax.axis_index("batch"), "seq": lax.axis_index("seq") ^ 8}


def swapped():
    batch, seq = lax.axis_index("batch"), lax.axis_index("seq")
    return {"batch": 1 - batch, "seq": seq ^ 8}, batch != seq // 8


def anyone(index):
    return index // group * 8 + index % 8, index % group // 8


def everywhere():
    return lax.axis_index("batch") * group + lax.axis_index("seq")


def remote(src, dst, send_sem, recv_sem, number):
    return pltpu.make_async_remote_copy(
        src_ref=src, dst_ref=dst, send_sem=send_sem, recv_sem=recv_sem,
        device_id=device(number), device_id_type=MESH,
    )


def greet(cross=False, swap=False):
    me = place()[0]
    barrier = pltpu.get_barrier_semaphore()
    count = 1 + len(sides)
    for mask in (1,) + sides:
        pl.semaphore_signal(barrier, inc=1, device_id=device(me ^ mask), device_id_type=MESH)
    if cross:
        pl.semaphore_signal(barrier, inc=1, device_id=partner(), device_id_type=MESH)
        count = count + 1
    if swap:
        target, moved = swapped()

        @pl.when(moved)
        def _():
            pl.semaphore_signal(barrier, inc=1, device_id=target, device_id_type=MESH)

        count = count + moved.astype(jnp.int32)
    pl.semaphore_wait(barrier, count)


def greet_all():
    barrier = pltpu.get_barrier_semaphore()
    me = everywhere()

    def tell(mask, carry):
        target = device(*anyone(me ^ mask))
        pl.semaphore_signal(barrier, inc=1, device_id=target, device_id_type=MESH)
        return carry

    lax.fori_loop(1, 2 * group, tell, 0)
    pl.semaphore_wait(barrier, 2 * group - 1)


class Cargo:
    def __init__(self, cross, swap, sems):
        self.cross, self.swap, self.sems = cross, swap, sems

    def copies(self):
        for i, (src, dst) in enumerate(self.cross):
            yield None, pltpu.make_async_remote_copy(
                src_ref=src, dst_ref=dst, send_sem=self.sems.at[0, i], recv_sem=self.sems.at[1, i],
                device_id=partner(), device_id_type=MESH,
            ), None
        target, moved = swapped()
        for i, (src, dst) in enumerate(self.swap):
            j = len(self.cross) + i
            yield moved, pltpu.make_async_remote_copy(
                src_ref=src, dst_ref=dst, send_sem=self.sems.at[0, j], recv_sem=self.sems.at[1, j],
                device_id=target, device_id_type=MESH,
            ), pltpu.make_async_copy(src, dst, self.sems.at[0, j])

    def start(self):
        for moved, far, near in self.copies():
            if moved is None:
                far.start()
            else:
                pl.when(moved)(lambda: far.start())
                pl.when(jnp.logical_not(moved))(lambda: near.start())

    def finish(self):
        for moved, far, near in self.copies():
            if moved is None:
                far.wait()
            else:
                pl.when(moved)(lambda: far.wait())
                pl.when(jnp.logical_not(moved))(lambda: near.wait())


class Gather:
    def __init__(self, items, send_sem, recv_sem, local_sem):
        self.items, self.send_sem, self.recv_sem, self.local_sem = items, send_sem, recv_sem, local_sem
        self.me = place()[0]

    def order(self, part):
        return [sides[(part + k) % 3] for k in range(3)]

    def view(self, item, part, number):
        src, out, row, parts = self.items[item]
        rows, width = src.shape[0], src.shape[-1] // parts
        at = pl.ds(row(number), rows)
        if parts == 1:
            return out.at[at]
        return out.at[at, pl.ds(part * width, width)]

    def copy(self, item, part, number, lane, target, own=False):
        src, out, row, parts = self.items[item]
        width = src.shape[-1] // parts
        here = self.view(item, part, number)
        source = (src if parts == 1 else src.at[:, pl.ds(part * width, width)]) if own else here
        return remote(
            source, here, self.send_sem.at[item, part, number, lane],
            self.recv_sem.at[item, part, number], target,
        )

    def every(self):
        return [(i, p) for i in range(len(self.items)) for p in range(self.items[i][3])]

    def local(self, item):
        src, out, row, _ = self.items[item]
        return pltpu.make_async_copy(src, out.at[pl.ds(row(self.me), src.shape[0])], self.local_sem.at[item])

    def start(self, items=None):
        chosen = [(i, p) for i, p in self.every() if items is None or i in items]
        for k in range(3):
            for i, p in chosen:
                self.copy(i, p, self.me, k, self.me ^ self.order(p)[k], True).start()
        for i, p in chosen:
            self.copy(i, p, self.me, 3, self.me ^ 1, True).start()
        for i in range(len(self.items)):
            if items is None or i in items:
                self.local(i).start()

    def arrivals(self, part, step):
        order = self.order(part)
        masks = [0]
        for side in order[:step]:
            masks = masks + [m ^ side for m in masks]
        return [m ^ order[step] for m in masks]

    def step(self, step, items=None):
        for i, p in self.every():
            if items is not None and i not in items:
                continue
            for mask in self.arrivals(p, step):
                number = self.me ^ mask
                self.copy(i, p, number, 0, self.me).wait_recv()
                for k in range(step + 1, 3):
                    self.copy(i, p, number, k, self.me ^ self.order(p)[k]).start()
                self.copy(i, p, number, 3, self.me ^ 1).start()

    def finish(self, items=None):
        for i, p in self.every():
            if items is not None and i not in items:
                continue

            def pair(j, carry, i=i, p=p):
                number = (self.me ^ 1) ^ (2 * j)
                self.copy(i, p, number, 3, self.me).wait_recv()
                self.copy(i, p, number ^ 1, 3, self.me).wait_send()
                return carry

            lax.fori_loop(0, 8, pair, 0)
            self.copy(i, p, self.me, 0, self.me).wait_send()
            for step in range(3):
                if step:
                    self.copy(i, p, self.me, step, self.me).wait_send()
                for mask in self.arrivals(p, step):
                    for k in range(step + 1, 3):
                        self.copy(i, p, self.me ^ mask, k, self.me).wait_send()
        for i in range(len(self.items)):
            if items is None or i in items:
                self.local(i).wait()

    @staticmethod
    def scratch(count):
        return [DMA((count, 3, group, 4)), DMA((count, 3, group)), DMA((count,))]


def natural(rows):
    return lambda number: pl.multiple_of(number * rows, rows)


def gather_kernel(parts, columns, *refs):
    count = len(parts)
    ins, weight, outs, column, sems = (
        refs[:count], refs[count], refs[count + 1 : 2 * count + 1], refs[2 * count + 1], refs[2 * count + 2 :]
    )
    greet_all()
    run = Gather([(a, b, natural(a.shape[0]), p) for a, b, p in zip(ins, outs, parts)], *sems[:3])
    deal = Deal([(weight, column, natural(columns))], *sems[3:])
    run.start()
    deal.start()
    for step in range(3):
        run.step(step)
    run.finish()
    deal.finish()


def gather(arrays, parts, weight, columns, collective_id):
    count = len(arrays)
    outs = [((group * a.shape[0],) + a.shape[1:], a.dtype) for a in arrays]
    outs.append(((2 * 8 * weight.shape[0], columns), bf16))
    return pl.pallas_call(
        functools.partial(gather_kernel, parts, columns),
        in_specs=[ANY] * (count + 1),
        out_specs=[ANY] * (count + 1),
        out_shape=[jax.ShapeDtypeStruct(shape, kind) for shape, kind in outs],
        scratch_shapes=Gather.scratch(count) + Deal.scratch(1),
        compiler_params=pltpu.CompilerParams(collective_id=collective_id, has_side_effects=True),
        cost_estimate=busy,
        name=f"gather{collective_id}",
    )(*arrays, weight)


class Scatter:
    def __init__(self, own, core_in, side_in, core_s, core_r, side_s, side_r):
        self.own, self.core_in, self.side_in = own, core_in, side_in
        self.core_s, self.core_r, self.side_s, self.side_r = core_s, core_r, side_s, side_r
        self.me = place()[0]
        self.core = self.me % 2
        self.rows, self.width = own.shape[2], own.shape[3]
        self.part = self.width // 3

    def cols(self, part):
        return pl.ds(part * self.part, self.part)

    def order(self, part):
        return [sides[(part + k) % 3] for k in range(3)]

    def core_copy(self, part):
        c = self.cols(part)
        return remote(
            self.own.at[1 - self.core, :, :, c], self.core_in.at[:, :, c],
            self.core_s.at[part], self.core_r.at[part], self.me ^ 1,
        )

    def moves(self, part, step):
        order = self.order(part)
        masks = [0]
        for side in order[:step:-1]:
            masks = masks + [m ^ side for m in masks]
        base = {0: 0, 1: 4, 2: 6}[step]
        masks = sorted(masks, key=lambda m: [not m & side for side in order[step + 1 :]])
        return [(m ^ order[step], base + j) for j, m in enumerate(masks)]

    def side_copy(self, part, step, mask, slot):
        c = self.cols(part)
        peer = self.me ^ self.order(part)[step]
        return remote(
            self.own.at[self.core, (self.me ^ mask) // 2, :, c], self.side_in.at[slot, :, c],
            self.side_s.at[part, slot], self.side_r.at[part, slot], peer,
        )

    def multiply(self, part, lhs, rhs):
        c = self.cols(part)
        chunk = 4 * self.rows
        for q in range(4):
            p = dot(lhs[q * chunk : (q + 1) * chunk, :], rhs[part * self.part : (part + 1) * self.part, :], 1, 1)
            p = p.astype(bf16).reshape(4, self.rows, self.part)
            for j in range(4):
                self.own[j % 2, 2 * q + j // 2, :, c] = p[j]
        self.core_copy(part).start()

    def add(self, number, part, extra):
        c = self.cols(part)
        at = (self.core, number // 2, slice(None), c)
        self.own[at] = (self.own[at].astype(f32) + extra.astype(f32)).astype(bf16)

    def merge(self, part):
        c = self.cols(part)
        self.core_copy(part).wait()
        moves = self.moves(part, 0)
        for mask, slot in moves:
            self.add(self.me ^ mask, part, self.core_in[(self.me ^ mask) // 2, :, c])
            self.side_copy(part, 0, mask, slot).start()
        for mask, _ in moves:
            number = self.me ^ mask ^ self.order(part)[0]
            self.add(number, part, self.core_in[number // 2, :, c])

    def halve(self, part, step, out=None):
        c = self.cols(part)
        leaving = dict(self.moves(part, step + 1)) if step < 2 else {}
        for mask, slot in self.moves(part, step):
            kept = mask ^ self.order(part)[step]
            self.side_copy(part, step, mask, slot).wait_recv()
            if out is not None:
                at = (self.core, self.me // 2, slice(None), c)
                out[:, c] = self.own[at].astype(f32) + self.side_in[slot, :, c].astype(f32)
                continue
            self.add(self.me ^ kept, part, self.side_in[slot, :, c])
            if kept in leaving:
                self.side_copy(part, step + 1, kept, leaving[kept]).start()

    def finish(self):
        for part in range(3):
            for step in range(3):
                for mask, slot in self.moves(part, step):
                    self.side_copy(part, step, mask, slot).wait_send()

    @staticmethod
    def scratch(rows, width):
        return [
            pltpu.VMEM((2, 8, rows, width), bf16), pltpu.VMEM((8, rows, width), bf16),
            pltpu.VMEM((7, rows, width), bf16), DMA((3,)), DMA((3,)), DMA((3, 7)), DMA((3, 7)),
        ]


def cargo_refs(cross, swap, ins, outs, sems):
    cube = place()[1]
    pairs = []
    for src, dst, whole in zip(ins, outs, list(cross) + [True] * swap):
        if not whole:
            rows = dst.shape[0]
            src = src.at[pl.ds(pl.multiple_of((1 - cube) * rows, rows), rows)]
        pairs.append((src, dst))
    return Cargo(pairs[: len(cross)], pairs[len(cross) :], sems)


def cargo_shapes(cross, swap):
    shapes = []
    for array, whole in cross:
        rows = array.shape[0] if whole else array.shape[0] // 2
        shapes.append(jax.ShapeDtypeStruct((rows,) + array.shape[1:], array.dtype))
    return shapes + [jax.ShapeDtypeStruct(a.shape, a.dtype) for a in swap]


def scatter_kernel(cross, swap, lhs, rhs, *refs):
    count = len(cross) + swap
    ins, out, outs, sems, scratch = refs[:count], refs[count], refs[count + 1 : 2 * count + 1], refs[2 * count + 1], refs[2 * count + 2 :]
    greet(cross=bool(cross), swap=bool(swap))
    cargo = cargo_refs(cross, swap, ins, outs, sems)
    cargo.start()
    run = Scatter(*scratch)
    run.multiply(0, lhs, rhs)
    run.multiply(1, lhs, rhs)
    run.merge(0)
    run.multiply(2, lhs, rhs)
    run.merge(1)
    run.merge(2)
    for step in range(3):
        for part in range(3):
            run.halve(part, step, out if step == 2 else None)
    run.finish()
    cargo.finish()


def scatter(lhs, rhs, collective_id, cross=(), swap=()):
    rows, width = lhs.shape[0] // group, rhs.shape[0]
    count = len(cross) + len(swap)
    return pl.pallas_call(
        functools.partial(scatter_kernel, tuple(whole for _, whole in cross), len(swap)),
        in_specs=[VMEM, VMEM] + [ANY] * count,
        out_specs=[VMEM] + [ANY] * count,
        out_shape=[jax.ShapeDtypeStruct((rows, width), f32)] + cargo_shapes(cross, swap),
        scratch_shapes=[DMA((2, max(count, 1)))] + Scatter.scratch(rows, width),
        compiler_params=pltpu.CompilerParams(
            collective_id=collective_id, has_side_effects=True, vmem_limit_bytes=56 * 2**20
        ),
        cost_estimate=busy,
        name=f"scatter{collective_id}",
    )(lhs, rhs, *[a for a, _ in cross], *swap)


def head_of(number, heads):
    return number * heads // group


def is_active(number, heads):
    return (number + 1) * heads // group > number * heads // group


def owner_of(head, heads):
    return ((head + 1) * group + heads - 1) // heads - 1


class Deal:
    def __init__(self, items, send_sem, recv_sem, local_sem):
        self.items, self.send_sem, self.recv_sem, self.local_sem = items, send_sem, recv_sem, local_sem
        self.me = everywhere()

    def views(self, item, source, target):
        own, out, column = self.items[item]
        rows, width = own.shape[0] // 2, out.shape[1]
        number, cube = anyone(source)
        half = pl.ds(pl.multiple_of(number // 8 * rows, rows), rows)
        row = (cube * 8 + number % 8) * (2 * rows) + number // 8 * rows
        cols = pl.ds(column(anyone(target)[0]), width)
        return own.at[half, cols], out.at[pl.ds(pl.multiple_of(row, rows), rows)]

    def copy(self, item, source, target):
        src, dst = self.views(item, source, target)
        return pltpu.make_async_remote_copy(
            src_ref=src, dst_ref=dst, send_sem=self.send_sem.at[item, target],
            recv_sem=self.recv_sem.at[item, source], device_id=device(*anyone(target)), device_id_type=MESH,
        )

    def local(self, item):
        src, dst = self.views(item, self.me, self.me)
        return pltpu.make_async_copy(src, dst, self.local_sem.at[item])

    def start(self):
        def begin(mask, carry):
            for i in range(len(self.items)):
                self.copy(i, self.me, self.me ^ mask).start()
            return carry

        lax.fori_loop(1, 2 * group, begin, 0)
        for i in range(len(self.items)):
            self.local(i).start()

    def finish(self):
        def end(mask, carry):
            for i in range(len(self.items)):
                self.copy(i, self.me ^ mask, self.me).wait_recv()
                self.copy(i, self.me, self.me ^ mask).wait_send()
            return carry

        lax.fori_loop(1, 2 * group, end, 0)
        for i in range(len(self.items)):
            self.local(i).wait()

    @staticmethod
    def scratch(count):
        return [DMA((count, 2 * group)), DMA((count, 2 * group)), DMA((count,))]


def first_kernel(
    head_width, heads, given, places, gain, w_q, w_k, w_v, tokens, tokens_all, places_all, w_head,
    land, places_land, normed, cargo_sem, *sems,
):
    greet_all()
    cargo = Cargo([], [(given, land), (places, places_land)], cargo_sem)
    cargo.start()
    column = lambda number: pl.multiple_of(head_of(number, heads) * head_width, head_width)
    deal = Deal(
        [
            (w, w_head.at[:, pl.ds(i * head_width, head_width)], column)
            for i, w in enumerate((w_q, w_k, w_v))
        ],
        *sems[3:],
    )
    deal.start()
    cargo.finish()
    value = land[...].astype(f32)
    factor = lax.rsqrt(jnp.mean(value * value, axis=-1, keepdims=True) + norm_eps)
    normed[...] = (value * factor * gain[...]).astype(bf16)
    run = Gather(
        [(normed, tokens_all, natural(normed.shape[0]), 3), (places_land, places_all, natural(1), 1)], *sems[:3]
    )
    run.start()
    tokens[...] = land[...]
    for step in range(3):
        run.step(step)
    run.finish()
    deal.finish()


def first_exchange(given, places, gain, weights, heads, head_width, collective_id):
    rows, width = given.shape
    outs = [
        ((rows, width), bf16), ((group * rows, width), bf16), ((group,) + places.shape[1:], jnp.int32),
        ((width, 3 * head_width), bf16),
    ]
    return pl.pallas_call(
        functools.partial(first_kernel, head_width, heads),
        in_specs=[VMEM, VMEM, VMEM] + [ANY] * 3,
        out_specs=[VMEM] + [ANY] * 3,
        out_shape=[jax.ShapeDtypeStruct(shape, kind) for shape, kind in outs],
        scratch_shapes=[
            pltpu.VMEM((rows, width), bf16), pltpu.VMEM(places.shape, jnp.int32),
            pltpu.VMEM((rows, width), bf16), DMA((2, 2)),
        ] + Gather.scratch(2) + Deal.scratch(3),
        compiler_params=pltpu.CompilerParams(
            collective_id=collective_id, has_side_effects=True, vmem_limit_bytes=32 * 2**20
        ),
        cost_estimate=busy,
        name="first_exchange",
    )(given, places, gain, *weights)


class Restore:
    def __init__(self, grads, land, sources, column, send_sem, recv_sem, local_sem):
        self.grads, self.land, self.sources, self.column = grads, land, sources, column
        self.send_sem, self.recv_sem, self.local_sem = send_sem, recv_sem, local_sem
        self.me = place()[0]
        self.count, self.rows = land.shape[0], land.shape[1]
        self.width = grads.shape[1] // self.count

    def move(self, i, source, target):
        rows = pl.ds(pl.multiple_of(target % 8 * self.rows, self.rows), self.rows)
        src = self.grads.at[rows, pl.ds(i * self.width, self.width)]
        return src, self.land.at[i, :, pl.ds(self.column(source), self.width)]

    def send(self, i, source, target):
        src, dst = self.move(i, source, target)
        return remote(src, dst, self.send_sem.at[i, target], self.recv_sem.at[i, source], target)

    def keep(self, i):
        src, dst = self.move(i, self.me, self.me)
        return pltpu.make_async_copy(src, dst, self.local_sem.at[i])

    def start(self):
        def begin(mask, carry):
            for i in range(self.count):
                pl.when(self.sources(self.me))(lambda: self.send(i, self.me, self.me ^ mask).start())
            return carry

        lax.fori_loop(1, group, begin, 0)
        for i in range(self.count):
            pl.when(self.sources(self.me))(lambda: self.keep(i).start())

    def finish(self):
        def taken(mask, carry):
            for i in range(self.count):
                other = self.me ^ mask
                pl.when(self.sources(other))(lambda: self.send(i, other, self.me).wait_recv())
                pl.when(self.sources(self.me))(lambda: self.send(i, self.me, other).wait_send())
            return carry

        lax.fori_loop(1, group, taken, 0)
        for i in range(self.count):
            pl.when(self.sources(self.me))(lambda: self.keep(i).wait())

    @staticmethod
    def scratch(count, rows, total):
        return [
            pltpu.VMEM((count, rows, total), bf16), DMA((count, group)), DMA((count, group)), DMA((count,)),
        ]


def last_kernel(
    heads, head_width, columns, ffn, head, small, out_sum, output, *refs,
):
    outs, (total_out, pair_out, output_out), refs = refs[:6], refs[6:9], refs[9:]
    ffn_land, *ffn_sems = refs[:4]
    head_land, *head_sems = refs[4:8]
    land, send_sem, recv_sem, pair_sem, cargo_sem = refs[8:]
    me = everywhere()
    greet_all()
    cargo = Cargo([], [(output, output_out)], cargo_sem)
    pair = remote(out_sum, pair_out, pair_sem.at[0], pair_sem.at[1], place()[0] ^ 8)

    def send(source, target):
        return pltpu.make_async_remote_copy(
            src_ref=small, dst_ref=land.at[source], send_sem=send_sem.at[target],
            recv_sem=recv_sem.at[source], device_id=device(*anyone(target)), device_id_type=MESH,
        )

    def begin(mask, carry):
        send(me, me ^ mask).start()
        return carry

    def taken(mask, carry):
        send(me ^ mask, me).wait_recv()
        send(me, me ^ mask).wait_send()
        return carry

    lax.fori_loop(1, 2 * group, begin, 0)
    land[me] = small[...]
    pair.start()
    cargo.start()
    first = Restore(ffn, ffn_land, lambda n: n >= 0, natural(columns), *ffn_sems)
    column = lambda n: pl.multiple_of(head_of(n, heads) * head_width, head_width)
    second = Restore(head, head_land, lambda n: is_active(n, heads), column, *head_sems)
    second.start()
    first.start()
    lax.fori_loop(1, 2 * group, taken, 0)
    result = land[0]
    for number in range(1, 2 * group):
        result = result + land[number]
    total_out[...] = result
    second.finish()
    for i in range(3):
        outs[3 + i][...] = head_land[i].astype(f32)
    first.finish()
    for i in range(3):
        outs[i][...] = ffn_land[i].astype(f32)
    pair.wait()
    cargo.finish()


def last_exchange(ffn, head, small, out_sum, output, heads, columns, collective_id):
    rows, width = out_sum.shape
    head_width = head.shape[1] // 3
    hidden = columns * group
    outs = [((rows, hidden), f32)] * 3 + [((rows, width), f32)] * 3
    outs += [(small.shape, f32), (out_sum.shape, bf16), (output.shape, bf16)]
    return pl.pallas_call(
        functools.partial(last_kernel, heads, head_width, columns),
        in_specs=[ANY, ANY, VMEM, ANY, ANY],
        out_specs=[VMEM] * 7 + [ANY] * 2,
        out_shape=[jax.ShapeDtypeStruct(shape, kind) for shape, kind in outs],
        scratch_shapes=Restore.scratch(3, rows, hidden) + Restore.scratch(3, rows, width) + [
            pltpu.VMEM((2 * group,) + small.shape, f32), DMA((2 * group,)), DMA((2 * group,)),
            DMA((2,)), DMA((2, 1)),
        ],
        compiler_params=pltpu.CompilerParams(
            collective_id=collective_id, has_side_effects=True, vmem_limit_bytes=48 * 2**20
        ),
        cost_estimate=busy,
        name="last_exchange",
    )(ffn, head, small, out_sum, output)


def rotated(value, cosine, sine, inverse=False):
    parts = []
    step = cosine.shape[0]
    sign = -1.0 if inverse else 1.0
    for start in range(0, value.shape[0], 2 * step):
        first = value[start : start + step]
        second = value[start + step : start + 2 * step]
        parts.append(first * cosine - sign * (second * sine))
        parts.append(second * cosine + sign * (first * sine))
    return jnp.concatenate(parts, axis=0)


def forward_kernel(
    block, share, lam_ref, qkv_ref, cos_ref, sin_ref, gain_ref, *refs,
):
    step = pl.program_id(0)
    if share:
        (w_one, w_two, w_rows, given), refs = refs[:4], refs[4:]
    q_ref, k_ref, v_ref, kt_ref, o1_ref, o2_ref, lse_ref, *refs = refs
    if share:
        out_ref, both_ref, w_all, taken_ref = refs[:4]
        qt_ref, vt_ref, att_ref, w_land, send_sem, recv_sem, local_sem, cargo_sem, *sems = refs[4:]
        me, cube = place()
        columns = both_ref.shape[1] // 2
        deal = Deal(
            [
                (w, both_ref.at[:, pl.ds(i * columns, columns)], natural(columns))
                for i, w in enumerate((w_one, w_two))
            ],
            *sems[3:],
        )
        sub = w_land.shape[0]
        w_half = w_rows.at[pl.ds(pl.multiple_of(me // 8 * sub, sub), sub)]

        def spot(which):
            return lambda number: pl.multiple_of((which * 8 + number % 8) * (2 * sub) + number // 8 * sub, sub)

        run = Gather([(w_half, w_all, spot(cube), 3), (w_land, w_all, spot(1 - cube), 3)], *sems[:3])
        rows_cargo = Cargo([(w_half, w_land)], [], cargo_sem.at[0])
        token_cargo = Cargo([], [(given, taken_ref)], cargo_sem.at[1])

        @pl.when(step == 0)
        def _():
            greet_all()
            rows_cargo.start()
            run.start([0])
            token_cargo.start()
            deal.start()

        @pl.when(step == 1)
        def _():
            rows_cargo.finish()
            run.start([1])
            run.step(0, [0])

        @pl.when(step == 2)
        def _():
            run.step(1, [0])
            run.step(0, [1])

        @pl.when(step == 3)
        def _():
            run.step(2, [0])
            run.step(1, [1])
    else:
        att_ref, qt_ref, vt_ref = refs
    width = v_ref.shape[1]
    half = width // 2
    length = q_ref.shape[0]
    scale = half ** -0.5 * log2e

    @pl.when(step == 0)
    def _():
        def prepare(index, carry):
            cols = pl.ds(pl.multiple_of(index * block, block), block)
            cosine, sine = cos_ref[:, cols], sin_ref[:, cols]
            query = rotated(qkv_ref[0:width, cols], cosine, sine)
            key = rotated(qkv_ref[width : 2 * width, cols], cosine, sine)
            value = qkv_ref[2 * width : 3 * width, cols]
            qt_ref[:, cols] = query.astype(bf16)
            kt_ref[:, cols] = key.astype(bf16)
            vt_ref[:, cols] = value.astype(bf16)
            q_ref[cols, :] = query.T.astype(bf16)
            k_ref[cols, :] = key.T.astype(bf16)
            v_ref[cols, :] = value.T.astype(bf16)
            return carry

        lax.fori_loop(0, length // block, prepare, 0)

    own = pl.ds(pl.multiple_of(step * block, block), block)
    queries = qt_ref[:, own]
    key_ids = lax.broadcasted_iota(jnp.int32, (block, block), 0)
    query_ids = lax.broadcasted_iota(jnp.int32, (block, block), 1)

    def visit(index, state, diagonal):
        rows = pl.ds(pl.multiple_of(index * block, block), block)
        values = vt_ref[:, rows]
        out = []
        for part in range(2):
            top, total, acc = state[part]
            lo, hi = part * half, (part + 1) * half
            scores = dot(k_ref[rows, lo:hi], queries[lo:hi]) * scale
            if diagonal:
                scores = jnp.where(key_ids <= query_ids, scores, neg_large)
            new_top = jnp.maximum(top, jnp.max(scores, axis=0, keepdims=True))
            weights = jnp.exp2(scores - new_top)
            fade = jnp.exp2(top - new_top)
            total = total * fade + jnp.sum(weights, axis=0, keepdims=True)
            acc = acc * fade + dot(values, weights.astype(bf16))
            out.append((new_top, total, acc))
        return tuple(out)

    start = tuple(
        (
            jnp.full((1, block), neg_large, f32),
            jnp.zeros((1, block), f32),
            jnp.zeros((width, block), f32),
        )
        for _ in range(2)
    )
    state = lax.fori_loop(0, step, lambda index, now: visit(index, now, False), start)
    state = visit(step, state, True)
    outs = []
    for part, ref in ((0, o1_ref), (1, o2_ref)):
        top, total, acc = state[part]
        result = acc / total
        ref[:, own] = result
        lse_ref[pl.ds(part, 1), own] = top + jnp.log2(total)
        outs.append(result)
    mixed = outs[0] - lam_ref[0] * outs[1]
    factor = lax.rsqrt(jnp.mean(mixed * mixed, axis=0, keepdims=True) + norm_eps)
    attended = mixed * factor * gain_ref[...] * (1.0 - lam_init)
    att_ref[own, :] = attended.T.astype(bf16)
    if share:
        rows, heads = out_ref.shape[0], out_ref.shape[1] // width
        active = is_active(me, heads)

        def part(number, head):
            cols = pl.ds(pl.multiple_of(head * width, width), width)
            return att_ref.at[pl.ds(pl.multiple_of(number * rows, rows), rows)], out_ref.at[:, cols]

        def send(number, head):
            src, dst = part(number, head)
            return remote(src, dst, send_sem.at[number], recv_sem.at[head], number)

        def keep():
            src, dst = part(me, head_of(me, heads))
            return pltpu.make_async_copy(src, dst, local_sem.at[0])

        for j in range(block // rows):
            number = step * (block // rows) + j
            pl.when(active & (number != me))(lambda: send(number, head_of(me, heads)).start())
            pl.when(active & (number == me))(lambda: keep().start())

        @pl.when(step == pl.num_programs(0) - 1)
        def _():
            def sent(number, carry):
                pl.when(active & (number != me))(lambda: send(number, 0).wait_send())
                return carry

            def taken(head, carry):
                pl.when(owner_of(head, heads) != me)(lambda: send(me, head).wait_recv())
                return carry

            lax.fori_loop(0, heads, taken, 0)
            lax.fori_loop(0, group, sent, 0)
            pl.when(active)(lambda: keep().wait())
            run.step(2, [1])
            run.finish()
            token_cargo.finish()
            deal.finish()


def forward_attention(lam, qkv, cosine, sine, gain, block, weights=(), rows=0, heads=0, columns=0, collective_id=None):
    width = qkv.shape[0] // 3
    length = qkv.shape[1]
    full = lambda shape: pl.BlockSpec(shape, lambda i: (0,) * len(shape))
    outs = [
        ((length, width), bf16),
        ((length, width), bf16),
        ((length, width), bf16),
        ((width, length), bf16),
        ((width, length), f32),
        ((width, length), f32),
        ((8, length), f32),
    ]
    scratch = [pltpu.VMEM((width, length), bf16), pltpu.VMEM((width, length), bf16)]
    out_specs = [full(shape) for shape, _ in outs]
    share = bool(weights)
    if share:
        wide = heads * width
        more = [((rows, wide), bf16), ((wide, 2 * columns), bf16), ((wide, wide), bf16), ((rows, wide), bf16)]
        outs, out_specs = outs + more, out_specs + [ANY] * 4
        scratch += [
            pltpu.VMEM((length, width), bf16), pltpu.VMEM((weights[2].shape[0] // 2, wide), bf16),
            DMA((group,)), DMA((heads,)), DMA((1,)), DMA((2, 2, 1)),
        ]
        scratch += Gather.scratch(2) + Deal.scratch(2)
    else:
        outs, out_specs = outs + [((length, width), bf16)], out_specs + [full((length, width))]
    return pl.pallas_call(
        functools.partial(forward_kernel, block, share),
        grid=(length // block,),
        in_specs=[SMEM] + [full(a.shape) for a in (qkv, cosine, sine, gain)] + [ANY] * len(weights),
        out_specs=out_specs,
        out_shape=[jax.ShapeDtypeStruct(shape, kind) for shape, kind in outs],
        scratch_shapes=scratch,
        compiler_params=pltpu.CompilerParams(
            dimension_semantics=("arbitrary",), vmem_limit_bytes=56 * 2**20,
            collective_id=collective_id, has_side_effects=share,
        ),
        cost_estimate=busy,
        name="attention_forward",
    )(lam, qkv, cosine, sine, gain, *weights)


def backward_kernel(
    block, share, lam_ref, q_ref, k_ref, v_ref, kt_ref, o1_ref, o2_ref, lse_ref, datt_ref,
    cos_ref, sin_ref, gain_ref, *refs,
):
    if share:
        cargo_in, refs = refs[0], refs[1:]
    dqkv_ref, dgain_ref, dlam_ref, *refs = refs
    if share:
        cargo_out, refs = refs[0], refs[1:]
    dmix_ref, dmixt_ref, delta_ref, dqt_ref, *refs = refs
    if share:
        cargo_sem, *refs = refs
        cargo = cargo_refs((False,), 0, [cargo_in], [cargo_out], cargo_sem)
    step = pl.program_id(0)
    blocks = pl.num_programs(0)
    width = v_ref.shape[1]
    half = width // 2
    length = q_ref.shape[0]
    scale = half ** -0.5
    lam = lam_ref[0]
    used = lam_ref[1] > 0.0

    @pl.when(step == 0)
    def _():
        if share:
            greet_all()
            collect(cargo, datt_ref, *refs)
        source = refs[0] if share else datt_ref
        dgain_ref[...] = jnp.zeros_like(dgain_ref)
        dlam_ref[...] = jnp.zeros_like(dlam_ref)
        dqt_ref[...] = jnp.zeros_like(dqt_ref)

        def prepare(index, carry):
            cols = pl.ds(pl.multiple_of(index * block, block), block)
            first, second = o1_ref[:, cols], o2_ref[:, cols]
            mixed = first - lam * second
            factor = lax.rsqrt(jnp.mean(mixed * mixed, axis=0, keepdims=True) + norm_eps)
            upstream = source[cols, :].astype(f32).T * (1.0 - lam_init)
            dgain_ref[...] += jnp.sum(upstream * mixed * factor, axis=1, keepdims=True)
            scaled = upstream * gain_ref[...]
            dmixed = factor * scaled - mixed * (factor * factor * factor) * jnp.mean(
                scaled * mixed, axis=0, keepdims=True
            )
            low = dmixed.astype(bf16)
            back = low.astype(f32)
            dmixt_ref[:, cols] = low
            dmix_ref[cols, :] = back.T.astype(bf16)
            along_second = jnp.sum(back * second, axis=0, keepdims=True)
            delta_ref[0:1, cols] = jnp.sum(back * first, axis=0, keepdims=True)
            delta_ref[1:2, cols] = -lam * along_second
            dlam_ref[...] -= jnp.sum(along_second, axis=1, keepdims=True)
            return carry

        lax.fori_loop(0, length // block, prepare, 0)

    own = pl.ds(pl.multiple_of(step * block, block), block)
    key_ids = lax.broadcasted_iota(jnp.int32, (block, block), 0)
    query_ids = lax.broadcasted_iota(jnp.int32, (block, block), 1)
    keys = k_ref[own, :]
    keys_t = kt_ref[:, own]
    values = v_ref[own, :]

    def visit(index, state, diagonal):
        dkeys, dvalues = state
        cols = pl.ds(pl.multiple_of(index * block, block), block)
        queries = q_ref[cols, :]
        dmix = dmix_ref[cols, :]
        dprob = dot(values, dmixt_ref[:, cols])
        new_keys = []
        blend = None
        for part in range(2):
            lo, hi = part * half, (part + 1) * half
            scores = dot(keys[:, lo:hi], queries[:, lo:hi], 1, 1) * (scale * log2e)
            weights = jnp.exp2(scores - lse_ref[pl.ds(part, 1), cols])
            if diagonal:
                weights = jnp.where(key_ids <= query_ids, weights, 0.0)
            delta = delta_ref[part : part + 1, cols]
            if part == 0:
                blend = weights
                dscore = (weights * (dprob - delta)).astype(bf16)
            else:
                blend = blend - lam * weights
                dscore = (weights * (-lam * dprob - delta)).astype(bf16)
            new_keys.append(dkeys[part] + dot(dscore, queries[:, lo:hi]))
            dqt_ref[lo:hi, cols] += dot(keys_t[lo:hi], dscore)
        dvalues = dvalues + dot(blend.astype(bf16), dmix)
        return tuple(new_keys), dvalues

    start = (
        (jnp.zeros((block, half), f32), jnp.zeros((block, half), f32)),
        jnp.zeros((block, width), f32),
    )
    state = visit(step, start, True)
    dkeys, dvalues = lax.fori_loop(
        step + 1, blocks, lambda index, now: visit(index, now, False), state
    )
    both = jnp.where(used, jnp.concatenate(dkeys, axis=1).T * scale, 0.0)
    dqkv_ref[own, width : 2 * width] = (
        rotated(both, cos_ref[:, own], sin_ref[:, own], True).T.astype(bf16)
    )
    dqkv_ref[own, 2 * width : 3 * width] = jnp.where(used, dvalues, 0.0).astype(bf16)

    dqkv_ref[own, 0:width] = (
        rotated(jnp.where(used, dqt_ref[:, own] * scale, 0.0), cos_ref[:, own], sin_ref[:, own], True).T.astype(bf16)
    )
    if share:
        pl.when(step == blocks - 1)(lambda: cargo.finish())


def collect(cargo, grad_ref, out_ref, send_sem, recv_sem, local_sem):
    me = place()[0]
    rows = grad_ref.shape[0]
    width = out_ref.shape[1]
    heads = grad_ref.shape[1] // width
    active = is_active(me, heads)

    def move(head, number):
        src = grad_ref.at[:, pl.ds(pl.multiple_of(head * width, width), width)]
        dst = out_ref.at[pl.ds(pl.multiple_of(number * rows, rows), rows)]
        return src, dst

    def send(head, number):
        src, dst = move(head, number)
        return remote(src, dst, send_sem.at[head], recv_sem.at[number], owner_of(head, heads))

    def keep():
        src, dst = move(head_of(me, heads), me)
        return pltpu.make_async_copy(src, dst, local_sem.at[0])

    def begin(head, carry):
        pl.when(owner_of(head, heads) != me)(lambda: send(head, me).start())
        return carry

    def taken(number, carry):
        pl.when(active & (number != me))(lambda: send(0, number).wait_recv())
        return carry

    def sent(head, carry):
        pl.when(owner_of(head, heads) != me)(lambda: send(head, me).wait_send())
        return carry

    lax.fori_loop(0, heads, begin, 0)
    pl.when(active)(lambda: keep().start())
    cargo.start()
    lax.fori_loop(0, group, taken, 0)
    pl.when(active)(lambda: keep().wait())
    lax.fori_loop(0, heads, sent, 0)


def backward_attention(lam, q, k, v, kt, o1, o2, lse, datt, cosine, sine, gain, block, cargo=None, collective_id=None):
    length, width = q.shape
    full = lambda shape: pl.BlockSpec(shape, lambda i: (0,) * len(shape))
    arrays = (q, k, v, kt, o1, o2, lse, datt, cosine, sine, gain)
    outs = [((length, 3 * width), bf16), ((width, 1), f32), ((1, 1), f32)]
    share = collective_id is not None
    more, cargo_out, cargo_in = [], [], []
    if share:
        cargo_out, cargo_in = cargo_shapes([(cargo, False)], ()), [cargo]
        more = [DMA((2, 1)), pltpu.VMEM((length, width), bf16), DMA((datt.shape[1] // width,)), DMA((group,)), DMA((1,))]
    return pl.pallas_call(
        functools.partial(backward_kernel, block, share),
        grid=(length // block,),
        in_specs=[SMEM] + [full(a.shape) for a in arrays] + [ANY] * len(cargo_in),
        out_specs=[full(shape) for shape, _ in outs] + [ANY] * len(cargo_in),
        out_shape=[jax.ShapeDtypeStruct(shape, kind) for shape, kind in outs] + cargo_out,
        scratch_shapes=[
            pltpu.VMEM((length, width), bf16),
            pltpu.VMEM((width, length), bf16),
            pltpu.VMEM((8, length), f32),
            pltpu.VMEM((width, length), f32),
        ] + more,
        compiler_params=pltpu.CompilerParams(
            dimension_semantics=("arbitrary",), vmem_limit_bytes=56 * 2**20,
            collective_id=collective_id, has_side_effects=share,
        ),
        cost_estimate=busy,
        name="attention_backward",
    )(lam, *arrays, *cargo_in)


def rms_parts(value):
    return lax.rsqrt(jnp.mean(value * value, axis=-1, keepdims=True) + norm_eps)


def rms_back(value, factor, gain, upstream):
    scaled = upstream * gain
    mean = jnp.mean(scaled * value, axis=-1, keepdims=True)
    grad = factor * scaled - value * (factor * factor * factor) * mean
    return grad, jnp.sum(upstream * value * factor, axis=0)


def cube_body(
    block_input, positions, needle, cotangent, norm_gain1, w_query, w_key, w_value,
    lam_q1, lam_k1, lam_q2, lam_k2, sub_gain, w_out, norm_gain2, w_gate, w_up, w_down,
):
    rows, width = block_input.shape[1:]
    heads, half = lam_q1.shape
    head_width = sub_gain.shape[0]
    hidden = w_gate.shape[1]
    depth = w_query.shape[0]
    length = rows * group
    columns = hidden // group
    y = lax.axis_index("batch")
    me, cube = place()
    my_head = head_of(me, heads)
    used = is_active(me, heads)
    active = used.astype(f32)
    here = jnp.broadcast_to(positions[0], (1, 8, rows))
    tokens_low, normed_all, places, w_head = first_exchange(
        block_input[0], here, norm_gain1[None], (w_query, w_key, w_value), heads, head_width, 0
    )
    tokens = tokens_low.astype(f32)
    factor1 = rms_parts(tokens)
    upstream = cotangent[0].astype(f32) * needle[0].astype(f32)[:, None]
    upstream_low = upstream.astype(bf16)
    places = places[:, 0].reshape(length)

    inv_freq = jnp.exp(-math.log(10000.0) * jnp.arange(half // 2, dtype=f32) / (half // 2))
    angles = inv_freq[:, None] * places.astype(f32)[None, :]
    cosine, sine = jnp.cos(angles), jnp.sin(angles)
    lam_vals, lam_pull = jax.vjp(lambdas, lam_q1, lam_k1, lam_q2, lam_k2)
    lam_mine = jnp.stack([lax.dynamic_index_in_dim(lam_vals, my_head, 0, False), active])
    gain_col = sub_gain[:, None]
    block = 4 * rows

    qkv = dot(w_head, normed_all, 0, 1)
    q, k, v, kt, o1, o2, lse, attended, w_gates, w_o, grad_low = forward_attention(
        lam_mine, qkv, cosine, sine, gain_col, block,
        (w_gate, w_up, w_out, upstream_low), rows, heads, columns, 1,
    )
    resid = tokens + dot(attended, w_o)
    factor2 = rms_parts(resid)
    normed_two = (resid * factor2 * norm_gain2).astype(bf16)
    two_all, grad_all, w_d = gather([normed_two, grad_low], (3, 3), w_down, columns, 2)

    both = dot(two_all, w_gates)
    gate, upper = both[:, :columns], both[:, columns:]
    grad_inner = dot(grad_all, w_d)
    sigma = jax.nn.sigmoid(gate)
    silu = gate * sigma
    inner = (silu * upper).astype(bf16)
    gate_low = (grad_inner * upper * sigma * (1.0 + gate * (1.0 - sigma))).astype(bf16)
    upper_low = (grad_inner * silu).astype(bf16)
    gates_low = jnp.concatenate([gate_low, upper_low], axis=1)
    gate_grads = dot(two_all, gates_low, 0, 0).astype(bf16)
    down_grads = dot(grad_all, inner, 0, 0).astype(bf16)
    early = jnp.concatenate([gate_grads[:, :columns], down_grads[:, : columns // 2]], axis=1)
    later = jnp.concatenate([gate_grads[:, columns:], down_grads[:, columns // 2 :]], axis=1)
    grad_two, early_theirs = scatter(gates_low, w_gates, 3, [(early, False)])

    grad_resid_two, gain_two = rms_back(resid, factor2, norm_gain2, grad_two)
    grad_resid = grad_low.astype(f32) + grad_resid_two
    resid_low = grad_resid.astype(bf16)
    grad_att = dot(resid_low, w_o, 1, 1).astype(bf16)

    def combine(mine, theirs):
        part = mine.shape[0] // 2
        mine = lax.dynamic_slice_in_dim(mine, cube * part, part, 0)
        return (mine.astype(f32) + theirs.astype(f32)).astype(bf16)

    dqkv, dgain, dlam, later_theirs = backward_attention(
        lam_mine, q, k, v, kt, o1, o2, lse, grad_att, cosine, sine, gain_col, block, later, 4,
    )
    head_grads = dot(normed_all, dqkv, 0, 0).astype(bf16)
    grad_normed, head_theirs = scatter(dqkv, w_head, 8, [(head_grads, False)])
    grad_tokens, gain_one = rms_back(tokens, factor1, norm_gain1, grad_normed)
    input_low = (grad_resid + grad_tokens).astype(bf16)
    out_part, input_back = scatter(attended.T, resid_low.T, 7, [], [input_low])
    out_part = out_part.astype(bf16)
    ffn_out, out_theirs = scatter(inner, w_d, 5, [(out_part, True)])
    output_low = (resid + ffn_out).astype(bf16)
    out_sum = (out_part.astype(f32) + out_theirs.astype(f32)).astype(bf16)
    early_sum, later_sum = combine(early, early_theirs), combine(later, later_theirs)
    ffn_sum = jnp.concatenate(
        [early_sum[:, :columns], later_sum[:, :columns], early_sum[:, columns:], later_sum[:, columns:]], axis=1
    )

    hot = jax.nn.one_hot(my_head, heads, dtype=f32)
    mine = jnp.concatenate([dgain[:, 0], hot * dlam[0, 0]])
    small = jnp.concatenate([gain_one, gain_two, jnp.where(used, mine, 0.0)])
    count = small.shape[0]
    lanes = -(-count // 1024) * 128
    small = jnp.pad(small, (0, 8 * lanes - count)).reshape(8, lanes)
    *grads, small, out_pair, output_back = last_exchange(
        ffn_sum, combine(head_grads, head_theirs), small, out_sum, output_low, heads, columns, 6
    )
    small = small.reshape(-1)
    output = output_back[None]
    input_grad = input_back.astype(f32)[None]
    out_grads = jnp.where(y == cube, out_sum, out_pair).astype(f32)
    gain_one, gain_two = small[:width], small[width : 2 * width]
    sub_grad = small[2 * width : 2 * width + head_width]
    lam_grads = lam_pull(small[2 * width + head_width : count])
    squares = sum(jnp.sum(g * g) for g in lam_grads)
    return (
        output, input_grad, gain_one, grads[3], grads[4], grads[5],
        lam_grads[0], lam_grads[1], lam_grads[2], lam_grads[3], sub_grad, out_grads, gain_two,
        grads[0], grads[1], grads[2], jnp.mean(lam_vals), jnp.sqrt(squares),
    )


def gather_rows(value):
    return lax.all_gather(value, "seq", axis=0, tiled=True)


def scatter_sum(value):
    return lax.psum_scatter(value, "seq", scatter_dimension=0, tiled=True)


def exchange(value):
    return lax.all_to_all(value, "seq", split_axis=0, concat_axis=0, tiled=True)


def plain_body(
    devices, block_input, positions, needle, cotangent, norm_gain1, w_query, w_key, w_value,
    lam_q1, lam_k1, lam_q2, lam_k2, sub_gain, w_out, norm_gain2, w_gate, w_up, w_down,
):
    rows, width = block_input.shape[1:]
    heads, half = lam_q1.shape
    head_width = sub_gain.shape[0]
    hidden = w_gate.shape[1]
    depth = w_query.shape[0]
    length = rows * devices
    columns = hidden // devices
    head_of = [d * heads // devices for d in range(devices)]
    owner_of = [max(d for d in range(devices) if head_of[d] == h) for h in range(heads)]
    me = lax.axis_index("seq")
    my_head = me * heads // devices
    active = ((me + 1) * heads // devices > my_head).astype(f32)

    tokens = block_input[0].astype(f32)
    factor1 = rms_parts(tokens)
    normed = (tokens * factor1 * norm_gain1).astype(bf16)
    normed_all = gather_rows(normed)
    places = gather_rows(positions[0])

    by_head = jnp.stack([w.reshape(depth, heads, head_width) for w in (w_query, w_key, w_value)], 2)
    by_head = by_head.reshape(depth, heads, 3 * head_width).transpose(1, 0, 2)
    w_head = exchange(by_head[jnp.array(head_of)]).reshape(width, 3 * head_width)

    w_o = gather_rows(w_out)
    grad_out = cotangent[0].astype(f32) * needle[0].astype(f32)[:, None]
    grad_low = grad_out.astype(bf16)
    grad_all = gather_rows(grad_low)

    ffn = jnp.stack([w.reshape(depth, devices, columns) for w in (w_gate, w_up, w_down)], 2)
    ffn = ffn.reshape(depth, devices, 3 * columns).transpose(1, 0, 2)
    w_ffn = exchange(ffn).reshape(width, 3 * columns)

    inv_freq = jnp.exp(-math.log(10000.0) * jnp.arange(half // 2, dtype=f32) / (half // 2))
    angles = inv_freq[:, None] * places.astype(f32)[None, :]
    cosine, sine = jnp.cos(angles), jnp.sin(angles)
    lam_vals, lam_pull = jax.vjp(lambdas, lam_q1, lam_k1, lam_q2, lam_k2)
    lam_mine = jnp.stack([lax.dynamic_index_in_dim(lam_vals, my_head, 0, False), active])
    gain_col = sub_gain[:, None]
    block = math.gcd(length, 512)

    qkv = dot(w_head, normed_all, 0, 1)
    q, k, v, kt, o1, o2, lse, att = forward_attention(
        lam_mine, qkv, cosine, sine, gain_col, block
    )
    att_rows = exchange(att.reshape(devices, rows, head_width))
    attended = jnp.concatenate([att_rows[d] for d in owner_of], axis=1)
    resid = tokens + dot(attended, w_o)
    factor2 = rms_parts(resid)
    normed_two = (resid * factor2 * norm_gain2).astype(bf16)
    two_all = gather_rows(normed_two)

    both = dot(two_all, w_ffn[:, : 2 * columns])
    gate, upper = both[:, :columns], both[:, columns:]
    grad_inner = dot(grad_all, w_ffn[:, 2 * columns :])
    sigma = jax.nn.sigmoid(gate)
    silu = gate * sigma
    inner = (silu * upper).astype(bf16)
    gate_low = (grad_inner * upper * sigma * (1.0 + gate * (1.0 - sigma))).astype(bf16)
    upper_low = (grad_inner * silu).astype(bf16)
    gates_low = jnp.concatenate([gate_low, upper_low], axis=1)
    grad_two = scatter_sum(dot(gates_low, w_ffn[:, : 2 * columns], 1, 1).astype(bf16)).astype(f32)
    ffn_out = scatter_sum(dot(inner, w_ffn[:, 2 * columns :], 1, 1).astype(bf16)).astype(f32)
    output = (resid + ffn_out).astype(bf16)[None]

    grad_resid_two, gain_two = rms_back(resid, factor2, norm_gain2, grad_two)
    grad_resid = grad_out + grad_resid_two
    resid_low = grad_resid.astype(bf16)
    grad_att = dot(resid_low, w_o, 1, 1).astype(bf16)
    pieces = jnp.stack(
        [grad_att[:, h * head_width : (h + 1) * head_width] for h in head_of], axis=0
    )
    datt = exchange(pieces).reshape(length, head_width)

    dqkv, dgain, dlam = backward_attention(
        lam_mine, q, k, v, kt, o1, o2, lse, datt, cosine, sine, gain_col, block
    )
    partial = (dot(dqkv, w_head, 1, 1) * active).astype(bf16)
    grad_normed = scatter_sum(partial).astype(f32)
    grad_tokens, gain_one = rms_back(tokens, factor1, norm_gain1, grad_normed)
    input_grad = (grad_resid + grad_tokens)[None]

    def settle(value):
        other = lax.ppermute(value, "batch", [(0, 1), (1, 0)])
        return value.astype(f32) + other.astype(f32)

    ffn_grads = jnp.concatenate(
        [dot(two_all, gates_low, 0, 0), dot(grad_all, inner, 0, 0)], axis=1
    ).astype(bf16)
    ffn_grads = settle(exchange(ffn_grads.reshape(devices, depth, 3 * columns)))
    ffn_grads = ffn_grads.reshape(devices, depth, 3, columns).transpose(2, 1, 0, 3)
    ffn_grads = ffn_grads.reshape(3, depth, hidden)

    head_grads = dot(normed_all, dqkv, 0, 0).astype(bf16)
    head_grads = settle(exchange(head_grads.reshape(devices, depth, 3 * head_width)))
    head_grads = jnp.stack([head_grads[d] for d in owner_of], axis=1)
    head_grads = head_grads.reshape(depth, heads, 3, head_width).transpose(2, 0, 1, 3)
    head_grads = head_grads.reshape(3, depth, width)

    out_grads = dot(attended, resid_low, 0, 0).astype(bf16)
    out_grads = settle(scatter_sum(out_grads))

    hot = jax.nn.one_hot(my_head, heads, dtype=f32) * active
    small = lax.psum(
        (gain_one, gain_two, dgain[:, 0] * active, hot * dlam[0, 0]), ("batch", "seq")
    )
    lam_grads = lam_pull(small[3])
    squares = sum(jnp.sum(g * g) for g in lam_grads)
    return (
        output, input_grad, small[0], head_grads[0], head_grads[1], head_grads[2],
        lam_grads[0], lam_grads[1], lam_grads[2], lam_grads[3], small[2], out_grads, small[1],
        ffn_grads[0], ffn_grads[1], ffn_grads[2], jnp.mean(lam_vals), jnp.sqrt(squares),
    )


def solution(mesh):
    rows = P("seq", None)
    in_specs = (
        P("batch", "seq", None), P("batch", "seq"), P("batch", "seq"), P("batch", "seq", None),
        P(), rows, rows, rows, P(), P(), P(), P(), P(), rows, P(), rows, rows, rows,
    )
    out_specs = (
        P("batch", "seq", None), P("batch", "seq", None), P(), rows, rows, rows,
        P(), P(), P(), P(), P(), rows, P(), rows, rows, rows, P(), P(),
    )
    if mesh.shape["seq"] == group and mesh.shape["batch"] == 2:
        body = cube_body
    else:
        body = functools.partial(plain_body, mesh.shape["seq"])
    return jax.shard_map(body, mesh=mesh, in_specs=in_specs, out_specs=out_specs, check_vma=False)
```

```python
import functools
import math

import jax
import jax.numpy as jnp
from jax import lax
from jax.experimental import pallas as pl
from jax.experimental.pallas import tpu as pltpu
from jax.sharding import PartitionSpec as P

lam_init = 0.619
norm_eps = 1e-05
log2e = math.log2(math.e)
neg_large = -1e30
f32 = jnp.float32
bf16 = jnp.bfloat16


def lambdas(lam_q1, lam_k1, lam_q2, lam_k2):
    return (
        jnp.exp(jnp.sum(lam_q1 * lam_k1, axis=-1))
        - jnp.exp(jnp.sum(lam_q2 * lam_k2, axis=-1))
        + lam_init
    )


def dims(left_axis, right_axis):
    return (((left_axis,), (right_axis,)), ((), ()))


def dot(left, right, left_axis=1, right_axis=0):
    return lax.dot_general(left, right, dims(left_axis, right_axis), preferred_element_type=f32)


MESH = pl.DeviceIdType.MESH
ANY = pl.BlockSpec(memory_space=pltpu.HBM)
VMEM = pl.BlockSpec(memory_space=pltpu.VMEM)
SMEM = pl.BlockSpec(memory_space=pltpu.SMEM)
DMA = pltpu.SemaphoreType.DMA
group = 16
busy = pl.CostEstimate(flops=4 * 10**10, bytes_accessed=10**7, transcendentals=0)
sides = (8, 4, 2)
even = ((8, 4, 2), (4, 2, 8), (2, 8, 4))
few_z = ((4, 8, 2), (4, 2, 8))
mid_z = ((4, 8, 2), (4, 2, 8), (2, 4, 8), (8, 4, 2))
sum_even = ((2, 8, 4), (8, 2, 4), (4, 2, 8))
sum_few_z = ((2, 8, 4), (8, 2, 4))


def place():
    seq = lax.axis_index("seq")
    return lax.axis_index("batch") * 8 + seq % 8, seq // 8


def device(number, cube=None):
    return {"batch": number // 8, "seq": (place()[1] if cube is None else cube) * 8 + number % 8}


def partner():
    return {"batch": lax.axis_index("batch"), "seq": lax.axis_index("seq") ^ 8}


def swapped():
    batch, seq = lax.axis_index("batch"), lax.axis_index("seq")
    return {"batch": 1 - batch, "seq": seq ^ 8}, batch != seq // 8


def anyone(index):
    return index // group * 8 + index % 8, index % group // 8


def everywhere():
    return lax.axis_index("batch") * group + lax.axis_index("seq")


def remote(src, dst, send_sem, recv_sem, number):
    return pltpu.make_async_remote_copy(
        src_ref=src, dst_ref=dst, send_sem=send_sem, recv_sem=recv_sem,
        device_id=device(number), device_id_type=MESH,
    )


def greet(cross=False, swap=False):
    me = place()[0]
    barrier = pltpu.get_barrier_semaphore()
    count = 1 + len(sides)
    for mask in (1,) + sides:
        pl.semaphore_signal(barrier, inc=1, device_id=device(me ^ mask), device_id_type=MESH)
    if cross:
        pl.semaphore_signal(barrier, inc=1, device_id=partner(), device_id_type=MESH)
        count = count + 1
    if swap:
        target, moved = swapped()

        @pl.when(moved)
        def _():
            pl.semaphore_signal(barrier, inc=1, device_id=target, device_id_type=MESH)

        count = count + moved.astype(jnp.int32)
    pl.semaphore_wait(barrier, count)


def greet_all():
    barrier = pltpu.get_barrier_semaphore()
    me = everywhere()

    def tell(mask, carry):
        target = device(*anyone(me ^ mask))
        pl.semaphore_signal(barrier, inc=1, device_id=target, device_id_type=MESH)
        return carry

    lax.fori_loop(1, 2 * group, tell, 0)
    pl.semaphore_wait(barrier, 2 * group - 1)


class Cargo:
    def __init__(self, cross, swap, sems):
        self.cross, self.swap, self.sems = cross, swap, sems

    def copies(self):
        for i, (src, dst) in enumerate(self.cross):
            yield None, pltpu.make_async_remote_copy(
                src_ref=src, dst_ref=dst, send_sem=self.sems.at[0, i], recv_sem=self.sems.at[1, i],
                device_id=partner(), device_id_type=MESH,
            ), None
        target, moved = swapped()
        for i, (src, dst) in enumerate(self.swap):
            j = len(self.cross) + i
            yield moved, pltpu.make_async_remote_copy(
                src_ref=src, dst_ref=dst, send_sem=self.sems.at[0, j], recv_sem=self.sems.at[1, j],
                device_id=target, device_id_type=MESH,
            ), pltpu.make_async_copy(src, dst, self.sems.at[0, j])

    def start(self):
        for moved, far, near in self.copies():
            if moved is None:
                far.start()
            else:
                pl.when(moved)(lambda: far.start())
                pl.when(jnp.logical_not(moved))(lambda: near.start())

    def finish(self):
        for moved, far, near in self.copies():
            if moved is None:
                far.wait()
            else:
                pl.when(moved)(lambda: far.wait())
                pl.when(jnp.logical_not(moved))(lambda: near.wait())


class Gather:
    def __init__(self, orders, items, send_sem, recv_sem, local_sem):
        self.orders = orders
        self.items = [item if len(item) == 4 else item + (len(orders),) for item in items]
        self.send_sem, self.recv_sem, self.local_sem = send_sem, recv_sem, local_sem
        self.me = place()[0]

    def order(self, part):
        return list(self.orders[part])

    def view(self, item, part, number):
        src, out, row, parts = self.items[item]
        rows, width = src.shape[0], src.shape[-1] // parts
        at = pl.ds(row(number), rows)
        if parts == 1:
            return out.at[at]
        return out.at[at, pl.ds(part * width, width)]

    def copy(self, item, part, number, lane, target, own=False):
        src, out, row, parts = self.items[item]
        width = src.shape[-1] // parts
        here = self.view(item, part, number)
        source = (src if parts == 1 else src.at[:, pl.ds(part * width, width)]) if own else here
        arrival = self.recv_sem.at[item, 0, group] if lane == 3 else self.recv_sem.at[item, part, number]
        return remote(source, here, self.send_sem.at[item], arrival, target)

    def every(self):
        return [(i, p) for i in range(len(self.items)) for p in range(self.items[i][3])]

    def local(self, item):
        src, out, row, _ = self.items[item]
        return pltpu.make_async_copy(src, out.at[pl.ds(row(self.me), src.shape[0])], self.local_sem.at[item])

    def start(self, items=None):
        chosen = [(i, p) for i, p in self.every() if items is None or i in items]
        for k in range(3):
            for i, p in chosen:
                self.copy(i, p, self.me, k, self.me ^ self.order(p)[k], True).start()
        for i, p in chosen:
            self.copy(i, p, self.me, 3, self.me ^ 1, True).start()
        for i in range(len(self.items)):
            if items is None or i in items:
                self.local(i).start()

    def arrivals(self, part, step):
        order = self.order(part)
        masks = [0]
        for side in order[:step]:
            masks = masks + [m ^ side for m in masks]
        return [m ^ order[step] for m in masks]

    def step(self, step, items=None):
        for i, p in self.every():
            if items is not None and i not in items:
                continue
            for mask in self.arrivals(p, step):
                number = self.me ^ mask
                self.copy(i, p, number, 0, self.me).wait_recv()
                for k in range(step + 1, 3):
                    self.copy(i, p, number, k, self.me ^ self.order(p)[k]).start()
                self.copy(i, p, number, 3, self.me ^ 1).start()

    def finish(self, items=None):
        for i in range(len(self.items)):
            if items is None or i in items:
                src, out = self.items[i][:2]
                for blocks, sem in ((8, self.recv_sem.at[i, 0, group]), (15, self.send_sem.at[i])):
                    some = out.at[pl.ds(0, blocks * src.shape[0])]
                    pltpu.make_async_copy(some, some, sem).wait()
                self.local(i).wait()

    @staticmethod
    def scratch(count):
        return [DMA((count,)), DMA((count, 4, group + 1)), DMA((count,))]


def natural(rows):
    return lambda number: pl.multiple_of(number * rows, rows)


def second_kernel(normed, given, grads, normed_all, grads_all, cargo_sem, *sems):
    greet(swap=True)
    cargo = Cargo([], [(given, grads)], cargo_sem)
    cargo.start()
    row = natural(normed.shape[0])
    run = Gather(even, [(normed, normed_all, row), (grads, grads_all, row)], *sems[:3])
    run.start([0])
    run.step(0, [0])
    run.step(1, [0])
    cargo.finish()
    run.start([1])
    run.step(2, [0])
    for step in range(3):
        run.step(step, [1])
    run.finish()


def second_exchange(normed, given, collective_id):
    rows, width = normed.shape
    outs = [(rows, width), (group * rows, width), (group * rows, width)]
    return pl.pallas_call(
        second_kernel,
        in_specs=[ANY] * 2,
        out_specs=[ANY] * 3,
        out_shape=[jax.ShapeDtypeStruct(shape, bf16) for shape in outs],
        scratch_shapes=[DMA((2, 1))] + Gather.scratch(2),
        compiler_params=pltpu.CompilerParams(collective_id=collective_id, has_side_effects=True),
        cost_estimate=busy,
        name="second_exchange",
    )(normed, given)


class Scatter:
    def __init__(self, orders, own, core_in, side_in, core_s, core_r, side_s, side_r):
        self.orders, self.parts = orders, len(orders)
        self.own, self.core_in, self.side_in = own, core_in, side_in
        self.core_s, self.core_r, self.side_s, self.side_r = core_s, core_r, side_s, side_r
        self.me = place()[0]
        self.core = self.me % 2
        self.rows, self.width = own.shape[2], own.shape[3]
        self.part = self.width // self.parts

    def cols(self, part):
        return pl.ds(part * self.part, self.part)

    def order(self, part):
        return list(self.orders[part])

    def core_copy(self, part):
        c = self.cols(part)
        return remote(
            self.own.at[1 - self.core, :, :, c], self.core_in.at[:, :, c],
            self.core_s.at[part], self.core_r.at[part], self.me ^ 1,
        )

    def moves(self, part, step):
        order = self.order(part)
        masks = [0]
        for side in order[:step:-1]:
            masks = masks + [m ^ side for m in masks]
        base = {0: 0, 1: 4, 2: 6}[step]
        masks = sorted(masks, key=lambda m: [not m & side for side in order[step + 1 :]])
        return [(m ^ order[step], base + j) for j, m in enumerate(masks)]

    def side_copy(self, part, step, mask, slot):
        c = self.cols(part)
        peer = self.me ^ self.order(part)[step]
        return remote(
            self.own.at[self.core, (self.me ^ mask) // 2, :, c], self.side_in.at[slot, :, c],
            self.side_s.at[part, slot], self.side_r.at[part, slot], peer,
        )

    def multiply(self, part, lhs, rhs):
        c = self.cols(part)
        chunk = 4 * self.rows

        def quarter(q, carry):
            left = lhs[pl.ds(pl.multiple_of(q * chunk, chunk), chunk), :]
            p = dot(left, rhs[part * self.part : (part + 1) * self.part, :], 1, 1)
            p = p.astype(bf16).reshape(4, self.rows, self.part)
            for j in range(4):
                self.own[j % 2, 2 * q + j // 2, :, c] = p[j]
            return carry

        lax.fori_loop(0, 4, quarter, 0)
        self.core_copy(part).start()

    def add(self, number, part, extra):
        c = self.cols(part)
        at = (self.core, number // 2, slice(None), c)
        self.own[at] = (self.own[at].astype(f32) + extra.astype(f32)).astype(bf16)

    def merge(self, part):
        c = self.cols(part)
        self.core_copy(part).wait()
        moves = self.moves(part, 0)
        for mask, slot in moves:
            self.add(self.me ^ mask, part, self.core_in[(self.me ^ mask) // 2, :, c])
            self.side_copy(part, 0, mask, slot).start()
        for mask, _ in moves:
            number = self.me ^ mask ^ self.order(part)[0]
            self.add(number, part, self.core_in[number // 2, :, c])

    def begin(self, lhs, rhs):
        self.multiply(0, lhs, rhs)
        for part in range(1, self.parts):
            self.multiply(part, lhs, rhs)
            self.merge(part - 1)
        self.merge(self.parts - 1)

    def halve(self, part, step, out=None):
        c = self.cols(part)
        leaving = dict(self.moves(part, step + 1)) if step < 2 else {}
        for mask, slot in self.moves(part, step):
            kept = mask ^ self.order(part)[step]
            self.side_copy(part, step, mask, slot).wait_recv()
            if out is not None:
                at = (self.core, self.me // 2, slice(None), c)
                out[:, c] = self.own[at].astype(f32) + self.side_in[slot, :, c].astype(f32)
                continue
            self.add(self.me ^ kept, part, self.side_in[slot, :, c])
            if kept in leaving:
                self.side_copy(part, step + 1, kept, leaving[kept]).start()

    def halve_all(self, step, out):
        for part in range(self.parts):
            self.halve(part, step, out if step == 2 else None)

    def finish(self):
        for part in range(self.parts):
            for step in range(3):
                for mask, slot in self.moves(part, step):
                    self.side_copy(part, step, mask, slot).wait_send()

    @staticmethod
    def scratch(rows, width):
        return [
            pltpu.VMEM((2, 8, rows, width), bf16), pltpu.VMEM((8, rows, width), bf16),
            pltpu.VMEM((7, rows, width), bf16), DMA((4,)), DMA((4,)), DMA((4, 7)), DMA((4, 7)),
        ]


def for_partner(grads, rows):
    return grads.at[pl.ds(pl.multiple_of((1 - place()[1]) * rows, rows), rows)]


def scatter_kernel(lhs, rhs, lhs_two, rhs_two, given, out, out_two, taken, cargo_sem, *scratch):
    greet(cross=True)
    cargo = Cargo([(for_partner(given, taken.shape[0]), taken)], [], cargo_sem)
    run, more = Scatter(sum_even, *scratch[:7]), Scatter(sum_even, *scratch[7:])
    run.begin(lhs, rhs)
    more.begin(lhs_two, rhs_two)
    cargo.start()
    for step in range(3):
        run.halve_all(step, out)
        more.halve_all(step, out_two)
    run.finish()
    more.finish()
    cargo.finish()


def scatter(lhs, rhs, lhs_two, rhs_two, given, collective_id):
    rows, width = lhs.shape[0] // group, rhs.shape[0]
    return pl.pallas_call(
        scatter_kernel,
        in_specs=[VMEM] * 4 + [ANY],
        out_specs=[VMEM, VMEM, ANY],
        out_shape=[jax.ShapeDtypeStruct((rows, width), f32)] * 2
        + [jax.ShapeDtypeStruct((given.shape[0] // 2, given.shape[1]), bf16)],
        scratch_shapes=[DMA((2, 1))] + Scatter.scratch(rows, width) + Scatter.scratch(rows, width),
        compiler_params=pltpu.CompilerParams(
            collective_id=collective_id, has_side_effects=True, vmem_limit_bytes=56 * 2**20
        ),
        cost_estimate=busy,
        name=f"scatter{collective_id}",
    )(lhs, rhs, lhs_two, rhs_two, given)


def head_of(number, heads):
    return number * heads // group


def is_active(number, heads):
    return (number + 1) * heads // group > number * heads // group


def owner_of(head, heads):
    return ((head + 1) * group + heads - 1) // heads - 1


class Deal:
    def __init__(self, items, send_sem, recv_sem):
        self.items, self.send_sem, self.recv_sem = items, send_sem, recv_sem
        self.me = everywhere()

    def views(self, item, source, target):
        own, out, column = self.items[item]
        rows, width = own.shape[0] // 2, out.shape[1]
        number, cube = anyone(source)
        half = pl.ds(pl.multiple_of(number // 8 * rows, rows), rows)
        row = (cube * 8 + number % 8) * (2 * rows) + number // 8 * rows
        cols = pl.ds(column(anyone(target)[0]), width)
        return own.at[half, cols], out.at[pl.ds(pl.multiple_of(row, rows), rows)]

    def copy(self, item, source, target, far):
        src, dst = self.views(item, source, target)
        return pltpu.make_async_remote_copy(
            src_ref=src, dst_ref=dst, send_sem=self.send_sem.at[item, far],
            recv_sem=self.recv_sem.at[item, far], device_id=device(*anyone(target)), device_id_type=MESH,
        )

    def local(self, item):
        src, dst = self.views(item, self.me, self.me)
        return pltpu.make_async_copy(src, dst, self.recv_sem.at[item, 0])

    def whole(self, item, sem, blocks):
        own, out, _ = self.items[item]
        some = out.at[pl.ds(0, blocks * own.shape[0] // 2)]
        pltpu.make_async_copy(some, some, sem).wait()

    def start_near(self):
        def begin(mask, carry):
            for i in range(len(self.items)):
                self.copy(i, self.me, self.me ^ (mask % 8 + mask // 8 * group), 0).start()
            return carry

        lax.fori_loop(1, group, begin, 0)
        for i in range(len(self.items)):
            self.local(i).start()

    def start_far(self):
        def begin(mask, carry):
            for i in range(len(self.items)):
                self.copy(i, self.me, self.me ^ (8 + mask % 8 + mask // 8 * group), 1).start()
            return carry

        lax.fori_loop(0, group, begin, 0)

    def finish_near(self):
        for i in range(len(self.items)):
            self.whole(i, self.recv_sem.at[i, 0], group)
            self.whole(i, self.send_sem.at[i, 0], group - 1)

    def finish_far(self):
        for i in range(len(self.items)):
            self.whole(i, self.recv_sem.at[i, 1], group)
            self.whole(i, self.send_sem.at[i, 1], group)

    @staticmethod
    def scratch(count):
        return [DMA((count, 2)), DMA((count, 2))]


def first_kernel(
    head_width, heads, columns, given, places, gain, w_q, w_k, w_v, w_down,
    tokens, tokens_all, places_all, w_head, w_d, land, places_land, normed, cargo_sem, *sems,
):
    greet_all()
    cargo = Cargo([], [(given, land), (places, places_land)], cargo_sem)
    cargo.start()
    column = lambda number: pl.multiple_of(head_of(number, heads) * head_width, head_width)
    deal = Deal(
        [
            (w, w_head.at[:, pl.ds(i * head_width, head_width)], column)
            for i, w in enumerate((w_q, w_k, w_v))
        ],
        *sems[3:5],
    )
    own = natural(columns)
    down = Deal([(w_down, w_d, own)], *sems[5:7])
    deal.start_near()
    down.start_near()
    cargo.finish()
    value = land[...].astype(f32)
    factor = lax.rsqrt(jnp.mean(value * value, axis=-1, keepdims=True) + norm_eps)
    normed[...] = (value * factor * gain[...]).astype(bf16)
    run = Gather(
        mid_z, [(normed, tokens_all, natural(normed.shape[0])), (places_land, places_all, natural(1), 1)], *sems[:3]
    )
    run.start()
    deal.start_far()
    tokens[...] = land[...]
    run.step(0)
    down.start_far()
    run.step(1)
    run.step(2)
    run.finish()
    for some in (deal, down):
        some.finish_near()
        some.finish_far()


def gate_deal(w_gate, w_up, w_gates, sems):
    columns = w_gates.shape[1] // 2
    views = [w_gates.at[:, pl.ds(i * columns, columns)] for i in range(2)]
    return Deal([(w, view, natural(columns)) for w, view in zip((w_gate, w_up), views)], *sems)


def first_exchange(given, places, gain, weights, heads, head_width, columns, collective_id):
    rows, width = given.shape
    outs = [
        ((rows, width), bf16), ((group * rows, width), bf16), ((group,) + places.shape[1:], jnp.int32),
        ((width, 3 * head_width), bf16), ((width, columns), bf16),
    ]
    return pl.pallas_call(
        functools.partial(first_kernel, head_width, heads, columns),
        in_specs=[VMEM, VMEM, VMEM] + [ANY] * 4,
        out_specs=[VMEM] + [ANY] * 4,
        out_shape=[jax.ShapeDtypeStruct(shape, kind) for shape, kind in outs],
        scratch_shapes=[
            pltpu.VMEM((rows, width), bf16), pltpu.VMEM(places.shape, jnp.int32),
            pltpu.VMEM((rows, width), bf16), DMA((2, 2)),
        ] + Gather.scratch(2) + Deal.scratch(3) + Deal.scratch(1),
        compiler_params=pltpu.CompilerParams(
            collective_id=collective_id, has_side_effects=True, vmem_limit_bytes=60 * 2**20
        ),
        cost_estimate=busy,
        name="first_exchange",
    )(given, places, gain, *weights)


class Restore:
    def __init__(self, grads, land, sources, column, send_sem, recv_sem, local_sem):
        self.grads, self.land, self.sources, self.column = grads, land, sources, column
        self.send_sem, self.recv_sem, self.local_sem = send_sem, recv_sem, local_sem
        self.me = place()[0]
        self.count, self.rows = land.shape[0], land.shape[1]
        self.width = grads.shape[1] // self.count
        self.blocks = land.shape[2] // self.width // 2

    def move(self, i, source, target):
        rows = pl.ds(pl.multiple_of(target % 8 * self.rows, self.rows), self.rows)
        src = self.grads.at[rows, pl.ds(i * self.width, self.width)]
        return src, self.land.at[i, :, pl.ds(self.column(source), self.width)]

    def send(self, i, source, target):
        src, dst = self.move(i, source, target)
        return remote(src, dst, self.send_sem.at[i, 0], self.recv_sem.at[i, source], target)

    def keep(self, i):
        src, dst = self.move(i, self.me, self.me)
        return pltpu.make_async_copy(src, dst, self.local_sem.at[i])

    def pass_on(self, i, source):
        here = self.move(i, source, self.me)[1]
        return remote(here, here, self.send_sem.at[i, 1], self.recv_sem.at[i, group], self.me ^ 8)

    def start(self):
        mine = self.sources(self.me)

        def begin(mask, carry):
            for i in range(self.count):
                pl.when(mine)(lambda: self.send(i, self.me, self.me ^ mask).start())
            return carry

        lax.fori_loop(1, 8, begin, 0)
        for i in range(self.count):
            pl.when(mine)(lambda: self.keep(i).start())

    def middle(self):
        mine = self.sources(self.me)

        def forward(mask, carry):
            other = self.me ^ mask
            for i in range(self.count):

                @pl.when(self.sources(other))
                def _():
                    self.send(i, other, self.me).wait_recv()
                    self.pass_on(i, other).start()

            return carry

        for i in range(self.count):

            @pl.when(mine)
            def _():
                self.keep(i).wait()
                self.pass_on(i, self.me).start()

        lax.fori_loop(1, 8, forward, 0)

    def finish(self):
        mine = self.sources(self.me)

        def wait(i, blocks, sem):
            some = self.land.at[i, :, pl.ds(0, blocks * self.width)]
            pltpu.make_async_copy(some, some, sem).wait()

        for i in range(self.count):
            pl.when(mine)(lambda: wait(i, 7, self.send_sem.at[i, 0]))
            wait(i, self.blocks, self.send_sem.at[i, 1])
            wait(i, self.blocks, self.recv_sem.at[i, group])

    @staticmethod
    def scratch(count):
        return [DMA((count, 2)), DMA((count, group + 1)), DMA((count,))]


def last_kernel(
    heads, head_width, columns,
    dqkv, w_head, tokens, gain, grad_resid, head, small, ffn_sum, out_sum,
    ffn_out, head_out, pair_out, total_out, input_out,
    result8, input_low, small_all, small_land, head_land, head_sum,
    cargo_sem, pair_sem, total_send, total_recv, *refs,
):
    me, cube = place()
    width = tokens.shape[1]
    greet_all()
    run = Scatter(sum_even, *refs[:7])
    sems = refs[7:]
    column = lambda n: pl.multiple_of(head_of(n, heads) * head_width, head_width)
    ffn_back = Restore(ffn_sum, ffn_out, lambda n: n >= 0, natural(columns), *sems[0:3])
    head_back = Restore(head_sum, head_out, lambda n: is_active(n, heads), column, *sems[3:6])
    half = head_land.shape[0]
    head_cargo = Cargo([(for_partner(head, half), head_land)], [], cargo_sem.at[0])
    input_cargo = Cargo([], [(input_low, input_out)], cargo_sem.at[1])
    small_cargo = Cargo([(small_all.at[me], small_land)], [], cargo_sem.at[3])
    pair = remote(out_sum, pair_out, pair_sem.at[0], pair_sem.at[1], me ^ 8)

    def send(source, target):
        return remote(
            small_all.at[me], small_all.at[source], total_send.at[target], total_recv.at[source], target
        )

    head_cargo.start()
    run.begin(dqkv, w_head)
    ffn_back.start()
    pair.start()
    run.halve_all(0, None)
    run.halve_all(1, None)
    ffn_back.middle()
    run.halve_all(2, result8)

    value = tokens[...].astype(f32)
    factor = lax.rsqrt(jnp.mean(value * value, axis=-1, keepdims=True) + norm_eps)
    upstream = result8[...]
    scaled = upstream * gain[...]
    mean = jnp.mean(scaled * value, axis=-1, keepdims=True)
    grad = factor * scaled - value * (factor * factor * factor) * mean
    input_low[...] = (grad_resid[...] + grad).astype(bf16)
    input_cargo.start()
    gain_one = jnp.sum(upstream * value * factor, axis=0, keepdims=True)
    small_all[me] = small[...]
    for i in range(width // head_width):
        small_all[me, i : i + 1, :] = gain_one[:, i * head_width : (i + 1) * head_width]
    small_cargo.start()
    head_cargo.finish()
    mine = pl.ds(pl.multiple_of(cube * half, half), half)
    head_sum[...] = (head[mine, :].astype(f32) + head_land[...].astype(f32)).astype(bf16)
    head_back.start()
    small_cargo.finish()
    small_all[me] = small_all[me] + small_land[...]

    def begin(mask, carry):
        send(me, me ^ mask).start()
        return carry

    lax.fori_loop(1, group, begin, 0)
    head_back.middle()

    def taken(mask, carry):
        send(me ^ mask, me).wait_recv()
        send(me, me ^ mask).wait_send()
        return carry

    lax.fori_loop(1, group, taken, 0)
    result = small_all[0]
    for number in range(1, group):
        result = result + small_all[number]
    total_out[...] = result
    pair.wait()
    run.finish()
    input_cargo.finish()
    ffn_back.finish()
    head_back.finish()


def last_exchange(arrays, heads, head_width, columns, collective_id):
    dqkv, w_head, tokens, gain, grad_resid, head, small, ffn_sum, out_sum = arrays
    rows, width = tokens.shape
    part = out_sum.shape[0]
    half = (head.shape[0] // 2, head.shape[1])
    outs = [
        ((1, part, columns * group), bf16), ((3, part, width), bf16), (out_sum.shape, bf16),
        (small.shape, f32), ((rows, width), bf16),
    ]
    memory = pltpu.VMEM
    return pl.pallas_call(
        functools.partial(last_kernel, heads, head_width, columns),
        in_specs=[VMEM] * 7 + [ANY] * 2,
        out_specs=[ANY, ANY, ANY, VMEM, ANY],
        out_shape=[jax.ShapeDtypeStruct(shape, kind) for shape, kind in outs],
        scratch_shapes=[
            memory((rows, width), f32), memory((rows, width), bf16),
            memory((group,) + small.shape, f32), memory(small.shape, f32), memory(half, bf16), memory(half, bf16),
            DMA((4, 2, 1)), DMA((2,)), DMA((group,)), DMA((group,)),
        ]
        + Scatter.scratch(rows, width) + Restore.scratch(1) + Restore.scratch(3),
        compiler_params=pltpu.CompilerParams(
            collective_id=collective_id, has_side_effects=True, vmem_limit_bytes=48 * 2**20
        ),
        cost_estimate=busy,
        name="last_exchange",
    )(*arrays)


def rotated(value, cosine, sine, inverse=False):
    parts = []
    step = cosine.shape[0]
    sign = -1.0 if inverse else 1.0
    for start in range(0, value.shape[0], 2 * step):
        first = value[start : start + step]
        second = value[start + step : start + 2 * step]
        parts.append(first * cosine - sign * (second * sine))
        parts.append(second * cosine + sign * (first * sine))
    return jnp.concatenate(parts, axis=0)


def forward_kernel(
    block, share, lam_ref, qkv_ref, cos_ref, sin_ref, gain_ref, *refs,
):
    step = pl.program_id(0)
    if share:
        (w_one, w_two, w_rows), refs = refs[:3], refs[3:]
    q_ref, k_ref, v_ref, kt_ref, o1_ref, o2_ref, lse_ref, *refs = refs
    if share:
        out_ref, both_ref, w_all = refs[:3]
        qt_ref, vt_ref, att_ref, w_land, send_sem, recv_sem, local_sem, cargo_sem, *sems = refs[3:]
        me, cube = place()
        deal = gate_deal(w_one, w_two, both_ref, sems[3:])
        sub = w_land.shape[0]
        w_half = w_rows.at[pl.ds(pl.multiple_of(me // 8 * sub, sub), sub)]

        def spot(which):
            return lambda number: pl.multiple_of((which * 8 + number % 8) * (2 * sub) + number // 8 * sub, sub)

        run = Gather(few_z, [(w_half, w_all, spot(cube)), (w_land, w_all, spot(1 - cube))], *sems[:3])
        rows_cargo = Cargo([(w_half, w_land)], [], cargo_sem)

        @pl.when(step == 0)
        def _():
            greet_all()
            rows_cargo.start()
            run.start([0])
            deal.start_near()

        @pl.when(step == 1)
        def _():
            rows_cargo.finish()
            run.start([1])
            deal.start_far()

        @pl.when(step == 2)
        def _():
            run.step(0)

        @pl.when(step == 3)
        def _():
            run.step(1)
    else:
        att_ref, qt_ref, vt_ref = refs
    width = v_ref.shape[1]
    half = width // 2
    length = q_ref.shape[0]
    scale = half ** -0.5 * log2e

    @pl.when(step == 0)
    def _():
        def prepare(index, carry):
            cols = pl.ds(pl.multiple_of(index * block, block), block)
            cosine, sine = cos_ref[:, cols], sin_ref[:, cols]
            query = rotated(qkv_ref[0:width, cols], cosine, sine)
            key = rotated(qkv_ref[width : 2 * width, cols], cosine, sine)
            value = qkv_ref[2 * width : 3 * width, cols]
            qt_ref[:, cols] = query.astype(bf16)
            kt_ref[:, cols] = key.astype(bf16)
            vt_ref[:, cols] = value.astype(bf16)
            q_ref[cols, :] = query.T.astype(bf16)
            k_ref[cols, :] = key.T.astype(bf16)
            v_ref[cols, :] = value.T.astype(bf16)
            return carry

        lax.fori_loop(0, length // block, prepare, 0)

    own = pl.ds(pl.multiple_of(step * block, block), block)
    queries = qt_ref[:, own]
    key_ids = lax.broadcasted_iota(jnp.int32, (block, block), 0)
    query_ids = lax.broadcasted_iota(jnp.int32, (block, block), 1)

    def visit(index, state, diagonal):
        rows = pl.ds(pl.multiple_of(index * block, block), block)
        values = vt_ref[:, rows]
        out = []
        for part in range(2):
            top, total, acc = state[part]
            lo, hi = part * half, (part + 1) * half
            scores = dot(k_ref[rows, lo:hi], queries[lo:hi]) * scale
            if diagonal:
                scores = jnp.where(key_ids <= query_ids, scores, neg_large)
            new_top = jnp.maximum(top, jnp.max(scores, axis=0, keepdims=True))
            weights = jnp.exp2(scores - new_top)
            fade = jnp.exp2(top - new_top)
            total = total * fade + jnp.sum(weights, axis=0, keepdims=True)
            acc = acc * fade + dot(values, weights.astype(bf16))
            out.append((new_top, total, acc))
        return tuple(out)

    start = tuple(
        (
            jnp.full((1, block), neg_large, f32),
            jnp.zeros((1, block), f32),
            jnp.zeros((width, block), f32),
        )
        for _ in range(2)
    )
    state = lax.fori_loop(0, step, lambda index, now: visit(index, now, False), start)
    state = visit(step, state, True)
    outs = []
    for part, ref in ((0, o1_ref), (1, o2_ref)):
        top, total, acc = state[part]
        result = acc / total
        ref[:, own] = result
        lse_ref[pl.ds(part, 1), own] = top + jnp.log2(total)
        outs.append(result)
    mixed = outs[0] - lam_ref[0] * outs[1]
    factor = lax.rsqrt(jnp.mean(mixed * mixed, axis=0, keepdims=True) + norm_eps)
    attended = mixed * factor * gain_ref[...] * (1.0 - lam_init)
    att_ref[own, :] = attended.T.astype(bf16)
    if share:
        rows, heads = out_ref.shape[0], out_ref.shape[1] // width
        active = is_active(me, heads)

        def part(number, head):
            cols = pl.ds(pl.multiple_of(head * width, width), width)
            return att_ref.at[pl.ds(pl.multiple_of(number * rows, rows), rows)], out_ref.at[:, cols]

        def send(number, head):
            src, dst = part(number, head)
            return remote(src, dst, send_sem.at[number], recv_sem.at[head], number)

        def keep():
            src, dst = part(me, head_of(me, heads))
            return pltpu.make_async_copy(src, dst, local_sem.at[0])

        for j in range(block // rows):
            number = step * (block // rows) + j
            pl.when(active & (number != me))(lambda: send(number, head_of(me, heads)).start())
            pl.when(active & (number == me))(lambda: keep().start())

        @pl.when(step == pl.num_programs(0) - 1)
        def _():
            def sent(number, carry):
                pl.when(active & (number != me))(lambda: send(number, 0).wait_send())
                return carry

            def taken(head, carry):
                pl.when(owner_of(head, heads) != me)(lambda: send(me, head).wait_recv())
                return carry

            lax.fori_loop(0, heads, taken, 0)
            lax.fori_loop(0, group, sent, 0)
            pl.when(active)(lambda: keep().wait())
            run.step(2)
            run.finish()
            deal.finish_near()
            deal.finish_far()


def forward_attention(lam, qkv, cosine, sine, gain, block, weights=(), rows=0, heads=0, columns=0, collective_id=None):
    width = qkv.shape[0] // 3
    length = qkv.shape[1]
    full = lambda shape: pl.BlockSpec(shape, lambda i: (0,) * len(shape))
    outs = [
        ((length, width), bf16),
        ((length, width), bf16),
        ((length, width), bf16),
        ((width, length), bf16),
        ((width, length), f32),
        ((width, length), f32),
        ((8, length), f32),
    ]
    scratch = [pltpu.VMEM((width, length), bf16), pltpu.VMEM((width, length), bf16)]
    out_specs = [full(shape) for shape, _ in outs]
    share = bool(weights)
    if share:
        wide = heads * width
        more = [((rows, wide), bf16), ((wide, 2 * columns), bf16), ((wide, wide), bf16)]
        outs, out_specs = outs + more, out_specs + [ANY] * 3
        scratch += [
            pltpu.VMEM((length, width), bf16), pltpu.VMEM((weights[2].shape[0] // 2, wide), bf16),
            DMA((group,)), DMA((heads,)), DMA((1,)), DMA((2, 1)),
        ]
        scratch += Gather.scratch(2) + Deal.scratch(2)
    else:
        outs, out_specs = outs + [((length, width), bf16)], out_specs + [full((length, width))]
    return pl.pallas_call(
        functools.partial(forward_kernel, block, share),
        grid=(length // block,),
        in_specs=[SMEM] + [full(a.shape) for a in (qkv, cosine, sine, gain)] + [ANY] * len(weights),
        out_specs=out_specs,
        out_shape=[jax.ShapeDtypeStruct(shape, kind) for shape, kind in outs],
        scratch_shapes=scratch,
        compiler_params=pltpu.CompilerParams(
            dimension_semantics=("arbitrary",), vmem_limit_bytes=56 * 2**20,
            collective_id=collective_id, has_side_effects=share,
        ),
        cost_estimate=busy,
        name="attention_forward",
    )(lam, qkv, cosine, sine, gain, *weights)


def backward_kernel(
    block, share, lam_ref, q_ref, k_ref, v_ref, kt_ref, o1_ref, o2_ref, lse_ref, datt_ref,
    cos_ref, sin_ref, gain_ref, *refs,
):
    if share:
        (left_ref, right_ref, cargo_in, given_ref, rows_ref), refs = refs[:5], refs[5:]
    dqkv_ref, dgain_ref, dlam_ref, *refs = refs
    if share:
        (part_ref, theirs_ref, cargo_out, taken_ref, back_ref), refs = refs[:5], refs[5:]
    dmix_ref, dmixt_ref, delta_ref, dqt_ref, *refs = refs
    if share:
        cargo_sem, part_sum, *refs = refs
        run, back_sems, refs = Scatter(sum_few_z, *refs[:7]), refs[7:10], refs[10:]
        back = Restore(rows_ref, back_ref, lambda n: n >= 0, natural(rows_ref.shape[1] // 2), *back_sems)
        part_cargo = Cargo([(part_ref, theirs_ref)], [], cargo_sem.at[1])
        cargo = Cargo(
            [(for_partner(cargo_in, cargo_out.shape[0]), cargo_out)], [(given_ref, taken_ref)], cargo_sem.at[0]
        )
    step = pl.program_id(0)
    blocks = pl.num_programs(0)
    width = v_ref.shape[1]
    half = width // 2
    length = q_ref.shape[0]
    scale = half ** -0.5
    lam = lam_ref[0]
    used = lam_ref[1] > 0.0

    @pl.when(step == 0)
    def _():
        if share:
            greet_all()


            def meanwhile():
                run.begin(left_ref, right_ref)
                cargo.start()
                back.start()

            collect(meanwhile, datt_ref, *refs)
        source = refs[0] if share else datt_ref
        dgain_ref[...] = jnp.zeros_like(dgain_ref)
        dlam_ref[...] = jnp.zeros_like(dlam_ref)
        dqt_ref[...] = jnp.zeros_like(dqt_ref)

        def prepare(index, carry):
            cols = pl.ds(pl.multiple_of(index * block, block), block)
            first, second = o1_ref[:, cols], o2_ref[:, cols]
            mixed = first - lam * second
            factor = lax.rsqrt(jnp.mean(mixed * mixed, axis=0, keepdims=True) + norm_eps)
            upstream = source[cols, :].astype(f32).T * (1.0 - lam_init)
            dgain_ref[...] += jnp.sum(upstream * mixed * factor, axis=1, keepdims=True)
            scaled = upstream * gain_ref[...]
            dmixed = factor * scaled - mixed * (factor * factor * factor) * jnp.mean(
                scaled * mixed, axis=0, keepdims=True
            )
            low = dmixed.astype(bf16)
            back = low.astype(f32)
            dmixt_ref[:, cols] = low
            dmix_ref[cols, :] = back.T.astype(bf16)
            along_second = jnp.sum(back * second, axis=0, keepdims=True)
            delta_ref[0:1, cols] = jnp.sum(back * first, axis=0, keepdims=True)
            delta_ref[1:2, cols] = -lam * along_second
            dlam_ref[...] -= jnp.sum(along_second, axis=1, keepdims=True)
            return carry

        lax.fori_loop(0, length // block, prepare, 0)

    if share:
        for i in range(3):

            @pl.when(step == i + 1)
            def _(i=i):
                run.halve_all(i, part_sum)
                if i == 0:
                    back.middle()
                if i == 2:
                    part_ref[...] = part_sum[...].astype(bf16)
                    part_cargo.start()

    own = pl.ds(pl.multiple_of(step * block, block), block)
    key_ids = lax.broadcasted_iota(jnp.int32, (block, block), 0)
    query_ids = lax.broadcasted_iota(jnp.int32, (block, block), 1)
    keys = k_ref[own, :]
    keys_t = kt_ref[:, own]
    values = v_ref[own, :]

    def visit(index, state, diagonal):
        dkeys, dvalues = state
        cols = pl.ds(pl.multiple_of(index * block, block), block)
        queries = q_ref[cols, :]
        dmix = dmix_ref[cols, :]
        dprob = dot(values, dmixt_ref[:, cols])
        new_keys = []
        blend = None
        for part in range(2):
            lo, hi = part * half, (part + 1) * half
            scores = dot(keys[:, lo:hi], queries[:, lo:hi], 1, 1) * (scale * log2e)
            weights = jnp.exp2(scores - lse_ref[pl.ds(part, 1), cols])
            if diagonal:
                weights = jnp.where(key_ids <= query_ids, weights, 0.0)
            delta = delta_ref[part : part + 1, cols]
            if part == 0:
                blend = weights
                dscore = (weights * (dprob - delta)).astype(bf16)
            else:
                blend = blend - lam * weights
                dscore = (weights * (-lam * dprob - delta)).astype(bf16)
            new_keys.append(dkeys[part] + dot(dscore, queries[:, lo:hi]))
            dqt_ref[lo:hi, cols] += dot(keys_t[lo:hi], dscore)
        dvalues = dvalues + dot(blend.astype(bf16), dmix)
        return tuple(new_keys), dvalues

    start = (
        (jnp.zeros((block, half), f32), jnp.zeros((block, half), f32)),
        jnp.zeros((block, width), f32),
    )
    state = visit(step, start, True)
    dkeys, dvalues = lax.fori_loop(
        step + 1, blocks, lambda index, now: visit(index, now, False), state
    )
    both = jnp.where(used, jnp.concatenate(dkeys, axis=1).T * scale, 0.0)
    dqkv_ref[own, width : 2 * width] = (
        rotated(both, cos_ref[:, own], sin_ref[:, own], True).T.astype(bf16)
    )
    dqkv_ref[own, 2 * width : 3 * width] = jnp.where(used, dvalues, 0.0).astype(bf16)

    dqkv_ref[own, 0:width] = (
        rotated(jnp.where(used, dqt_ref[:, own] * scale, 0.0), cos_ref[:, own], sin_ref[:, own], True).T.astype(bf16)
    )
    if share:

        @pl.when(step == blocks - 1)
        def _():
            run.finish()
            cargo.finish()
            part_cargo.finish()
            back.finish()


def collect(meanwhile, grad_ref, out_ref, send_sem, recv_sem, local_sem):
    me = place()[0]
    rows = grad_ref.shape[0]
    width = out_ref.shape[1]
    heads = grad_ref.shape[1] // width
    active = is_active(me, heads)

    def move(head, number):
        src = grad_ref.at[:, pl.ds(pl.multiple_of(head * width, width), width)]
        dst = out_ref.at[pl.ds(pl.multiple_of(number * rows, rows), rows)]
        return src, dst

    def send(head, number):
        src, dst = move(head, number)
        return remote(src, dst, send_sem.at[head], recv_sem.at[number], owner_of(head, heads))

    def keep():
        src, dst = move(head_of(me, heads), me)
        return pltpu.make_async_copy(src, dst, local_sem.at[0])

    def begin(head, carry):
        pl.when(owner_of(head, heads) != me)(lambda: send(head, me).start())
        return carry

    def taken(number, carry):
        pl.when(active & (number != me))(lambda: send(0, number).wait_recv())
        return carry

    def sent(head, carry):
        pl.when(owner_of(head, heads) != me)(lambda: send(head, me).wait_send())
        return carry

    lax.fori_loop(0, heads, begin, 0)
    pl.when(active)(lambda: keep().start())
    meanwhile()
    lax.fori_loop(0, group, taken, 0)
    pl.when(active)(lambda: keep().wait())
    lax.fori_loop(0, heads, sent, 0)


def backward_attention(lam, q, k, v, kt, o1, o2, lse, datt, cosine, sine, gain, block, extra=None, collective_id=None):
    length, width = q.shape
    full = lambda shape: pl.BlockSpec(shape, lambda i: (0,) * len(shape))
    arrays = (q, k, v, kt, o1, o2, lse, datt, cosine, sine, gain)
    outs = [((length, 3 * width), bf16), ((width, 1), f32), ((1, 1), f32)]
    share = collective_id is not None
    more, more_out, more_in, more_specs, out_specs = [], [], [], [], []
    if share:
        rows, wide = datt.shape
        grads, part = extra[2], (extra[0].shape[0] // group, wide)
        more_in, more_specs = list(extra), [full(a.shape) for a in extra[:2]] + [ANY] * 3
        more_out = [
            jax.ShapeDtypeStruct(part, bf16), jax.ShapeDtypeStruct(part, bf16),
            jax.ShapeDtypeStruct((grads.shape[0] // 2, grads.shape[1]), bf16),
            jax.ShapeDtypeStruct((rows, wide), bf16),
            jax.ShapeDtypeStruct((2, part[0], extra[4].shape[1] // 2 * group), bf16),
        ]
        out_specs = [full(part), ANY, ANY, ANY, ANY]
        more = [DMA((2, 2, 2)), pltpu.VMEM(part, f32)] + Scatter.scratch(*part) + Restore.scratch(2) + [
            pltpu.VMEM((length, width), bf16), DMA((wide // width,)), DMA((group,)), DMA((1,)),
        ]
    return pl.pallas_call(
        functools.partial(backward_kernel, block, share),
        grid=(length // block,),
        in_specs=[SMEM] + [full(a.shape) for a in arrays] + more_specs,
        out_specs=[full(shape) for shape, _ in outs] + out_specs,
        out_shape=[jax.ShapeDtypeStruct(shape, kind) for shape, kind in outs] + more_out,
        scratch_shapes=[
            pltpu.VMEM((length, width), bf16),
            pltpu.VMEM((width, length), bf16),
            pltpu.VMEM((8, length), f32),
            pltpu.VMEM((width, length), f32),
        ] + more,
        compiler_params=pltpu.CompilerParams(
            dimension_semantics=("arbitrary",), vmem_limit_bytes=56 * 2**20,
            collective_id=collective_id, has_side_effects=share,
        ),
        cost_estimate=busy,
        name="attention_backward",
    )(lam, *arrays, *more_in)


def rms_parts(value):
    return lax.rsqrt(jnp.mean(value * value, axis=-1, keepdims=True) + norm_eps)


def rms_back(value, factor, gain, upstream):
    scaled = upstream * gain
    mean = jnp.mean(scaled * value, axis=-1, keepdims=True)
    grad = factor * scaled - value * (factor * factor * factor) * mean
    return grad, jnp.sum(upstream * value * factor, axis=0)


def cube_body(
    block_input, positions, needle, cotangent, norm_gain1, w_query, w_key, w_value,
    lam_q1, lam_k1, lam_q2, lam_k2, sub_gain, w_out, norm_gain2, w_gate, w_up, w_down,
):
    rows, width = block_input.shape[1:]
    heads, half = lam_q1.shape
    head_width = sub_gain.shape[0]
    hidden = w_gate.shape[1]
    depth = w_query.shape[0]
    length = rows * group
    columns = hidden // group
    me, cube = place()
    my_head = head_of(me, heads)
    used = is_active(me, heads)
    active = used.astype(f32)
    here = jnp.broadcast_to(positions[0], (1, 8, rows))
    tokens_low, normed_all, places, w_head, w_d = first_exchange(
        block_input[0], here, norm_gain1[None], (w_query, w_key, w_value, w_down),
        heads, head_width, columns, 0,
    )
    tokens = tokens_low.astype(f32)
    factor1 = rms_parts(tokens)
    upstream = cotangent[0].astype(f32) * needle[0].astype(f32)[:, None]
    upstream_low = upstream.astype(bf16)
    places = places[:, 0].reshape(length)

    inv_freq = jnp.exp(-math.log(10000.0) * jnp.arange(half // 2, dtype=f32) / (half // 2))
    angles = inv_freq[:, None] * places.astype(f32)[None, :]
    cosine, sine = jnp.cos(angles), jnp.sin(angles)
    lam_vals, lam_pull = jax.vjp(lambdas, lam_q1, lam_k1, lam_q2, lam_k2)
    lam_mine = jnp.stack([lax.dynamic_index_in_dim(lam_vals, my_head, 0, False), active])
    gain_col = sub_gain[:, None]
    block = 4 * rows

    qkv = dot(w_head, normed_all, 0, 1)
    q, k, v, kt, o1, o2, lse, attended, w_gates, w_o = forward_attention(
        lam_mine, qkv, cosine, sine, gain_col, block,
        (w_gate, w_up, w_out), rows, heads, columns, 1,
    )
    resid = tokens + dot(attended, w_o)
    factor2 = rms_parts(resid)
    normed_two = (resid * factor2 * norm_gain2).astype(bf16)
    grad_low, two_all, grad_all = second_exchange(normed_two, upstream_low, 2)

    both = dot(two_all, w_gates)
    gate, upper = both[:, :columns], both[:, columns:]
    grad_inner = dot(grad_all, w_d)
    sigma = jax.nn.sigmoid(gate)
    silu = gate * sigma
    inner = (silu * upper).astype(bf16)
    gate_low = (grad_inner * upper * sigma * (1.0 + gate * (1.0 - sigma))).astype(bf16)
    upper_low = (grad_inner * silu).astype(bf16)
    gates_low = jnp.concatenate([gate_low, upper_low], axis=1)
    gate_grads = dot(two_all, gates_low, 0, 0).astype(bf16)
    down_grads = dot(grad_all, inner, 0, 0).astype(bf16)
    grad_two, ffn_out, gate_theirs = scatter(gates_low, w_gates, inner, w_d, gate_grads, 3)
    output_low = (resid + ffn_out).astype(bf16)

    grad_resid_two, gain_two = rms_back(resid, factor2, norm_gain2, grad_two)
    grad_resid = grad_low.astype(f32) + grad_resid_two
    resid_low = grad_resid.astype(bf16)
    grad_att = dot(resid_low, w_o, 1, 1).astype(bf16)

    def combine(mine, theirs):
        part = theirs.shape[0]
        mine = lax.dynamic_slice_in_dim(mine, cube * part, part, 0)
        return (mine.astype(f32) + theirs.astype(f32)).astype(bf16)

    dqkv, dgain, dlam, out_part, out_theirs, down_theirs, output_back, gate_back = backward_attention(
        lam_mine, q, k, v, kt, o1, o2, lse, grad_att, cosine, sine, gain_col, block,
        (attended.T, resid_low.T, down_grads, output_low, combine(gate_grads, gate_theirs)), 4,
    )
    head_grads = dot(normed_all, dqkv, 0, 0).astype(bf16)

    hot = jax.nn.one_hot(my_head, heads, dtype=f32)
    lines = width // head_width
    small = jnp.concatenate([
        jnp.zeros((lines, head_width), f32), gain_two.reshape(lines, head_width),
        jnp.where(used, dgain[:, 0], 0.0)[None],
        jnp.pad(jnp.where(used, hot * dlam[0, 0], 0.0), (0, head_width - heads))[None],
    ])
    small = jnp.pad(small, ((0, -small.shape[0] % 8), (0, 0)))
    out_sum = (out_part.astype(f32) + out_theirs.astype(f32)).astype(bf16)
    down_back, head_back, out_pair, small, input_back = last_exchange(
        (
            dqkv, w_head, tokens_low, norm_gain1[None], grad_resid, head_grads, small,
            combine(down_grads, down_theirs), out_sum,
        ),
        heads, head_width, columns, 5,
    )
    output = output_back[None]
    input_grad = input_back.astype(f32)[None]
    out_grads = jnp.where(me // 8 == cube, out_sum, out_pair).astype(f32)
    grads = [a.astype(f32) for a in (gate_back[0], gate_back[1], down_back[0])]
    grads += [head_back[i].astype(f32) for i in range(3)]
    gain_one = small[:lines].reshape(-1)
    gain_two = small[lines : 2 * lines].reshape(-1)
    sub_grad = small[2 * lines]
    lam_grads = lam_pull(small[2 * lines + 1, :heads])
    squares = sum(jnp.sum(g * g) for g in lam_grads)
    return (
        output, input_grad, gain_one, grads[3], grads[4], grads[5],
        lam_grads[0], lam_grads[1], lam_grads[2], lam_grads[3], sub_grad, out_grads, gain_two,
        grads[0], grads[1], grads[2], jnp.mean(lam_vals), jnp.sqrt(squares),
    )


def gather_rows(value):
    return lax.all_gather(value, "seq", axis=0, tiled=True)


def scatter_sum(value):
    return lax.psum_scatter(value, "seq", scatter_dimension=0, tiled=True)


def exchange(value):
    return lax.all_to_all(value, "seq", split_axis=0, concat_axis=0, tiled=True)


def plain_body(
    devices, block_input, positions, needle, cotangent, norm_gain1, w_query, w_key, w_value,
    lam_q1, lam_k1, lam_q2, lam_k2, sub_gain, w_out, norm_gain2, w_gate, w_up, w_down,
):
    rows, width = block_input.shape[1:]
    heads, half = lam_q1.shape
    head_width = sub_gain.shape[0]
    hidden = w_gate.shape[1]
    depth = w_query.shape[0]
    length = rows * devices
    columns = hidden // devices
    head_of = [d * heads // devices for d in range(devices)]
    owner_of = [max(d for d in range(devices) if head_of[d] == h) for h in range(heads)]
    me = lax.axis_index("seq")
    my_head = me * heads // devices
    active = ((me + 1) * heads // devices > my_head).astype(f32)

    tokens = block_input[0].astype(f32)
    factor1 = rms_parts(tokens)
    normed = (tokens * factor1 * norm_gain1).astype(bf16)
    normed_all = gather_rows(normed)
    places = gather_rows(positions[0])

    by_head = jnp.stack([w.reshape(depth, heads, head_width) for w in (w_query, w_key, w_value)], 2)
    by_head = by_head.reshape(depth, heads, 3 * head_width).transpose(1, 0, 2)
    w_head = exchange(by_head[jnp.array(head_of)]).reshape(width, 3 * head_width)

    w_o = gather_rows(w_out)
    grad_out = cotangent[0].astype(f32) * needle[0].astype(f32)[:, None]
    grad_low = grad_out.astype(bf16)
    grad_all = gather_rows(grad_low)

    ffn = jnp.stack([w.reshape(depth, devices, columns) for w in (w_gate, w_up, w_down)], 2)
    ffn = ffn.reshape(depth, devices, 3 * columns).transpose(1, 0, 2)
    w_ffn = exchange(ffn).reshape(width, 3 * columns)

    inv_freq = jnp.exp(-math.log(10000.0) * jnp.arange(half // 2, dtype=f32) / (half // 2))
    angles = inv_freq[:, None] * places.astype(f32)[None, :]
    cosine, sine = jnp.cos(angles), jnp.sin(angles)
    lam_vals, lam_pull = jax.vjp(lambdas, lam_q1, lam_k1, lam_q2, lam_k2)
    lam_mine = jnp.stack([lax.dynamic_index_in_dim(lam_vals, my_head, 0, False), active])
    gain_col = sub_gain[:, None]
    block = math.gcd(length, 512)

    qkv = dot(w_head, normed_all, 0, 1)
    q, k, v, kt, o1, o2, lse, att = forward_attention(
        lam_mine, qkv, cosine, sine, gain_col, block
    )
    att_rows = exchange(att.reshape(devices, rows, head_width))
    attended = jnp.concatenate([att_rows[d] for d in owner_of], axis=1)
    resid = tokens + dot(attended, w_o)
    factor2 = rms_parts(resid)
    normed_two = (resid * factor2 * norm_gain2).astype(bf16)
    two_all = gather_rows(normed_two)

    both = dot(two_all, w_ffn[:, : 2 * columns])
    gate, upper = both[:, :columns], both[:, columns:]
    grad_inner = dot(grad_all, w_ffn[:, 2 * columns :])
    sigma = jax.nn.sigmoid(gate)
    silu = gate * sigma
    inner = (silu * upper).astype(bf16)
    gate_low = (grad_inner * upper * sigma * (1.0 + gate * (1.0 - sigma))).astype(bf16)
    upper_low = (grad_inner * silu).astype(bf16)
    gates_low = jnp.concatenate([gate_low, upper_low], axis=1)
    grad_two = scatter_sum(dot(gates_low, w_ffn[:, : 2 * columns], 1, 1).astype(bf16)).astype(f32)
    ffn_out = scatter_sum(dot(inner, w_ffn[:, 2 * columns :], 1, 1).astype(bf16)).astype(f32)
    output = (resid + ffn_out).astype(bf16)[None]

    grad_resid_two, gain_two = rms_back(resid, factor2, norm_gain2, grad_two)
    grad_resid = grad_out + grad_resid_two
    resid_low = grad_resid.astype(bf16)
    grad_att = dot(resid_low, w_o, 1, 1).astype(bf16)
    pieces = jnp.stack(
        [grad_att[:, h * head_width : (h + 1) * head_width] for h in head_of], axis=0
    )
    datt = exchange(pieces).reshape(length, head_width)

    dqkv, dgain, dlam = backward_attention(
        lam_mine, q, k, v, kt, o1, o2, lse, datt, cosine, sine, gain_col, block
    )
    partial = (dot(dqkv, w_head, 1, 1) * active).astype(bf16)
    grad_normed = scatter_sum(partial).astype(f32)
    grad_tokens, gain_one = rms_back(tokens, factor1, norm_gain1, grad_normed)
    input_grad = (grad_resid + grad_tokens)[None]

    def settle(value):
        other = lax.ppermute(value, "batch", [(0, 1), (1, 0)])
        return value.astype(f32) + other.astype(f32)

    ffn_grads = jnp.concatenate(
        [dot(two_all, gates_low, 0, 0), dot(grad_all, inner, 0, 0)], axis=1
    ).astype(bf16)
    ffn_grads = settle(exchange(ffn_grads.reshape(devices, depth, 3 * columns)))
    ffn_grads = ffn_grads.reshape(devices, depth, 3, columns).transpose(2, 1, 0, 3)
    ffn_grads = ffn_grads.reshape(3, depth, hidden)

    head_grads = dot(normed_all, dqkv, 0, 0).astype(bf16)
    head_grads = settle(exchange(head_grads.reshape(devices, depth, 3 * head_width)))
    head_grads = jnp.stack([head_grads[d] for d in owner_of], axis=1)
    head_grads = head_grads.reshape(depth, heads, 3, head_width).transpose(2, 0, 1, 3)
    head_grads = head_grads.reshape(3, depth, width)

    out_grads = dot(attended, resid_low, 0, 0).astype(bf16)
    out_grads = settle(scatter_sum(out_grads))

    hot = jax.nn.one_hot(my_head, heads, dtype=f32) * active
    small = lax.psum(
        (gain_one, gain_two, dgain[:, 0] * active, hot * dlam[0, 0]), ("batch", "seq")
    )
    lam_grads = lam_pull(small[3])
    squares = sum(jnp.sum(g * g) for g in lam_grads)
    return (
        output, input_grad, small[0], head_grads[0], head_grads[1], head_grads[2],
        lam_grads[0], lam_grads[1], lam_grads[2], lam_grads[3], small[2], out_grads, small[1],
        ffn_grads[0], ffn_grads[1], ffn_grads[2], jnp.mean(lam_vals), jnp.sqrt(squares),
    )


def solution(mesh):
    rows = P("seq", None)
    in_specs = (
        P("batch", "seq", None), P("batch", "seq"), P("batch", "seq"), P("batch", "seq", None),
        P(), rows, rows, rows, P(), P(), P(), P(), P(), rows, P(), rows, rows, rows,
    )
    out_specs = (
        P("batch", "seq", None), P("batch", "seq", None), P(), rows, rows, rows,
        P(), P(), P(), P(), P(), rows, P(), rows, rows, rows, P(), P(),
    )
    if mesh.shape["seq"] == group and mesh.shape["batch"] == 2:
        body = cube_body
    else:
        body = functools.partial(plain_body, mesh.shape["seq"])
    return jax.shard_map(body, mesh=mesh, in_specs=in_specs, out_specs=out_specs, check_vma=False)
```

```python
import functools
import math

import jax
import jax.numpy as jnp
from jax import lax
from jax.experimental import pallas as pl
from jax.experimental.pallas import tpu as pltpu
from jax.sharding import PartitionSpec as P

lam_init = 0.619
norm_eps = 1e-05
log2e = math.log2(math.e)
neg_large = -1e30
f32 = jnp.float32
bf16 = jnp.bfloat16


def lambdas(lam_q1, lam_k1, lam_q2, lam_k2):
    return (
        jnp.exp(jnp.sum(lam_q1 * lam_k1, axis=-1))
        - jnp.exp(jnp.sum(lam_q2 * lam_k2, axis=-1))
        + lam_init
    )


def dims(left_axis, right_axis):
    return (((left_axis,), (right_axis,)), ((), ()))


def dot(left, right, left_axis=1, right_axis=0):
    return lax.dot_general(left, right, dims(left_axis, right_axis), preferred_element_type=f32)


MESH = pl.DeviceIdType.MESH
ANY = pl.BlockSpec(memory_space=pltpu.HBM)
VMEM = pl.BlockSpec(memory_space=pltpu.VMEM)
SMEM = pl.BlockSpec(memory_space=pltpu.SMEM)
DMA = pltpu.SemaphoreType.DMA
group = 16
busy = pl.CostEstimate(flops=4 * 10**10, bytes_accessed=10**7, transcendentals=0)
sides = (8, 4, 2)
even = ((8, 4, 2), (4, 2, 8), (2, 8, 4))
few_z = ((4, 8, 2), (4, 2, 8))
mid_z = ((4, 8, 2), (4, 2, 8), (2, 4, 8), (8, 4, 2))
sum_even = ((2, 8, 4), (8, 2, 4), (4, 2, 8))
sum_few_z = ((2, 8, 4), (8, 2, 4))


def place():
    seq = lax.axis_index("seq")
    return lax.axis_index("batch") * 8 + seq % 8, seq // 8


def device(number, cube=None):
    return {"batch": number // 8, "seq": (place()[1] if cube is None else cube) * 8 + number % 8}


def partner():
    return {"batch": lax.axis_index("batch"), "seq": lax.axis_index("seq") ^ 8}


def swapped():
    batch, seq = lax.axis_index("batch"), lax.axis_index("seq")
    return {"batch": 1 - batch, "seq": seq ^ 8}, batch != seq // 8


def anyone(index):
    return index // group * 8 + index % 8, index % group // 8


def everywhere():
    return lax.axis_index("batch") * group + lax.axis_index("seq")


def remote(src, dst, send_sem, recv_sem, number):
    return pltpu.make_async_remote_copy(
        src_ref=src, dst_ref=dst, send_sem=send_sem, recv_sem=recv_sem,
        device_id=device(number), device_id_type=MESH,
    )


def greet(cross=False, swap=False):
    me = place()[0]
    barrier = pltpu.get_barrier_semaphore()
    count = 1 + len(sides)
    for mask in (1,) + sides:
        pl.semaphore_signal(barrier, inc=1, device_id=device(me ^ mask), device_id_type=MESH)
    if cross:
        pl.semaphore_signal(barrier, inc=1, device_id=partner(), device_id_type=MESH)
        count = count + 1
    if swap:
        target, moved = swapped()

        @pl.when(moved)
        def _():
            pl.semaphore_signal(barrier, inc=1, device_id=target, device_id_type=MESH)

        count = count + moved.astype(jnp.int32)
    pl.semaphore_wait(barrier, count)


def greet_all():
    barrier = pltpu.get_barrier_semaphore()
    me = everywhere()

    def tell(mask, carry):
        target = device(*anyone(me ^ mask))
        pl.semaphore_signal(barrier, inc=1, device_id=target, device_id_type=MESH)
        return carry

    lax.fori_loop(1, 2 * group, tell, 0)
    pl.semaphore_wait(barrier, 2 * group - 1)


class Cargo:
    def __init__(self, cross, swap, sems):
        self.cross, self.swap, self.sems = cross, swap, sems

    def copies(self):
        for i, (src, dst) in enumerate(self.cross):
            yield None, pltpu.make_async_remote_copy(
                src_ref=src, dst_ref=dst, send_sem=self.sems.at[0, i], recv_sem=self.sems.at[1, i],
                device_id=partner(), device_id_type=MESH,
            ), None
        target, moved = swapped()
        for i, (src, dst) in enumerate(self.swap):
            j = len(self.cross) + i
            yield moved, pltpu.make_async_remote_copy(
                src_ref=src, dst_ref=dst, send_sem=self.sems.at[0, j], recv_sem=self.sems.at[1, j],
                device_id=target, device_id_type=MESH,
            ), pltpu.make_async_copy(src, dst, self.sems.at[0, j])

    def start(self):
        for moved, far, near in self.copies():
            if moved is None:
                far.start()
            else:
                pl.when(moved)(lambda: far.start())
                pl.when(jnp.logical_not(moved))(lambda: near.start())

    def finish(self):
        for moved, far, near in self.copies():
            if moved is None:
                far.wait()
            else:
                pl.when(moved)(lambda: far.wait())
                pl.when(jnp.logical_not(moved))(lambda: near.wait())


class Gather:
    def __init__(self, orders, items, send_sem, recv_sem, local_sem):
        self.orders = orders
        self.items = [item if len(item) == 4 else item + (len(orders),) for item in items]
        self.send_sem, self.recv_sem, self.local_sem = send_sem, recv_sem, local_sem
        self.me = place()[0]

    def order(self, part):
        return list(self.orders[part])

    def view(self, item, part, number):
        src, out, row, parts = self.items[item]
        rows, width = src.shape[0], src.shape[-1] // parts
        at = pl.ds(row(number), rows)
        if parts == 1:
            return out.at[at]
        return out.at[at, pl.ds(part * width, width)]

    def copy(self, item, part, number, lane, target, own=False):
        src, out, row, parts = self.items[item]
        width = src.shape[-1] // parts
        here = self.view(item, part, number)
        source = (src if parts == 1 else src.at[:, pl.ds(part * width, width)]) if own else here
        arrival = self.recv_sem.at[item, 0, group] if lane == 3 else self.recv_sem.at[item, part, number]
        return remote(source, here, self.send_sem.at[item], arrival, target)

    def every(self):
        return [(i, p) for i in range(len(self.items)) for p in range(self.items[i][3])]

    def local(self, item):
        src, out, row, _ = self.items[item]
        return pltpu.make_async_copy(src, out.at[pl.ds(row(self.me), src.shape[0])], self.local_sem.at[item])

    def start(self, items=None):
        chosen = [(i, p) for i, p in self.every() if items is None or i in items]
        for k in range(3):
            for i, p in chosen:
                self.copy(i, p, self.me, k, self.me ^ self.order(p)[k], True).start()
        for i, p in chosen:
            self.copy(i, p, self.me, 3, self.me ^ 1, True).start()
        for i in range(len(self.items)):
            if items is None or i in items:
                self.local(i).start()

    def arrivals(self, part, step):
        order = self.order(part)
        masks = [0]
        for side in order[:step]:
            masks = masks + [m ^ side for m in masks]
        return [m ^ order[step] for m in masks]

    def step(self, step, items=None):
        for i, p in self.every():
            if items is not None and i not in items:
                continue
            for mask in self.arrivals(p, step):
                number = self.me ^ mask
                self.copy(i, p, number, 0, self.me).wait_recv()
                for k in range(step + 1, 3):
                    self.copy(i, p, number, k, self.me ^ self.order(p)[k]).start()
                self.copy(i, p, number, 3, self.me ^ 1).start()

    def finish(self, items=None):
        for i in range(len(self.items)):
            if items is None or i in items:
                src, out = self.items[i][:2]
                for blocks, sem in ((8, self.recv_sem.at[i, 0, group]), (15, self.send_sem.at[i])):
                    some = out.at[pl.ds(0, blocks * src.shape[0])]
                    pltpu.make_async_copy(some, some, sem).wait()
                self.local(i).wait()

    @staticmethod
    def scratch(count):
        return [DMA((count,)), DMA((count, 4, group + 1)), DMA((count,))]


def natural(rows):
    return lambda number: pl.multiple_of(number * rows, rows)


def second_kernel(normed, given, grads, normed_all, grads_all, cargo_sem, *sems):
    greet(swap=True)
    cargo = Cargo([], [(given, grads)], cargo_sem)
    cargo.start()
    row = natural(normed.shape[0])
    run = Gather(even, [(normed, normed_all, row), (grads, grads_all, row)], *sems[:3])
    run.start([0])
    run.step(0, [0])
    run.step(1, [0])
    cargo.finish()
    run.start([1])
    run.step(2, [0])
    for step in range(3):
        run.step(step, [1])
    run.finish()


def second_exchange(normed, given, collective_id):
    rows, width = normed.shape
    outs = [(rows, width), (group * rows, width), (group * rows, width)]
    return pl.pallas_call(
        second_kernel,
        in_specs=[ANY] * 2,
        out_specs=[ANY] * 3,
        out_shape=[jax.ShapeDtypeStruct(shape, bf16) for shape in outs],
        scratch_shapes=[DMA((2, 1))] + Gather.scratch(2),
        compiler_params=pltpu.CompilerParams(collective_id=collective_id, has_side_effects=True),
        cost_estimate=busy,
        name="second_exchange",
    )(normed, given)


class Scatter:
    def __init__(self, orders, own, core_in, side_in, core_s, core_r, side_s, side_r):
        self.orders, self.parts = orders, len(orders)
        self.own, self.core_in, self.side_in = own, core_in, side_in
        self.core_s, self.core_r, self.side_s, self.side_r = core_s, core_r, side_s, side_r
        self.me = place()[0]
        self.core = self.me % 2
        self.rows, self.width = own.shape[2], own.shape[3]
        self.part = self.width // self.parts

    def cols(self, part):
        return pl.ds(part * self.part, self.part)

    def order(self, part):
        return list(self.orders[part])

    def core_copy(self, part):
        c = self.cols(part)
        return remote(
            self.own.at[1 - self.core, :, :, c], self.core_in.at[:, :, c],
            self.core_s.at[part], self.core_r.at[part], self.me ^ 1,
        )

    def moves(self, part, step):
        order = self.order(part)
        masks = [0]
        for side in order[:step:-1]:
            masks = masks + [m ^ side for m in masks]
        base = {0: 0, 1: 4, 2: 6}[step]
        masks = sorted(masks, key=lambda m: [not m & side for side in order[step + 1 :]])
        return [(m ^ order[step], base + j) for j, m in enumerate(masks)]

    def side_copy(self, part, step, mask, slot):
        c = self.cols(part)
        peer = self.me ^ self.order(part)[step]
        return remote(
            self.own.at[self.core, (self.me ^ mask) // 2, :, c], self.side_in.at[slot, :, c],
            self.side_s.at[part, slot], self.side_r.at[part, slot], peer,
        )

    def multiply(self, part, lhs, rhs, axis=1):
        c = self.cols(part)
        chunk = 4 * self.rows

        def quarter(q, carry):
            at = pl.ds(pl.multiple_of(q * chunk, chunk), chunk)
            if axis:
                p = dot(lhs[at, :], rhs[part * self.part : (part + 1) * self.part, :], 1, 1)
            else:
                p = dot(lhs[:, at], rhs[:, part * self.part : (part + 1) * self.part], 0, 0)
            p = p.astype(bf16).reshape(4, self.rows, self.part)
            for j in range(4):
                self.own[j % 2, 2 * q + j // 2, :, c] = p[j]
            return carry

        lax.fori_loop(0, 4, quarter, 0)
        self.core_copy(part).start()

    def add(self, number, part, extra):
        c = self.cols(part)
        at = (self.core, number // 2, slice(None), c)
        self.own[at] = (self.own[at].astype(f32) + extra.astype(f32)).astype(bf16)

    def merge(self, part):
        c = self.cols(part)
        self.core_copy(part).wait()
        moves = self.moves(part, 0)
        for mask, slot in moves:
            self.add(self.me ^ mask, part, self.core_in[(self.me ^ mask) // 2, :, c])
            self.side_copy(part, 0, mask, slot).start()
        for mask, _ in moves:
            number = self.me ^ mask ^ self.order(part)[0]
            self.add(number, part, self.core_in[number // 2, :, c])

    def begin(self, lhs, rhs, axis=1):
        self.multiply(0, lhs, rhs, axis)
        for part in range(1, self.parts):
            self.multiply(part, lhs, rhs, axis)
            self.merge(part - 1)
        self.merge(self.parts - 1)

    def halve(self, part, step, out=None):
        c = self.cols(part)
        leaving = dict(self.moves(part, step + 1)) if step < 2 else {}
        for mask, slot in self.moves(part, step):
            kept = mask ^ self.order(part)[step]
            self.side_copy(part, step, mask, slot).wait_recv()
            if out is not None:
                at = (self.core, self.me // 2, slice(None), c)
                out[:, c] = self.own[at].astype(f32) + self.side_in[slot, :, c].astype(f32)
                continue
            self.add(self.me ^ kept, part, self.side_in[slot, :, c])
            if kept in leaving:
                self.side_copy(part, step + 1, kept, leaving[kept]).start()

    def halve_all(self, step, out):
        for part in range(self.parts):
            self.halve(part, step, out if step == 2 else None)

    def finish(self):
        for part in range(self.parts):
            for step in range(3):
                for mask, slot in self.moves(part, step):
                    self.side_copy(part, step, mask, slot).wait_send()

    @staticmethod
    def scratch(rows, width):
        return [
            pltpu.VMEM((2, 8, rows, width), bf16), pltpu.VMEM((8, rows, width), bf16),
            pltpu.VMEM((7, rows, width), bf16), DMA((4,)), DMA((4,)), DMA((4, 7)), DMA((4, 7)),
        ]


def for_partner(grads, rows):
    return grads.at[pl.ds(pl.multiple_of((1 - place()[1]) * rows, rows), rows)]


def weight_grads(left, right, out):
    chunk = 512

    def some(j, carry):
        at = pl.ds(pl.multiple_of(j * chunk, chunk), chunk)
        out[at, :] = dot(left[:, at], right[...], 0, 0).astype(bf16)
        return carry

    lax.fori_loop(0, left.shape[1] // chunk, some, 0)


def scatter_kernel(
    lhs, rhs, lhs_two, rhs_two, left, left_two, out, out_two, grads, grads_two, taken,
    cargo_sem, copy_sem, held, held_two, *scratch,
):
    greet(cross=True)
    cargo = Cargo([(for_partner(grads, taken.shape[0]), taken)], [], cargo_sem)
    copies = [pltpu.make_async_copy(a, b, copy_sem.at[i]) for i, (a, b) in enumerate(((left, held), (left_two, held_two)))]
    for copy in copies:
        copy.start()
    run, more = Scatter(sum_even, *scratch[:7]), Scatter(sum_even, *scratch[7:])
    run.begin(lhs, rhs)
    more.begin(lhs_two, rhs_two)
    copies[0].wait()
    weight_grads(held, lhs, grads)
    cargo.start()
    for step in range(3):
        run.halve_all(step, out)
        more.halve_all(step, out_two)
        if step == 0:
            copies[1].wait()
            weight_grads(held_two, lhs_two, grads_two)
    run.finish()
    more.finish()
    cargo.finish()


def scatter(lhs, rhs, lhs_two, rhs_two, left, left_two, collective_id):
    rows, width = lhs.shape[0] // group, rhs.shape[0]
    return pl.pallas_call(
        scatter_kernel,
        in_specs=[VMEM] * 4 + [ANY] * 2,
        out_specs=[VMEM] * 4 + [ANY],
        out_shape=[jax.ShapeDtypeStruct((rows, width), f32)] * 2
        + [
            jax.ShapeDtypeStruct((width, lhs.shape[1]), bf16), jax.ShapeDtypeStruct((width, lhs_two.shape[1]), bf16),
            jax.ShapeDtypeStruct((width // 2, lhs.shape[1]), bf16),
        ],
        scratch_shapes=[DMA((2, 1)), DMA((2,)), pltpu.VMEM(left.shape, bf16), pltpu.VMEM(left.shape, bf16)] + Scatter.scratch(rows, width) + Scatter.scratch(rows, width),
        compiler_params=pltpu.CompilerParams(
            collective_id=collective_id, has_side_effects=True, vmem_limit_bytes=60 * 2**20
        ),
        cost_estimate=busy,
        name=f"scatter{collective_id}",
    )(lhs, rhs, lhs_two, rhs_two, left, left_two)


def head_of(number, heads):
    return number * heads // group


def is_active(number, heads):
    return (number + 1) * heads // group > number * heads // group


def owner_of(head, heads):
    return ((head + 1) * group + heads - 1) // heads - 1


class Deal:
    def __init__(self, items, send_sem, recv_sem):
        self.items, self.send_sem, self.recv_sem = items, send_sem, recv_sem
        self.me = everywhere()

    def views(self, item, source, target):
        own, out, column = self.items[item]
        rows, width = own.shape[0] // 2, out.shape[1]
        number, cube = anyone(source)
        half = pl.ds(pl.multiple_of(number // 8 * rows, rows), rows)
        row = (cube * 8 + number % 8) * (2 * rows) + number // 8 * rows
        cols = pl.ds(column(anyone(target)[0]), width)
        return own.at[half, cols], out.at[pl.ds(pl.multiple_of(row, rows), rows)]

    def copy(self, item, source, target, far):
        src, dst = self.views(item, source, target)
        return pltpu.make_async_remote_copy(
            src_ref=src, dst_ref=dst, send_sem=self.send_sem.at[item, far],
            recv_sem=self.recv_sem.at[item, far], device_id=device(*anyone(target)), device_id_type=MESH,
        )

    def local(self, item):
        src, dst = self.views(item, self.me, self.me)
        return pltpu.make_async_copy(src, dst, self.recv_sem.at[item, 0])

    def whole(self, item, sem, blocks):
        own, out, _ = self.items[item]
        some = out.at[pl.ds(0, blocks * own.shape[0] // 2)]
        pltpu.make_async_copy(some, some, sem).wait()

    def start_near(self):
        def begin(mask, carry):
            for i in range(len(self.items)):
                self.copy(i, self.me, self.me ^ (mask % 8 + mask // 8 * group), 0).start()
            return carry

        lax.fori_loop(1, group, begin, 0)
        for i in range(len(self.items)):
            self.local(i).start()

    def start_far(self):
        def begin(mask, carry):
            for i in range(len(self.items)):
                self.copy(i, self.me, self.me ^ (8 + mask % 8 + mask // 8 * group), 1).start()
            return carry

        lax.fori_loop(0, group, begin, 0)

    def finish_near(self):
        for i in range(len(self.items)):
            self.whole(i, self.recv_sem.at[i, 0], group)
            self.whole(i, self.send_sem.at[i, 0], group - 1)

    def finish_far(self):
        for i in range(len(self.items)):
            self.whole(i, self.recv_sem.at[i, 1], group)
            self.whole(i, self.send_sem.at[i, 1], group)

    @staticmethod
    def scratch(count):
        return [DMA((count, 2)), DMA((count, 2))]


def first_kernel(
    head_width, heads, columns, given, places, gain, w_q, w_k, w_v, w_down,
    tokens, tokens_all, places_all, w_head, w_d, land, places_land, normed, cargo_sem, *sems,
):
    greet_all()
    cargo = Cargo([], [(given, land), (places, places_land)], cargo_sem)
    cargo.start()
    column = lambda number: pl.multiple_of(head_of(number, heads) * head_width, head_width)
    deal = Deal(
        [
            (w, w_head.at[:, pl.ds(i * head_width, head_width)], column)
            for i, w in enumerate((w_q, w_k, w_v))
        ],
        *sems[3:5],
    )
    own = natural(columns)
    down = Deal([(w_down, w_d, own)], *sems[5:7])
    deal.start_near()
    down.start_near()
    cargo.finish()
    value = land[...].astype(f32)
    factor = lax.rsqrt(jnp.mean(value * value, axis=-1, keepdims=True) + norm_eps)
    normed[...] = (value * factor * gain[...]).astype(bf16)
    run = Gather(
        mid_z, [(normed, tokens_all, natural(normed.shape[0])), (places_land, places_all, natural(1), 1)], *sems[:3]
    )
    run.start()
    deal.start_far()
    tokens[...] = land[...]
    run.step(0)
    down.start_far()
    run.step(1)
    run.step(2)
    run.finish()
    for some in (deal, down):
        some.finish_near()
        some.finish_far()


def gate_deal(w_gate, w_up, w_gates, sems):
    columns = w_gates.shape[1] // 2
    views = [w_gates.at[:, pl.ds(i * columns, columns)] for i in range(2)]
    return Deal([(w, view, natural(columns)) for w, view in zip((w_gate, w_up), views)], *sems)


def first_exchange(given, places, gain, weights, heads, head_width, columns, collective_id):
    rows, width = given.shape
    outs = [
        ((rows, width), bf16), ((group * rows, width), bf16), ((group,) + places.shape[1:], jnp.int32),
        ((width, 3 * head_width), bf16), ((width, columns), bf16),
    ]
    return pl.pallas_call(
        functools.partial(first_kernel, head_width, heads, columns),
        in_specs=[VMEM, VMEM, VMEM] + [ANY] * 4,
        out_specs=[VMEM] + [ANY] * 4,
        out_shape=[jax.ShapeDtypeStruct(shape, kind) for shape, kind in outs],
        scratch_shapes=[
            pltpu.VMEM((rows, width), bf16), pltpu.VMEM(places.shape, jnp.int32),
            pltpu.VMEM((rows, width), bf16), DMA((2, 2)),
        ] + Gather.scratch(2) + Deal.scratch(3) + Deal.scratch(1),
        compiler_params=pltpu.CompilerParams(
            collective_id=collective_id, has_side_effects=True, vmem_limit_bytes=60 * 2**20
        ),
        cost_estimate=busy,
        name="first_exchange",
    )(given, places, gain, *weights)


class Restore:
    def __init__(self, grads, land, sources, column, send_sem, recv_sem, local_sem):
        self.grads, self.land, self.sources, self.column = grads, land, sources, column
        self.send_sem, self.recv_sem, self.local_sem = send_sem, recv_sem, local_sem
        self.me = place()[0]
        self.count, self.rows = land.shape[0], land.shape[1]
        self.width = grads.shape[1] // self.count
        self.blocks = land.shape[2] // self.width // 2

    def move(self, i, source, target):
        rows = pl.ds(pl.multiple_of(target % 8 * self.rows, self.rows), self.rows)
        src = self.grads.at[rows, pl.ds(i * self.width, self.width)]
        return src, self.land.at[i, :, pl.ds(self.column(source), self.width)]

    def send(self, i, source, target):
        src, dst = self.move(i, source, target)
        return remote(src, dst, self.send_sem.at[i, 0], self.recv_sem.at[i, source], target)

    def keep(self, i):
        src, dst = self.move(i, self.me, self.me)
        return pltpu.make_async_copy(src, dst, self.local_sem.at[i])

    def pass_on(self, i, source):
        here = self.move(i, source, self.me)[1]
        return remote(here, here, self.send_sem.at[i, 1], self.recv_sem.at[i, group], self.me ^ 8)

    def start(self):
        mine = self.sources(self.me)

        def begin(mask, carry):
            for i in range(self.count):
                pl.when(mine)(lambda: self.send(i, self.me, self.me ^ mask).start())
            return carry

        lax.fori_loop(1, 8, begin, 0)
        for i in range(self.count):
            pl.when(mine)(lambda: self.keep(i).start())

    def middle(self):
        mine = self.sources(self.me)

        def forward(mask, carry):
            other = self.me ^ mask
            for i in range(self.count):

                @pl.when(self.sources(other))
                def _():
                    self.send(i, other, self.me).wait_recv()
                    self.pass_on(i, other).start()

            return carry

        for i in range(self.count):

            @pl.when(mine)
            def _():
                self.keep(i).wait()
                self.pass_on(i, self.me).start()

        lax.fori_loop(1, 8, forward, 0)

    def finish(self):
        mine = self.sources(self.me)

        def wait(i, blocks, sem):
            some = self.land.at[i, :, pl.ds(0, blocks * self.width)]
            pltpu.make_async_copy(some, some, sem).wait()

        for i in range(self.count):
            pl.when(mine)(lambda: wait(i, 7, self.send_sem.at[i, 0]))
            wait(i, self.blocks, self.send_sem.at[i, 1])
            wait(i, self.blocks, self.recv_sem.at[i, group])

    @staticmethod
    def scratch(count):
        return [DMA((count, 2)), DMA((count, group + 1)), DMA((count,))]


def last_kernel(
    heads, head_width, columns,
    dqkv, w_head, tokens, gain, grad_resid, head, small, ffn_sum, out_sum,
    ffn_out, head_out, pair_out, total_out, input_out,
    result8, input_low, small_all, small_land, head_land, head_sum,
    cargo_sem, pair_sem, total_send, total_recv, *refs,
):
    me, cube = place()
    width = tokens.shape[1]
    greet_all()
    run = Scatter(sum_even, *refs[:7])
    sems = refs[7:]
    column = lambda n: pl.multiple_of(head_of(n, heads) * head_width, head_width)
    ffn_back = Restore(ffn_sum, ffn_out, lambda n: n >= 0, natural(columns), *sems[0:3])
    head_back = Restore(head_sum, head_out, lambda n: is_active(n, heads), column, *sems[3:6])
    half = head_land.shape[0]
    head_cargo = Cargo([(for_partner(head, half), head_land)], [], cargo_sem.at[0])
    input_cargo = Cargo([], [(input_low, input_out)], cargo_sem.at[1])
    small_cargo = Cargo([(small_all.at[me], small_land)], [], cargo_sem.at[3])
    pair = remote(out_sum, pair_out, pair_sem.at[0], pair_sem.at[1], me ^ 8)

    def send(source, target):
        return remote(
            small_all.at[me], small_all.at[source], total_send.at[target], total_recv.at[source], target
        )

    head_cargo.start()
    run.begin(dqkv, w_head)
    ffn_back.start()
    pair.start()
    run.halve_all(0, None)
    run.halve_all(1, None)
    ffn_back.middle()
    run.halve_all(2, result8)

    value = tokens[...].astype(f32)
    factor = lax.rsqrt(jnp.mean(value * value, axis=-1, keepdims=True) + norm_eps)
    upstream = result8[...]
    scaled = upstream * gain[...]
    mean = jnp.mean(scaled * value, axis=-1, keepdims=True)
    grad = factor * scaled - value * (factor * factor * factor) * mean
    input_low[...] = (grad_resid[...] + grad).astype(bf16)
    input_cargo.start()
    gain_one = jnp.sum(upstream * value * factor, axis=0, keepdims=True)
    small_all[me] = small[...]
    for i in range(width // head_width):
        small_all[me, i : i + 1, :] = gain_one[:, i * head_width : (i + 1) * head_width]
    small_cargo.start()
    head_cargo.finish()
    mine = pl.ds(pl.multiple_of(cube * half, half), half)
    head_sum[...] = (head[mine, :].astype(f32) + head_land[...].astype(f32)).astype(bf16)
    head_back.start()
    small_cargo.finish()
    small_all[me] = small_all[me] + small_land[...]

    def begin(mask, carry):
        send(me, me ^ mask).start()
        return carry

    lax.fori_loop(1, group, begin, 0)
    head_back.middle()

    def taken(mask, carry):
        send(me ^ mask, me).wait_recv()
        send(me, me ^ mask).wait_send()
        return carry

    lax.fori_loop(1, group, taken, 0)
    result = small_all[0]
    for number in range(1, group):
        result = result + small_all[number]
    total_out[...] = result
    pair.wait()
    run.finish()
    input_cargo.finish()
    ffn_back.finish()
    head_back.finish()


def last_exchange(arrays, heads, head_width, columns, collective_id):
    dqkv, w_head, tokens, gain, grad_resid, head, small, ffn_sum, out_sum = arrays
    rows, width = tokens.shape
    part = out_sum.shape[0]
    half = (head.shape[0] // 2, head.shape[1])
    outs = [
        ((1, part, columns * group), bf16), ((3, part, width), bf16), (out_sum.shape, bf16),
        (small.shape, f32), ((rows, width), bf16),
    ]
    memory = pltpu.VMEM
    return pl.pallas_call(
        functools.partial(last_kernel, heads, head_width, columns),
        in_specs=[VMEM] * 7 + [ANY] * 2,
        out_specs=[ANY, ANY, ANY, VMEM, ANY],
        out_shape=[jax.ShapeDtypeStruct(shape, kind) for shape, kind in outs],
        scratch_shapes=[
            memory((rows, width), f32), memory((rows, width), bf16),
            memory((group,) + small.shape, f32), memory(small.shape, f32), memory(half, bf16), memory(half, bf16),
            DMA((4, 2, 1)), DMA((2,)), DMA((group,)), DMA((group,)),
        ]
        + Scatter.scratch(rows, width) + Restore.scratch(1) + Restore.scratch(3),
        compiler_params=pltpu.CompilerParams(
            collective_id=collective_id, has_side_effects=True, vmem_limit_bytes=48 * 2**20
        ),
        cost_estimate=busy,
        name="last_exchange",
    )(*arrays)


def rotated(value, cosine, sine, inverse=False):
    parts = []
    step = cosine.shape[0]
    sign = -1.0 if inverse else 1.0
    for start in range(0, value.shape[0], 2 * step):
        first = value[start : start + step]
        second = value[start + step : start + 2 * step]
        parts.append(first * cosine - sign * (second * sine))
        parts.append(second * cosine + sign * (first * sine))
    return jnp.concatenate(parts, axis=0)


def forward_kernel(
    block, share, lam_ref, qkv_ref, cos_ref, sin_ref, gain_ref, *refs,
):
    step = pl.program_id(0)
    if share:
        (w_one, w_two, w_rows, normed), refs = refs[:4], refs[4:]
    q_ref, k_ref, v_ref, kt_ref, o1_ref, o2_ref, lse_ref, *refs = refs
    if share:
        out_ref, both_ref, w_all = refs[:3]
        qt_ref, vt_ref, att_ref, w_land, held, send_sem, recv_sem, local_sem, cargo_sem, *sems = refs[3:]
        copy = pltpu.make_async_copy(normed, held, local_sem.at[1])
        me, cube = place()
        deal = gate_deal(w_one, w_two, both_ref, sems[3:])
        sub = w_land.shape[0]
        w_half = w_rows.at[pl.ds(pl.multiple_of(me // 8 * sub, sub), sub)]

        def spot(which):
            return lambda number: pl.multiple_of((which * 8 + number % 8) * (2 * sub) + number // 8 * sub, sub)

        run = Gather(few_z, [(w_half, w_all, spot(cube)), (w_land, w_all, spot(1 - cube))], *sems[:3])
        rows_cargo = Cargo([(w_half, w_land)], [], cargo_sem)

        @pl.when(step == 0)
        def _():
            copy.start()
            greet_all()
            rows_cargo.start()
            run.start([0])
            deal.start_near()

        @pl.when(step == 1)
        def _():
            rows_cargo.finish()
            run.start([1])
            deal.start_far()

        @pl.when(step == 2)
        def _():
            run.step(0)

        @pl.when(step == 3)
        def _():
            run.step(1)
    else:
        att_ref, qt_ref, vt_ref = refs
    width = v_ref.shape[1]
    half = width // 2
    length = q_ref.shape[0]
    scale = half ** -0.5 * log2e

    @pl.when(step == 0)
    def _():
        def prepare(index, carry):
            cols = pl.ds(pl.multiple_of(index * block, block), block)
            cosine, sine = cos_ref[:, cols], sin_ref[:, cols]
            qkv = dot(held[cols, :], qkv_ref[...]).T if share else qkv_ref[:, cols]
            query = rotated(qkv[0:width], cosine, sine)
            key = rotated(qkv[width : 2 * width], cosine, sine)
            value = qkv[2 * width : 3 * width]
            qt_ref[:, cols] = query.astype(bf16)
            kt_ref[:, cols] = key.astype(bf16)
            vt_ref[:, cols] = value.astype(bf16)
            q_ref[cols, :] = query.T.astype(bf16)
            k_ref[cols, :] = key.T.astype(bf16)
            v_ref[cols, :] = value.T.astype(bf16)
            return carry

        if share:
            copy.wait()
        lax.fori_loop(0, length // block, prepare, 0)

    own = pl.ds(pl.multiple_of(step * block, block), block)
    queries = qt_ref[:, own]
    key_ids = lax.broadcasted_iota(jnp.int32, (block, block), 0)
    query_ids = lax.broadcasted_iota(jnp.int32, (block, block), 1)

    def visit(index, state, diagonal):
        rows = pl.ds(pl.multiple_of(index * block, block), block)
        values = vt_ref[:, rows]
        out = []
        for part in range(2):
            top, total, acc = state[part]
            lo, hi = part * half, (part + 1) * half
            scores = dot(k_ref[rows, lo:hi], queries[lo:hi]) * scale
            if diagonal:
                scores = jnp.where(key_ids <= query_ids, scores, neg_large)
            new_top = jnp.maximum(top, jnp.max(scores, axis=0, keepdims=True))
            weights = jnp.exp2(scores - new_top)
            fade = jnp.exp2(top - new_top)
            total = total * fade + jnp.sum(weights, axis=0, keepdims=True)
            acc = acc * fade + dot(values, weights.astype(bf16))
            out.append((new_top, total, acc))
        return tuple(out)

    start = tuple(
        (
            jnp.full((1, block), neg_large, f32),
            jnp.zeros((1, block), f32),
            jnp.zeros((width, block), f32),
        )
        for _ in range(2)
    )
    state = lax.fori_loop(0, step, lambda index, now: visit(index, now, False), start)
    state = visit(step, state, True)
    outs = []
    for part, ref in ((0, o1_ref), (1, o2_ref)):
        top, total, acc = state[part]
        result = acc / total
        ref[:, own] = result
        lse_ref[pl.ds(part, 1), own] = top + jnp.log2(total)
        outs.append(result)
    mixed = outs[0] - lam_ref[0] * outs[1]
    factor = lax.rsqrt(jnp.mean(mixed * mixed, axis=0, keepdims=True) + norm_eps)
    attended = mixed * factor * gain_ref[...] * (1.0 - lam_init)
    att_ref[own, :] = attended.T.astype(bf16)
    if share:
        rows, heads = out_ref.shape[0], out_ref.shape[1] // width
        active = is_active(me, heads)

        def part(number, head):
            cols = pl.ds(pl.multiple_of(head * width, width), width)
            return att_ref.at[pl.ds(pl.multiple_of(number * rows, rows), rows)], out_ref.at[:, cols]

        def send(number, head):
            src, dst = part(number, head)
            return remote(src, dst, send_sem.at[number], recv_sem.at[head], number)

        def keep():
            src, dst = part(me, head_of(me, heads))
            return pltpu.make_async_copy(src, dst, local_sem.at[0])

        for j in range(block // rows):
            number = step * (block // rows) + j
            pl.when(active & (number != me))(lambda: send(number, head_of(me, heads)).start())
            pl.when(active & (number == me))(lambda: keep().start())

        @pl.when(step == pl.num_programs(0) - 1)
        def _():
            def sent(number, carry):
                pl.when(active & (number != me))(lambda: send(number, 0).wait_send())
                return carry

            def taken(head, carry):
                pl.when(owner_of(head, heads) != me)(lambda: send(me, head).wait_recv())
                return carry

            lax.fori_loop(0, heads, taken, 0)
            lax.fori_loop(0, group, sent, 0)
            pl.when(active)(lambda: keep().wait())
            run.step(2)
            run.finish()
            deal.finish_near()
            deal.finish_far()


def forward_attention(lam, qkv, cosine, sine, gain, block, weights=(), rows=0, heads=0, columns=0, collective_id=None):
    width, length = gain.shape[0], cosine.shape[1]
    full = lambda shape: pl.BlockSpec(shape, lambda i: (0,) * len(shape))
    outs = [
        ((length, width), bf16),
        ((length, width), bf16),
        ((length, width), bf16),
        ((width, length), bf16),
        ((width, length), f32),
        ((width, length), f32),
        ((8, length), f32),
    ]
    scratch = [pltpu.VMEM((width, length), bf16), pltpu.VMEM((width, length), bf16)]
    out_specs = [full(shape) for shape, _ in outs]
    share = bool(weights)
    if share:
        wide = heads * width
        more = [((rows, wide), bf16), ((wide, 2 * columns), bf16), ((wide, wide), bf16)]
        outs, out_specs = outs + more, out_specs + [ANY] * 3
        scratch += [
            pltpu.VMEM((length, width), bf16), pltpu.VMEM((weights[2].shape[0] // 2, wide), bf16),
            pltpu.VMEM(weights[3].shape, bf16), DMA((group,)), DMA((heads,)), DMA((2,)), DMA((2, 1)),
        ]
        scratch += Gather.scratch(2) + Deal.scratch(2)
    else:
        outs, out_specs = outs + [((length, width), bf16)], out_specs + [full((length, width))]
    return pl.pallas_call(
        functools.partial(forward_kernel, block, share),
        grid=(length // block,),
        in_specs=[SMEM] + [full(a.shape) for a in (qkv, cosine, sine, gain)] + [ANY] * len(weights),
        out_specs=out_specs,
        out_shape=[jax.ShapeDtypeStruct(shape, kind) for shape, kind in outs],
        scratch_shapes=scratch,
        compiler_params=pltpu.CompilerParams(
            dimension_semantics=("arbitrary",), vmem_limit_bytes=56 * 2**20,
            collective_id=collective_id, has_side_effects=share,
        ),
        cost_estimate=busy,
        name="attention_forward",
    )(lam, qkv, cosine, sine, gain, *weights)


def backward_kernel(
    block, share, lam_ref, q_ref, k_ref, v_ref, kt_ref, o1_ref, o2_ref, lse_ref, datt_ref,
    cos_ref, sin_ref, gain_ref, *refs,
):
    if share:
        (left_ref, right_ref, cargo_in, given_ref, rows_ref, normed), refs = refs[:6], refs[6:]
    dqkv_ref, dgain_ref, dlam_ref, *refs = refs
    if share:
        (part_ref, theirs_ref, cargo_out, taken_ref, back_ref, head_ref), refs = refs[:6], refs[6:]
    dmix_ref, dmixt_ref, delta_ref, dqt_ref, *refs = refs
    if share:
        cargo_sem, held_sem, held, part_sum, *refs = refs
        copy = pltpu.make_async_copy(normed, held, held_sem.at[0])
        run, back_sems, refs = Scatter(sum_few_z, *refs[:7]), refs[7:10], refs[10:]
        back = Restore(rows_ref, back_ref, lambda n: n >= 0, natural(rows_ref.shape[1] // 2), *back_sems)
        part_cargo = Cargo([(part_ref, theirs_ref)], [], cargo_sem.at[1])
        cargo = Cargo(
            [(for_partner(cargo_in, cargo_out.shape[0]), cargo_out)], [(given_ref, taken_ref)], cargo_sem.at[0]
        )
    step = pl.program_id(0)
    blocks = pl.num_programs(0)
    width = v_ref.shape[1]
    half = width // 2
    length = q_ref.shape[0]
    scale = half ** -0.5
    lam = lam_ref[0]
    used = lam_ref[1] > 0.0

    @pl.when(step == 0)
    def _():
        if share:
            greet_all()


            def meanwhile():
                run.begin(left_ref, right_ref, 0)
                cargo.start()
                back.start()
                copy.start()

            collect(meanwhile, datt_ref, *refs)
        source = refs[0] if share else datt_ref
        dgain_ref[...] = jnp.zeros_like(dgain_ref)
        dlam_ref[...] = jnp.zeros_like(dlam_ref)
        dqt_ref[...] = jnp.zeros_like(dqt_ref)

        def prepare(index, carry):
            cols = pl.ds(pl.multiple_of(index * block, block), block)
            first, second = o1_ref[:, cols], o2_ref[:, cols]
            mixed = first - lam * second
            factor = lax.rsqrt(jnp.mean(mixed * mixed, axis=0, keepdims=True) + norm_eps)
            upstream = source[cols, :].astype(f32).T * (1.0 - lam_init)
            dgain_ref[...] += jnp.sum(upstream * mixed * factor, axis=1, keepdims=True)
            scaled = upstream * gain_ref[...]
            dmixed = factor * scaled - mixed * (factor * factor * factor) * jnp.mean(
                scaled * mixed, axis=0, keepdims=True
            )
            low = dmixed.astype(bf16)
            back = low.astype(f32)
            dmixt_ref[:, cols] = low
            dmix_ref[cols, :] = back.T.astype(bf16)
            along_second = jnp.sum(back * second, axis=0, keepdims=True)
            delta_ref[0:1, cols] = jnp.sum(back * first, axis=0, keepdims=True)
            delta_ref[1:2, cols] = -lam * along_second
            dlam_ref[...] -= jnp.sum(along_second, axis=1, keepdims=True)
            return carry

        lax.fori_loop(0, length // block, prepare, 0)

    if share:
        for i in range(3):

            @pl.when(step == i + 1)
            def _(i=i):
                run.halve_all(i, part_sum)
                if i == 0:
                    back.middle()
                if i == 2:
                    part_ref[...] = part_sum[...].astype(bf16)
                    part_cargo.start()

    own = pl.ds(pl.multiple_of(step * block, block), block)
    key_ids = lax.broadcasted_iota(jnp.int32, (block, block), 0)
    query_ids = lax.broadcasted_iota(jnp.int32, (block, block), 1)
    keys = k_ref[own, :]
    keys_t = kt_ref[:, own]
    values = v_ref[own, :]

    def visit(index, state, diagonal):
        dkeys, dvalues = state
        cols = pl.ds(pl.multiple_of(index * block, block), block)
        queries = q_ref[cols, :]
        dmix = dmix_ref[cols, :]
        dprob = dot(values, dmixt_ref[:, cols])
        new_keys = []
        blend = None
        for part in range(2):
            lo, hi = part * half, (part + 1) * half
            scores = dot(keys[:, lo:hi], queries[:, lo:hi], 1, 1) * (scale * log2e)
            weights = jnp.exp2(scores - lse_ref[pl.ds(part, 1), cols])
            if diagonal:
                weights = jnp.where(key_ids <= query_ids, weights, 0.0)
            delta = delta_ref[part : part + 1, cols]
            if part == 0:
                blend = weights
                dscore = (weights * (dprob - delta)).astype(bf16)
            else:
                blend = blend - lam * weights
                dscore = (weights * (-lam * dprob - delta)).astype(bf16)
            new_keys.append(dkeys[part] + dot(dscore, queries[:, lo:hi]))
            dqt_ref[lo:hi, cols] += dot(keys_t[lo:hi], dscore)
        dvalues = dvalues + dot(blend.astype(bf16), dmix)
        return tuple(new_keys), dvalues

    start = (
        (jnp.zeros((block, half), f32), jnp.zeros((block, half), f32)),
        jnp.zeros((block, width), f32),
    )
    state = visit(step, start, True)
    dkeys, dvalues = lax.fori_loop(
        step + 1, blocks, lambda index, now: visit(index, now, False), state
    )
    both = jnp.where(used, jnp.concatenate(dkeys, axis=1).T * scale, 0.0)
    dqkv_ref[own, width : 2 * width] = (
        rotated(both, cos_ref[:, own], sin_ref[:, own], True).T.astype(bf16)
    )
    dqkv_ref[own, 2 * width : 3 * width] = jnp.where(used, dvalues, 0.0).astype(bf16)

    dqkv_ref[own, 0:width] = (
        rotated(jnp.where(used, dqt_ref[:, own] * scale, 0.0), cos_ref[:, own], sin_ref[:, own], True).T.astype(bf16)
    )
    if share:

        @pl.when(step == blocks - 1)
        def _():
            copy.wait()
            weight_grads(held, dqkv_ref, head_ref)
            run.finish()
            cargo.finish()
            part_cargo.finish()
            back.finish()


def collect(meanwhile, grad_ref, out_ref, send_sem, recv_sem, local_sem):
    me = place()[0]
    rows = grad_ref.shape[0]
    width = out_ref.shape[1]
    heads = grad_ref.shape[1] // width
    active = is_active(me, heads)

    def move(head, number):
        src = grad_ref.at[:, pl.ds(pl.multiple_of(head * width, width), width)]
        dst = out_ref.at[pl.ds(pl.multiple_of(number * rows, rows), rows)]
        return src, dst

    def send(head, number):
        src, dst = move(head, number)
        return remote(src, dst, send_sem.at[head], recv_sem.at[number], owner_of(head, heads))

    def keep():
        src, dst = move(head_of(me, heads), me)
        return pltpu.make_async_copy(src, dst, local_sem.at[0])

    def begin(head, carry):
        pl.when(owner_of(head, heads) != me)(lambda: send(head, me).start())
        return carry

    def taken(number, carry):
        pl.when(active & (number != me))(lambda: send(0, number).wait_recv())
        return carry

    def sent(head, carry):
        pl.when(owner_of(head, heads) != me)(lambda: send(head, me).wait_send())
        return carry

    lax.fori_loop(0, heads, begin, 0)
    pl.when(active)(lambda: keep().start())
    meanwhile()
    lax.fori_loop(0, group, taken, 0)
    pl.when(active)(lambda: keep().wait())
    lax.fori_loop(0, heads, sent, 0)


def backward_attention(lam, q, k, v, kt, o1, o2, lse, datt, cosine, sine, gain, block, extra=None, collective_id=None):
    length, width = q.shape
    full = lambda shape: pl.BlockSpec(shape, lambda i: (0,) * len(shape))
    arrays = (q, k, v, kt, o1, o2, lse, datt, cosine, sine, gain)
    outs = [((length, 3 * width), bf16), ((width, 1), f32), ((1, 1), f32)]
    share = collective_id is not None
    more, more_out, more_in, more_specs, out_specs = [], [], [], [], []
    if share:
        rows, wide = datt.shape
        grads, part = extra[2], (wide // group, wide)
        more_in, more_specs = list(extra), [full(a.shape) for a in extra[:2]] + [ANY] * 4
        more_out = [
            jax.ShapeDtypeStruct(part, bf16), jax.ShapeDtypeStruct(part, bf16),
            jax.ShapeDtypeStruct((grads.shape[0] // 2, grads.shape[1]), bf16),
            jax.ShapeDtypeStruct((rows, wide), bf16),
            jax.ShapeDtypeStruct((2, part[0], extra[4].shape[1] // 2 * group), bf16),
            jax.ShapeDtypeStruct((wide, 3 * width), bf16),
        ]
        out_specs = [full(part), ANY, ANY, ANY, ANY, full((wide, 3 * width))]
        more = [DMA((2, 2, 2)), DMA((1,)), pltpu.VMEM(extra[5].shape, bf16), pltpu.VMEM(part, f32)] + Scatter.scratch(*part) + Restore.scratch(2) + [
            pltpu.VMEM((length, width), bf16), DMA((wide // width,)), DMA((group,)), DMA((1,)),
        ]
    return pl.pallas_call(
        functools.partial(backward_kernel, block, share),
        grid=(length // block,),
        in_specs=[SMEM] + [full(a.shape) for a in arrays] + more_specs,
        out_specs=[full(shape) for shape, _ in outs] + out_specs,
        out_shape=[jax.ShapeDtypeStruct(shape, kind) for shape, kind in outs] + more_out,
        scratch_shapes=[
            pltpu.VMEM((length, width), bf16),
            pltpu.VMEM((width, length), bf16),
            pltpu.VMEM((8, length), f32),
            pltpu.VMEM((width, length), f32),
        ] + more,
        compiler_params=pltpu.CompilerParams(
            dimension_semantics=("arbitrary",), vmem_limit_bytes=56 * 2**20,
            collective_id=collective_id, has_side_effects=share,
        ),
        cost_estimate=busy,
        name="attention_backward",
    )(lam, *arrays, *more_in)


def rms_parts(value):
    return lax.rsqrt(jnp.mean(value * value, axis=-1, keepdims=True) + norm_eps)


def rms_back(value, factor, gain, upstream):
    scaled = upstream * gain
    mean = jnp.mean(scaled * value, axis=-1, keepdims=True)
    grad = factor * scaled - value * (factor * factor * factor) * mean
    return grad, jnp.sum(upstream * value * factor, axis=0)


def cube_body(
    block_input, positions, needle, cotangent, norm_gain1, w_query, w_key, w_value,
    lam_q1, lam_k1, lam_q2, lam_k2, sub_gain, w_out, norm_gain2, w_gate, w_up, w_down,
):
    rows, width = block_input.shape[1:]
    heads, half = lam_q1.shape
    head_width = sub_gain.shape[0]
    hidden = w_gate.shape[1]
    depth = w_query.shape[0]
    length = rows * group
    columns = hidden // group
    me, cube = place()
    my_head = head_of(me, heads)
    used = is_active(me, heads)
    active = used.astype(f32)
    here = jnp.broadcast_to(positions[0], (1, 8, rows))
    tokens_low, normed_all, places, w_head, w_d = first_exchange(
        block_input[0], here, norm_gain1[None], (w_query, w_key, w_value, w_down),
        heads, head_width, columns, 0,
    )
    tokens = tokens_low.astype(f32)
    factor1 = rms_parts(tokens)
    upstream = cotangent[0].astype(f32) * needle[0].astype(f32)[:, None]
    upstream_low = upstream.astype(bf16)
    places = places[:, 0].reshape(length)

    inv_freq = jnp.exp(-math.log(10000.0) * jnp.arange(half // 2, dtype=f32) / (half // 2))
    angles = inv_freq[:, None] * places.astype(f32)[None, :]
    cosine, sine = jnp.cos(angles), jnp.sin(angles)
    lam_vals, lam_pull = jax.vjp(lambdas, lam_q1, lam_k1, lam_q2, lam_k2)
    lam_mine = jnp.stack([lax.dynamic_index_in_dim(lam_vals, my_head, 0, False), active])
    gain_col = sub_gain[:, None]
    block = 4 * rows

    q, k, v, kt, o1, o2, lse, attended, w_gates, w_o = forward_attention(
        lam_mine, w_head, cosine, sine, gain_col, block,
        (w_gate, w_up, w_out, normed_all), rows, heads, columns, 1,
    )
    resid = tokens + dot(attended, w_o)
    factor2 = rms_parts(resid)
    normed_two = (resid * factor2 * norm_gain2).astype(bf16)
    grad_low, two_all, grad_all = second_exchange(normed_two, upstream_low, 2)

    both = dot(two_all, w_gates)
    gate, upper = both[:, :columns], both[:, columns:]
    grad_inner = dot(grad_all, w_d)
    sigma = jax.nn.sigmoid(gate)
    silu = gate * sigma
    inner = (silu * upper).astype(bf16)
    gate_low = (grad_inner * upper * sigma * (1.0 + gate * (1.0 - sigma))).astype(bf16)
    upper_low = (grad_inner * silu).astype(bf16)
    gates_low = jnp.concatenate([gate_low, upper_low], axis=1)
    grad_two, ffn_out, gate_grads, down_grads, gate_theirs = scatter(
        gates_low, w_gates, inner, w_d, two_all, grad_all, 3
    )
    output_low = (resid + ffn_out).astype(bf16)

    grad_resid_two, gain_two = rms_back(resid, factor2, norm_gain2, grad_two)
    grad_resid = grad_low.astype(f32) + grad_resid_two
    resid_low = grad_resid.astype(bf16)
    grad_att = dot(resid_low, w_o, 1, 1).astype(bf16)

    def combine(mine, theirs):
        part = theirs.shape[0]
        mine = lax.dynamic_slice_in_dim(mine, cube * part, part, 0)
        return (mine.astype(f32) + theirs.astype(f32)).astype(bf16)

    dqkv, dgain, dlam, out_part, out_theirs, down_theirs, output_back, gate_back, head_grads = backward_attention(
        lam_mine, q, k, v, kt, o1, o2, lse, grad_att, cosine, sine, gain_col, block,
        (attended, resid_low, down_grads, output_low, combine(gate_grads, gate_theirs), normed_all), 4,
    )
    hot = jax.nn.one_hot(my_head, heads, dtype=f32)
    lines = width // head_width
    small = jnp.concatenate([
        jnp.zeros((lines, head_width), f32), gain_two.reshape(lines, head_width),
        jnp.where(used, dgain[:, 0], 0.0)[None],
        jnp.pad(jnp.where(used, hot * dlam[0, 0], 0.0), (0, head_width - heads))[None],
    ])
    small = jnp.pad(small, ((0, -small.shape[0] % 8), (0, 0)))
    out_sum = (out_part.astype(f32) + out_theirs.astype(f32)).astype(bf16)
    down_back, head_back, out_pair, small, input_back = last_exchange(
        (
            dqkv, w_head, tokens_low, norm_gain1[None], grad_resid, head_grads, small,
            combine(down_grads, down_theirs), out_sum,
        ),
        heads, head_width, columns, 5,
    )
    output = output_back[None]
    input_grad = input_back.astype(f32)[None]
    out_grads = jnp.where(me // 8 == cube, out_sum, out_pair).astype(f32)
    grads = [a.astype(f32) for a in (gate_back[0], gate_back[1], down_back[0])]
    grads += [head_back[i].astype(f32) for i in range(3)]
    gain_one = small[:lines].reshape(-1)
    gain_two = small[lines : 2 * lines].reshape(-1)
    sub_grad = small[2 * lines]
    lam_grads = lam_pull(small[2 * lines + 1, :heads])
    squares = sum(jnp.sum(g * g) for g in lam_grads)
    return (
        output, input_grad, gain_one, grads[3], grads[4], grads[5],
        lam_grads[0], lam_grads[1], lam_grads[2], lam_grads[3], sub_grad, out_grads, gain_two,
        grads[0], grads[1], grads[2], jnp.mean(lam_vals), jnp.sqrt(squares),
    )


def gather_rows(value):
    return lax.all_gather(value, "seq", axis=0, tiled=True)


def scatter_sum(value):
    return lax.psum_scatter(value, "seq", scatter_dimension=0, tiled=True)


def exchange(value):
    return lax.all_to_all(value, "seq", split_axis=0, concat_axis=0, tiled=True)


def plain_body(
    devices, block_input, positions, needle, cotangent, norm_gain1, w_query, w_key, w_value,
    lam_q1, lam_k1, lam_q2, lam_k2, sub_gain, w_out, norm_gain2, w_gate, w_up, w_down,
):
    rows, width = block_input.shape[1:]
    heads, half = lam_q1.shape
    head_width = sub_gain.shape[0]
    hidden = w_gate.shape[1]
    depth = w_query.shape[0]
    length = rows * devices
    columns = hidden // devices
    head_of = [d * heads // devices for d in range(devices)]
    owner_of = [max(d for d in range(devices) if head_of[d] == h) for h in range(heads)]
    me = lax.axis_index("seq")
    my_head = me * heads // devices
    active = ((me + 1) * heads // devices > my_head).astype(f32)

    tokens = block_input[0].astype(f32)
    factor1 = rms_parts(tokens)
    normed = (tokens * factor1 * norm_gain1).astype(bf16)
    normed_all = gather_rows(normed)
    places = gather_rows(positions[0])

    by_head = jnp.stack([w.reshape(depth, heads, head_width) for w in (w_query, w_key, w_value)], 2)
    by_head = by_head.reshape(depth, heads, 3 * head_width).transpose(1, 0, 2)
    w_head = exchange(by_head[jnp.array(head_of)]).reshape(width, 3 * head_width)

    w_o = gather_rows(w_out)
    grad_out = cotangent[0].astype(f32) * needle[0].astype(f32)[:, None]
    grad_low = grad_out.astype(bf16)
    grad_all = gather_rows(grad_low)

    ffn = jnp.stack([w.reshape(depth, devices, columns) for w in (w_gate, w_up, w_down)], 2)
    ffn = ffn.reshape(depth, devices, 3 * columns).transpose(1, 0, 2)
    w_ffn = exchange(ffn).reshape(width, 3 * columns)

    inv_freq = jnp.exp(-math.log(10000.0) * jnp.arange(half // 2, dtype=f32) / (half // 2))
    angles = inv_freq[:, None] * places.astype(f32)[None, :]
    cosine, sine = jnp.cos(angles), jnp.sin(angles)
    lam_vals, lam_pull = jax.vjp(lambdas, lam_q1, lam_k1, lam_q2, lam_k2)
    lam_mine = jnp.stack([lax.dynamic_index_in_dim(lam_vals, my_head, 0, False), active])
    gain_col = sub_gain[:, None]
    block = math.gcd(length, 512)

    qkv = dot(w_head, normed_all, 0, 1)
    q, k, v, kt, o1, o2, lse, att = forward_attention(
        lam_mine, qkv, cosine, sine, gain_col, block
    )
    att_rows = exchange(att.reshape(devices, rows, head_width))
    attended = jnp.concatenate([att_rows[d] for d in owner_of], axis=1)
    resid = tokens + dot(attended, w_o)
    factor2 = rms_parts(resid)
    normed_two = (resid * factor2 * norm_gain2).astype(bf16)
    two_all = gather_rows(normed_two)

    both = dot(two_all, w_ffn[:, : 2 * columns])
    gate, upper = both[:, :columns], both[:, columns:]
    grad_inner = dot(grad_all, w_ffn[:, 2 * columns :])
    sigma = jax.nn.sigmoid(gate)
    silu = gate * sigma
    inner = (silu * upper).astype(bf16)
    gate_low = (grad_inner * upper * sigma * (1.0 + gate * (1.0 - sigma))).astype(bf16)
    upper_low = (grad_inner * silu).astype(bf16)
    gates_low = jnp.concatenate([gate_low, upper_low], axis=1)
    grad_two = scatter_sum(dot(gates_low, w_ffn[:, : 2 * columns], 1, 1).astype(bf16)).astype(f32)
    ffn_out = scatter_sum(dot(inner, w_ffn[:, 2 * columns :], 1, 1).astype(bf16)).astype(f32)
    output = (resid + ffn_out).astype(bf16)[None]

    grad_resid_two, gain_two = rms_back(resid, factor2, norm_gain2, grad_two)
    grad_resid = grad_out + grad_resid_two
    resid_low = grad_resid.astype(bf16)
    grad_att = dot(resid_low, w_o, 1, 1).astype(bf16)
    pieces = jnp.stack(
        [grad_att[:, h * head_width : (h + 1) * head_width] for h in head_of], axis=0
    )
    datt = exchange(pieces).reshape(length, head_width)

    dqkv, dgain, dlam = backward_attention(
        lam_mine, q, k, v, kt, o1, o2, lse, datt, cosine, sine, gain_col, block
    )
    partial = (dot(dqkv, w_head, 1, 1) * active).astype(bf16)
    grad_normed = scatter_sum(partial).astype(f32)
    grad_tokens, gain_one = rms_back(tokens, factor1, norm_gain1, grad_normed)
    input_grad = (grad_resid + grad_tokens)[None]

    def settle(value):
        other = lax.ppermute(value, "batch", [(0, 1), (1, 0)])
        return value.astype(f32) + other.astype(f32)

    ffn_grads = jnp.concatenate(
        [dot(two_all, gates_low, 0, 0), dot(grad_all, inner, 0, 0)], axis=1
    ).astype(bf16)
    ffn_grads = settle(exchange(ffn_grads.reshape(devices, depth, 3 * columns)))
    ffn_grads = ffn_grads.reshape(devices, depth, 3, columns).transpose(2, 1, 0, 3)
    ffn_grads = ffn_grads.reshape(3, depth, hidden)

    head_grads = dot(normed_all, dqkv, 0, 0).astype(bf16)
    head_grads = settle(exchange(head_grads.reshape(devices, depth, 3 * head_width)))
    head_grads = jnp.stack([head_grads[d] for d in owner_of], axis=1)
    head_grads = head_grads.reshape(depth, heads, 3, head_width).transpose(2, 0, 1, 3)
    head_grads = head_grads.reshape(3, depth, width)

    out_grads = dot(attended, resid_low, 0, 0).astype(bf16)
    out_grads = settle(scatter_sum(out_grads))

    hot = jax.nn.one_hot(my_head, heads, dtype=f32) * active
    small = lax.psum(
        (gain_one, gain_two, dgain[:, 0] * active, hot * dlam[0, 0]), ("batch", "seq")
    )
    lam_grads = lam_pull(small[3])
    squares = sum(jnp.sum(g * g) for g in lam_grads)
    return (
        output, input_grad, small[0], head_grads[0], head_grads[1], head_grads[2],
        lam_grads[0], lam_grads[1], lam_grads[2], lam_grads[3], small[2], out_grads, small[1],
        ffn_grads[0], ffn_grads[1], ffn_grads[2], jnp.mean(lam_vals), jnp.sqrt(squares),
    )


def solution(mesh):
    rows = P("seq", None)
    in_specs = (
        P("batch", "seq", None), P("batch", "seq"), P("batch", "seq"), P("batch", "seq", None),
        P(), rows, rows, rows, P(), P(), P(), P(), P(), rows, P(), rows, rows, rows,
    )
    out_specs = (
        P("batch", "seq", None), P("batch", "seq", None), P(), rows, rows, rows,
        P(), P(), P(), P(), P(), rows, P(), rows, rows, rows, P(), P(),
    )
    if mesh.shape["seq"] == group and mesh.shape["batch"] == 2:
        body = cube_body
    else:
        body = functools.partial(plain_body, mesh.shape["seq"])
    return jax.shard_map(body, mesh=mesh, in_specs=in_specs, out_specs=out_specs, check_vma=False)
```

```python
import functools
import math

import jax
import jax.numpy as jnp
from jax import lax
from jax.experimental import pallas as pl
from jax.experimental.pallas import tpu as pltpu
from jax.sharding import PartitionSpec as P

lam_init = 0.619
norm_eps = 1e-05
log2e = math.log2(math.e)
neg_large = -1e30
f32 = jnp.float32
bf16 = jnp.bfloat16


def lambdas(lam_q1, lam_k1, lam_q2, lam_k2):
    return (
        jnp.exp(jnp.sum(lam_q1 * lam_k1, axis=-1))
        - jnp.exp(jnp.sum(lam_q2 * lam_k2, axis=-1))
        + lam_init
    )


def dims(left_axis, right_axis):
    return (((left_axis,), (right_axis,)), ((), ()))


def dot(left, right, left_axis=1, right_axis=0):
    return lax.dot_general(left, right, dims(left_axis, right_axis), preferred_element_type=f32)


MESH = pl.DeviceIdType.MESH
ANY = pl.BlockSpec(memory_space=pltpu.HBM)
VMEM = pl.BlockSpec(memory_space=pltpu.VMEM)
SMEM = pl.BlockSpec(memory_space=pltpu.SMEM)
DMA = pltpu.SemaphoreType.DMA
group = 16
busy = pl.CostEstimate(flops=4 * 10**10, bytes_accessed=10**7, transcendentals=0)
sides = (8, 4, 2)
even = ((8, 4, 2), (4, 2, 8), (2, 8, 4))
few_z = ((4, 8, 2), (4, 2, 8))
mid_z = ((4, 8, 2), (4, 2, 8), (2, 4, 8), (8, 4, 2))
sum_even = ((2, 8, 4), (8, 2, 4), (4, 2, 8))
sum_few_z = ((2, 8, 4), (8, 2, 4))


def place():
    seq = lax.axis_index("seq")
    return lax.axis_index("batch") * 8 + seq % 8, seq // 8


def device(number, cube=None):
    return {"batch": number // 8, "seq": (place()[1] if cube is None else cube) * 8 + number % 8}


def partner():
    return {"batch": lax.axis_index("batch"), "seq": lax.axis_index("seq") ^ 8}


def swapped():
    batch, seq = lax.axis_index("batch"), lax.axis_index("seq")
    return {"batch": 1 - batch, "seq": seq ^ 8}, batch != seq // 8


def anyone(index):
    return index // group * 8 + index % 8, index % group // 8


def everywhere():
    return lax.axis_index("batch") * group + lax.axis_index("seq")


def remote(src, dst, send_sem, recv_sem, number):
    return pltpu.make_async_remote_copy(
        src_ref=src, dst_ref=dst, send_sem=send_sem, recv_sem=recv_sem,
        device_id=device(number), device_id_type=MESH,
    )


def greet(cross=False, swap=False):
    me = place()[0]
    barrier = pltpu.get_barrier_semaphore()
    count = 1 + len(sides)
    for mask in (1,) + sides:
        pl.semaphore_signal(barrier, inc=1, device_id=device(me ^ mask), device_id_type=MESH)
    if cross:
        pl.semaphore_signal(barrier, inc=1, device_id=partner(), device_id_type=MESH)
        count = count + 1
    if swap:
        target, moved = swapped()

        @pl.when(moved)
        def _():
            pl.semaphore_signal(barrier, inc=1, device_id=target, device_id_type=MESH)

        count = count + moved.astype(jnp.int32)
    pl.semaphore_wait(barrier, count)


def greet_all():
    barrier = pltpu.get_barrier_semaphore()
    me = everywhere()

    def tell(mask, carry):
        target = device(*anyone(me ^ mask))
        pl.semaphore_signal(barrier, inc=1, device_id=target, device_id_type=MESH)
        return carry

    lax.fori_loop(1, 2 * group, tell, 0)
    pl.semaphore_wait(barrier, 2 * group - 1)


class Cargo:
    def __init__(self, cross, swap, sems):
        self.cross, self.swap, self.sems = cross, swap, sems

    def copies(self):
        for i, (src, dst) in enumerate(self.cross):
            yield None, pltpu.make_async_remote_copy(
                src_ref=src, dst_ref=dst, send_sem=self.sems.at[0, i], recv_sem=self.sems.at[1, i],
                device_id=partner(), device_id_type=MESH,
            ), None
        target, moved = swapped()
        for i, (src, dst) in enumerate(self.swap):
            j = len(self.cross) + i
            yield moved, pltpu.make_async_remote_copy(
                src_ref=src, dst_ref=dst, send_sem=self.sems.at[0, j], recv_sem=self.sems.at[1, j],
                device_id=target, device_id_type=MESH,
            ), pltpu.make_async_copy(src, dst, self.sems.at[0, j])

    def start(self):
        for moved, far, near in self.copies():
            if moved is None:
                far.start()
            else:
                pl.when(moved)(lambda: far.start())
                pl.when(jnp.logical_not(moved))(lambda: near.start())

    def finish(self):
        for moved, far, near in self.copies():
            if moved is None:
                far.wait()
            else:
                pl.when(moved)(lambda: far.wait())
                pl.when(jnp.logical_not(moved))(lambda: near.wait())


class Gather:
    def __init__(self, orders, items, send_sem, recv_sem, local_sem):
        self.orders = orders
        self.items = [item if len(item) == 4 else item + (len(orders),) for item in items]
        self.send_sem, self.recv_sem, self.local_sem = send_sem, recv_sem, local_sem
        self.me = place()[0]

    def order(self, part):
        return list(self.orders[part])

    def view(self, item, part, number):
        src, out, row, parts = self.items[item]
        rows, width = src.shape[0], src.shape[-1] // parts
        at = pl.ds(row(number), rows)
        if parts == 1:
            return out.at[at]
        return out.at[at, pl.ds(part * width, width)]

    def copy(self, item, part, number, lane, target, own=False):
        src, out, row, parts = self.items[item]
        width = src.shape[-1] // parts
        here = self.view(item, part, number)
        source = (src if parts == 1 else src.at[:, pl.ds(part * width, width)]) if own else here
        arrival = self.recv_sem.at[item, 0, group] if lane == 3 else self.recv_sem.at[item, part, number]
        return remote(source, here, self.send_sem.at[item], arrival, target)

    def every(self):
        return [(i, p) for i in range(len(self.items)) for p in range(self.items[i][3])]

    def local(self, item):
        src, out, row, _ = self.items[item]
        return pltpu.make_async_copy(src, out.at[pl.ds(row(self.me), src.shape[0])], self.local_sem.at[item])

    def start(self, items=None):
        chosen = [(i, p) for i, p in self.every() if items is None or i in items]
        for k in range(3):
            for i, p in chosen:
                self.copy(i, p, self.me, k, self.me ^ self.order(p)[k], True).start()
        for i, p in chosen:
            self.copy(i, p, self.me, 3, self.me ^ 1, True).start()
        for i in range(len(self.items)):
            if items is None or i in items:
                self.local(i).start()

    def arrivals(self, part, step):
        order = self.order(part)
        masks = [0]
        for side in order[:step]:
            masks = masks + [m ^ side for m in masks]
        return [m ^ order[step] for m in masks]

    def step(self, step, items=None):
        for i, p in self.every():
            if items is not None and i not in items:
                continue
            for mask in self.arrivals(p, step):
                number = self.me ^ mask
                self.copy(i, p, number, 0, self.me).wait_recv()
                for k in range(step + 1, 3):
                    self.copy(i, p, number, k, self.me ^ self.order(p)[k]).start()
                self.copy(i, p, number, 3, self.me ^ 1).start()

    def finish(self, items=None):
        for i in range(len(self.items)):
            if items is None or i in items:
                src, out = self.items[i][:2]
                for blocks, sem in ((8, self.recv_sem.at[i, 0, group]), (15, self.send_sem.at[i])):
                    some = out.at[pl.ds(0, blocks * src.shape[0])]
                    pltpu.make_async_copy(some, some, sem).wait()
                self.local(i).wait()

    @staticmethod
    def scratch(count):
        return [DMA((count,)), DMA((count, 4, group + 1)), DMA((count,))]


def natural(rows):
    return lambda number: pl.multiple_of(number * rows, rows)


def second_kernel(normed, given, grads, normed_all, grads_all, cargo_sem, *sems):
    greet(swap=True)
    cargo = Cargo([], [(given, grads)], cargo_sem)
    cargo.start()
    row = natural(normed.shape[0])
    run = Gather(even, [(normed, normed_all, row), (grads, grads_all, row)], *sems[:3])
    run.start([0])
    run.step(0, [0])
    run.step(1, [0])
    cargo.finish()
    run.start([1])
    run.step(2, [0])
    for step in range(3):
        run.step(step, [1])
    run.finish()


def second_exchange(normed, given, collective_id):
    rows, width = normed.shape
    outs = [(rows, width), (group * rows, width), (group * rows, width)]
    return pl.pallas_call(
        second_kernel,
        in_specs=[ANY] * 2,
        out_specs=[ANY] * 3,
        out_shape=[jax.ShapeDtypeStruct(shape, bf16) for shape in outs],
        scratch_shapes=[DMA((2, 1))] + Gather.scratch(2),
        compiler_params=pltpu.CompilerParams(collective_id=collective_id, has_side_effects=True),
        cost_estimate=busy,
        name="second_exchange",
    )(normed, given)


class Scatter:
    def __init__(self, orders, own, core_in, side_in, core_s, core_r, side_s, side_r):
        self.orders, self.parts = orders, len(orders)
        self.own, self.core_in, self.side_in = own, core_in, side_in
        self.core_s, self.core_r, self.side_s, self.side_r = core_s, core_r, side_s, side_r
        self.me = place()[0]
        self.core = self.me % 2
        self.rows, self.width = own.shape[2], own.shape[3]
        self.part = self.width // self.parts

    def cols(self, part):
        return pl.ds(part * self.part, self.part)

    def order(self, part):
        return list(self.orders[part])

    def core_copy(self, part):
        c = self.cols(part)
        return remote(
            self.own.at[1 - self.core, :, :, c], self.core_in.at[:, :, c],
            self.core_s.at[part], self.core_r.at[part], self.me ^ 1,
        )

    def moves(self, part, step):
        order = self.order(part)
        masks = [0]
        for side in order[:step:-1]:
            masks = masks + [m ^ side for m in masks]
        base = {0: 0, 1: 4, 2: 6}[step]
        masks = sorted(masks, key=lambda m: [not m & side for side in order[step + 1 :]])
        return [(m ^ order[step], base + j) for j, m in enumerate(masks)]

    def side_copy(self, part, step, mask, slot):
        c = self.cols(part)
        peer = self.me ^ self.order(part)[step]
        return remote(
            self.own.at[self.core, (self.me ^ mask) // 2, :, c], self.side_in.at[slot, :, c],
            self.side_s.at[part, slot], self.side_r.at[part, slot], peer,
        )

    def multiply(self, part, lhs, rhs, axis=1):
        c = self.cols(part)
        chunk = 4 * self.rows

        def quarter(q, carry):
            at = pl.ds(pl.multiple_of(q * chunk, chunk), chunk)
            if isinstance(lhs, tuple):
                rows, k = slice(part * self.part, (part + 1) * self.part), lhs[0].shape[1]
                p = dot(lhs[0][at, :], rhs[rows, :k], 1, 1) + dot(lhs[1][at, :], rhs[rows, k:], 1, 1)
            elif axis:
                p = dot(lhs[at, :], rhs[part * self.part : (part + 1) * self.part, :], 1, 1)
            else:
                p = dot(lhs[:, at], rhs[:, part * self.part : (part + 1) * self.part], 0, 0)
            p = p.astype(bf16).reshape(4, self.rows, self.part)
            for j in range(4):
                self.own[j % 2, 2 * q + j // 2, :, c] = p[j]
            return carry

        lax.fori_loop(0, 4, quarter, 0)
        self.core_copy(part).start()

    def add(self, number, part, extra):
        c = self.cols(part)
        at = (self.core, number // 2, slice(None), c)
        self.own[at] = (self.own[at].astype(f32) + extra.astype(f32)).astype(bf16)

    def merge(self, part):
        c = self.cols(part)
        self.core_copy(part).wait()
        moves = self.moves(part, 0)
        for mask, slot in moves:
            self.add(self.me ^ mask, part, self.core_in[(self.me ^ mask) // 2, :, c])
            self.side_copy(part, 0, mask, slot).start()
        for mask, _ in moves:
            number = self.me ^ mask ^ self.order(part)[0]
            self.add(number, part, self.core_in[number // 2, :, c])

    def begin(self, lhs, rhs, axis=1):
        self.multiply(0, lhs, rhs, axis)
        for part in range(1, self.parts):
            self.multiply(part, lhs, rhs, axis)
            self.merge(part - 1)
        self.merge(self.parts - 1)

    def halve(self, part, step, out=None):
        c = self.cols(part)
        leaving = dict(self.moves(part, step + 1)) if step < 2 else {}
        for mask, slot in self.moves(part, step):
            kept = mask ^ self.order(part)[step]
            self.side_copy(part, step, mask, slot).wait_recv()
            if out is not None:
                at = (self.core, self.me // 2, slice(None), c)
                out[:, c] = self.own[at].astype(f32) + self.side_in[slot, :, c].astype(f32)
                continue
            self.add(self.me ^ kept, part, self.side_in[slot, :, c])
            if kept in leaving:
                self.side_copy(part, step + 1, kept, leaving[kept]).start()

    def halve_all(self, step, out):
        for part in range(self.parts):
            self.halve(part, step, out if step == 2 else None)

    def finish(self):
        for part in range(self.parts):
            for step in range(3):
                for mask, slot in self.moves(part, step):
                    self.side_copy(part, step, mask, slot).wait_send()

    @staticmethod
    def scratch(rows, width):
        return [
            pltpu.VMEM((2, 8, rows, width), bf16), pltpu.VMEM((8, rows, width), bf16),
            pltpu.VMEM((7, rows, width), bf16), DMA((4,)), DMA((4,)), DMA((4, 7)), DMA((4, 7)),
        ]


def for_partner(grads, rows):
    return grads.at[pl.ds(pl.multiple_of((1 - place()[1]) * rows, rows), rows)]


def weight_grads(left, right, out, start=0):
    chunk, width = 512, right.shape[1]

    def some(j, carry):
        at = pl.ds(pl.multiple_of(j * chunk, chunk), chunk)
        out[at, start : start + width] = dot(left[:, at], right[...], 0, 0).astype(bf16)
        return carry

    lax.fori_loop(0, left.shape[1] // chunk, some, 0)


def scatter_kernel(
    gate, upper, rhs, lhs_two, rhs_two, left, left_two, out, out_two, grads, grads_two, taken,
    cargo_sem, copy_sem, held, held_two, *scratch,
):
    greet(cross=True)
    cargo = Cargo([(for_partner(grads, taken.shape[0]), taken)], [], cargo_sem)
    copies = [pltpu.make_async_copy(a, b, copy_sem.at[i]) for i, (a, b) in enumerate(((left, held), (left_two, held_two)))]
    for copy in copies:
        copy.start()
    run, more = Scatter(sum_even, *scratch[:7]), Scatter(sum_even, *scratch[7:])
    run.begin((gate, upper), rhs)
    more.begin(lhs_two, rhs_two)
    copies[0].wait()
    weight_grads(held, gate, grads)
    weight_grads(held, upper, grads, gate.shape[1])
    cargo.start()
    for step in range(3):
        run.halve_all(step, out)
        more.halve_all(step, out_two)
        if step == 0:
            copies[1].wait()
            weight_grads(held_two, lhs_two, grads_two)
    run.finish()
    more.finish()
    cargo.finish()


def scatter(gate, upper, rhs, lhs_two, rhs_two, left, left_two, collective_id):
    rows, width = gate.shape[0] // group, rhs.shape[0]
    return pl.pallas_call(
        scatter_kernel,
        in_specs=[VMEM] * 5 + [ANY] * 2,
        out_specs=[VMEM] * 4 + [ANY],
        out_shape=[jax.ShapeDtypeStruct((rows, width), f32)] * 2
        + [
            jax.ShapeDtypeStruct(rhs.shape, bf16), jax.ShapeDtypeStruct((width, lhs_two.shape[1]), bf16),
            jax.ShapeDtypeStruct((width // 2, rhs.shape[1]), bf16),
        ],
        scratch_shapes=[DMA((2, 1)), DMA((2,)), pltpu.VMEM(left.shape, bf16), pltpu.VMEM(left.shape, bf16)] + Scatter.scratch(rows, width) + Scatter.scratch(rows, width),
        compiler_params=pltpu.CompilerParams(
            collective_id=collective_id, has_side_effects=True, vmem_limit_bytes=60 * 2**20
        ),
        cost_estimate=busy,
        name=f"scatter{collective_id}",
    )(gate, upper, rhs, lhs_two, rhs_two, left, left_two)


def head_of(number, heads):
    return number * heads // group


def is_active(number, heads):
    return (number + 1) * heads // group > number * heads // group


def owner_of(head, heads):
    return ((head + 1) * group + heads - 1) // heads - 1


class Deal:
    def __init__(self, items, send_sem, recv_sem):
        self.items, self.send_sem, self.recv_sem = items, send_sem, recv_sem
        self.me = everywhere()

    def views(self, item, source, target):
        own, out, column = self.items[item]
        rows, width = own.shape[0] // 2, out.shape[1]
        number, cube = anyone(source)
        half = pl.ds(pl.multiple_of(number // 8 * rows, rows), rows)
        row = (cube * 8 + number % 8) * (2 * rows) + number // 8 * rows
        cols = pl.ds(column(anyone(target)[0]), width)
        return own.at[half, cols], out.at[pl.ds(pl.multiple_of(row, rows), rows)]

    def copy(self, item, source, target, far):
        src, dst = self.views(item, source, target)
        return pltpu.make_async_remote_copy(
            src_ref=src, dst_ref=dst, send_sem=self.send_sem.at[item, far],
            recv_sem=self.recv_sem.at[item, far], device_id=device(*anyone(target)), device_id_type=MESH,
        )

    def local(self, item):
        src, dst = self.views(item, self.me, self.me)
        return pltpu.make_async_copy(src, dst, self.recv_sem.at[item, 0])

    def whole(self, item, sem, blocks):
        own, out, _ = self.items[item]
        some = out.at[pl.ds(0, blocks * own.shape[0] // 2)]
        pltpu.make_async_copy(some, some, sem).wait()

    def start_near(self):
        def begin(mask, carry):
            for i in range(len(self.items)):
                self.copy(i, self.me, self.me ^ (mask % 8 + mask // 8 * group), 0).start()
            return carry

        lax.fori_loop(1, group, begin, 0)
        for i in range(len(self.items)):
            self.local(i).start()

    def start_far(self):
        def begin(mask, carry):
            for i in range(len(self.items)):
                self.copy(i, self.me, self.me ^ (8 + mask % 8 + mask // 8 * group), 1).start()
            return carry

        lax.fori_loop(0, group, begin, 0)

    def finish_near(self):
        for i in range(len(self.items)):
            self.whole(i, self.recv_sem.at[i, 0], group)
            self.whole(i, self.send_sem.at[i, 0], group - 1)

    def finish_far(self):
        for i in range(len(self.items)):
            self.whole(i, self.recv_sem.at[i, 1], group)
            self.whole(i, self.send_sem.at[i, 1], group)

    @staticmethod
    def scratch(count):
        return [DMA((count, 2)), DMA((count, 2))]


def first_kernel(
    head_width, heads, columns, given, places, gain, w_q, w_k, w_v, w_down,
    tokens, tokens_all, places_all, w_head, w_d, land, places_land, normed, cargo_sem, *sems,
):
    greet_all()
    cargo = Cargo([], [(given, land), (places, places_land)], cargo_sem)
    cargo.start()
    column = lambda number: pl.multiple_of(head_of(number, heads) * head_width, head_width)
    deal = Deal(
        [
            (w, w_head.at[:, pl.ds(i * head_width, head_width)], column)
            for i, w in enumerate((w_q, w_k, w_v))
        ],
        *sems[3:5],
    )
    own = natural(columns)
    down = Deal([(w_down, w_d, own)], *sems[5:7])
    deal.start_near()
    down.start_near()
    cargo.finish()
    value = land[...].astype(f32)
    factor = lax.rsqrt(jnp.mean(value * value, axis=-1, keepdims=True) + norm_eps)
    normed[...] = (value * factor * gain[...]).astype(bf16)
    run = Gather(
        mid_z, [(normed, tokens_all, natural(normed.shape[0])), (places_land, places_all, natural(1), 1)], *sems[:3]
    )
    run.start()
    deal.start_far()
    tokens[...] = land[...]
    run.step(0)
    down.start_far()
    run.step(1)
    run.step(2)
    run.finish()
    for some in (deal, down):
        some.finish_near()
        some.finish_far()


def gate_deal(w_gate, w_up, w_gates, sems):
    columns = w_gates.shape[1] // 2
    views = [w_gates.at[:, pl.ds(i * columns, columns)] for i in range(2)]
    return Deal([(w, view, natural(columns)) for w, view in zip((w_gate, w_up), views)], *sems)


def first_exchange(given, places, gain, weights, heads, head_width, columns, collective_id):
    rows, width = given.shape
    outs = [
        ((rows, width), bf16), ((group * rows, width), bf16), ((group,) + places.shape[1:], jnp.int32),
        ((width, 3 * head_width), bf16), ((width, columns), bf16),
    ]
    return pl.pallas_call(
        functools.partial(first_kernel, head_width, heads, columns),
        in_specs=[VMEM, VMEM, VMEM] + [ANY] * 4,
        out_specs=[VMEM] + [ANY] * 4,
        out_shape=[jax.ShapeDtypeStruct(shape, kind) for shape, kind in outs],
        scratch_shapes=[
            pltpu.VMEM((rows, width), bf16), pltpu.VMEM(places.shape, jnp.int32),
            pltpu.VMEM((rows, width), bf16), DMA((2, 2)),
        ] + Gather.scratch(2) + Deal.scratch(3) + Deal.scratch(1),
        compiler_params=pltpu.CompilerParams(
            collective_id=collective_id, has_side_effects=True, vmem_limit_bytes=60 * 2**20
        ),
        cost_estimate=busy,
        name="first_exchange",
    )(given, places, gain, *weights)


class Restore:
    def __init__(self, grads, land, sources, column, send_sem, recv_sem, local_sem):
        self.grads, self.land, self.sources, self.column = grads, land, sources, column
        self.send_sem, self.recv_sem, self.local_sem = send_sem, recv_sem, local_sem
        self.me = place()[0]
        self.count, self.rows = land.shape[0], land.shape[1]
        self.width = grads.shape[1] // self.count
        self.blocks = land.shape[2] // self.width // 2

    def move(self, i, source, target):
        rows = pl.ds(pl.multiple_of(target % 8 * self.rows, self.rows), self.rows)
        src = self.grads.at[rows, pl.ds(i * self.width, self.width)]
        return src, self.land.at[i, :, pl.ds(self.column(source), self.width)]

    def send(self, i, source, target):
        src, dst = self.move(i, source, target)
        return remote(src, dst, self.send_sem.at[i, 0], self.recv_sem.at[i, source], target)

    def keep(self, i):
        src, dst = self.move(i, self.me, self.me)
        return pltpu.make_async_copy(src, dst, self.local_sem.at[i])

    def pass_on(self, i, source):
        here = self.move(i, source, self.me)[1]
        return remote(here, here, self.send_sem.at[i, 1], self.recv_sem.at[i, group], self.me ^ 8)

    def start(self):
        mine = self.sources(self.me)

        def begin(mask, carry):
            for i in range(self.count):
                pl.when(mine)(lambda: self.send(i, self.me, self.me ^ mask).start())
            return carry

        lax.fori_loop(1, 8, begin, 0)
        for i in range(self.count):
            pl.when(mine)(lambda: self.keep(i).start())

    def middle(self):
        mine = self.sources(self.me)

        def forward(mask, carry):
            other = self.me ^ mask
            for i in range(self.count):

                @pl.when(self.sources(other))
                def _():
                    self.send(i, other, self.me).wait_recv()
                    self.pass_on(i, other).start()

            return carry

        for i in range(self.count):

            @pl.when(mine)
            def _():
                self.keep(i).wait()
                self.pass_on(i, self.me).start()

        lax.fori_loop(1, 8, forward, 0)

    def finish(self):
        mine = self.sources(self.me)

        def wait(i, blocks, sem):
            some = self.land.at[i, :, pl.ds(0, blocks * self.width)]
            pltpu.make_async_copy(some, some, sem).wait()

        for i in range(self.count):
            pl.when(mine)(lambda: wait(i, 7, self.send_sem.at[i, 0]))
            wait(i, self.blocks, self.send_sem.at[i, 1])
            wait(i, self.blocks, self.recv_sem.at[i, group])

    @staticmethod
    def scratch(count):
        return [DMA((count, 2)), DMA((count, group + 1)), DMA((count,))]


def last_kernel(
    heads, head_width, columns,
    dqkv, w_head, tokens, gain, grad_resid, head, small, ffn_sum, out_sum,
    ffn_out, head_out, pair_out, total_out, input_out,
    result8, input_low, small_all, small_land, head_land, head_sum,
    cargo_sem, pair_sem, total_send, total_recv, *refs,
):
    me, cube = place()
    width = tokens.shape[1]
    greet_all()
    run = Scatter(sum_even, *refs[:7])
    sems = refs[7:]
    column = lambda n: pl.multiple_of(head_of(n, heads) * head_width, head_width)
    ffn_back = Restore(ffn_sum, ffn_out, lambda n: n >= 0, natural(columns), *sems[0:3])
    head_back = Restore(head_sum, head_out, lambda n: is_active(n, heads), column, *sems[3:6])
    half = head_land.shape[0]
    head_cargo = Cargo([(for_partner(head, half), head_land)], [], cargo_sem.at[0])
    input_cargo = Cargo([], [(input_low, input_out)], cargo_sem.at[1])
    small_cargo = Cargo([(small_all.at[me], small_land)], [], cargo_sem.at[3])
    pair = remote(out_sum, pair_out, pair_sem.at[0], pair_sem.at[1], me ^ 8)

    def send(source, target):
        return remote(
            small_all.at[me], small_all.at[source], total_send.at[target], total_recv.at[source], target
        )

    head_cargo.start()
    run.begin(dqkv, w_head)
    ffn_back.start()
    pair.start()
    run.halve_all(0, None)
    run.halve_all(1, None)
    ffn_back.middle()
    run.halve_all(2, result8)

    value = tokens[...].astype(f32)
    factor = lax.rsqrt(jnp.mean(value * value, axis=-1, keepdims=True) + norm_eps)
    upstream = result8[...]
    scaled = upstream * gain[...]
    mean = jnp.mean(scaled * value, axis=-1, keepdims=True)
    grad = factor * scaled - value * (factor * factor * factor) * mean
    input_low[...] = (grad_resid[...] + grad).astype(bf16)
    input_cargo.start()
    gain_one = jnp.sum(upstream * value * factor, axis=0, keepdims=True)
    small_all[me] = small[...]
    for i in range(width // head_width):
        small_all[me, i : i + 1, :] = gain_one[:, i * head_width : (i + 1) * head_width]
    small_cargo.start()
    head_cargo.finish()
    mine = pl.ds(pl.multiple_of(cube * half, half), half)
    head_sum[...] = (head[mine, :].astype(f32) + head_land[...].astype(f32)).astype(bf16)
    head_back.start()
    small_cargo.finish()
    small_all[me] = small_all[me] + small_land[...]

    def begin(mask, carry):
        send(me, me ^ mask).start()
        return carry

    lax.fori_loop(1, group, begin, 0)
    head_back.middle()

    def taken(mask, carry):
        send(me ^ mask, me).wait_recv()
        send(me, me ^ mask).wait_send()
        return carry

    lax.fori_loop(1, group, taken, 0)
    result = small_all[0]
    for number in range(1, group):
        result = result + small_all[number]
    total_out[...] = result
    pair.wait()
    run.finish()
    input_cargo.finish()
    ffn_back.finish()
    head_back.finish()


def last_exchange(arrays, heads, head_width, columns, collective_id):
    dqkv, w_head, tokens, gain, grad_resid, head, small, ffn_sum, out_sum = arrays
    rows, width = tokens.shape
    part = out_sum.shape[0]
    half = (head.shape[0] // 2, head.shape[1])
    outs = [
        ((1, part, columns * group), bf16), ((3, part, width), bf16), (out_sum.shape, bf16),
        (small.shape, f32), ((rows, width), bf16),
    ]
    memory = pltpu.VMEM
    return pl.pallas_call(
        functools.partial(last_kernel, heads, head_width, columns),
        in_specs=[VMEM] * 7 + [ANY] * 2,
        out_specs=[ANY, ANY, ANY, VMEM, ANY],
        out_shape=[jax.ShapeDtypeStruct(shape, kind) for shape, kind in outs],
        scratch_shapes=[
            memory((rows, width), f32), memory((rows, width), bf16),
            memory((group,) + small.shape, f32), memory(small.shape, f32), memory(half, bf16), memory(half, bf16),
            DMA((4, 2, 1)), DMA((2,)), DMA((group,)), DMA((group,)),
        ]
        + Scatter.scratch(rows, width) + Restore.scratch(1) + Restore.scratch(3),
        compiler_params=pltpu.CompilerParams(
            collective_id=collective_id, has_side_effects=True, vmem_limit_bytes=48 * 2**20
        ),
        cost_estimate=busy,
        name="last_exchange",
    )(*arrays)


def rotated(value, cosine, sine, inverse=False):
    parts = []
    step = cosine.shape[0]
    sign = -1.0 if inverse else 1.0
    for start in range(0, value.shape[0], 2 * step):
        first = value[start : start + step]
        second = value[start + step : start + 2 * step]
        parts.append(first * cosine - sign * (second * sine))
        parts.append(second * cosine + sign * (first * sine))
    return jnp.concatenate(parts, axis=0)


def forward_kernel(
    block, share, lam_ref, qkv_ref, cos_ref, sin_ref, gain_ref, *refs,
):
    step = pl.program_id(0)
    if share:
        (w_one, w_two, w_rows, normed), refs = refs[:4], refs[4:]
    q_ref, k_ref, v_ref, kt_ref, o1_ref, o2_ref, lse_ref, *refs = refs
    if share:
        out_ref, both_ref, w_all = refs[:3]
        qt_ref, vt_ref, att_ref, w_land, held, send_sem, recv_sem, local_sem, cargo_sem, *sems = refs[3:]
        copy = pltpu.make_async_copy(normed, held, local_sem.at[1])
        me, cube = place()
        deal = gate_deal(w_one, w_two, both_ref, sems[3:])
        sub = w_land.shape[0]
        w_half = w_rows.at[pl.ds(pl.multiple_of(me // 8 * sub, sub), sub)]

        def spot(which):
            return lambda number: pl.multiple_of((which * 8 + number % 8) * (2 * sub) + number // 8 * sub, sub)

        run = Gather(few_z, [(w_half, w_all, spot(cube)), (w_land, w_all, spot(1 - cube))], *sems[:3])
        rows_cargo = Cargo([(w_half, w_land)], [], cargo_sem)

        @pl.when(step == 0)
        def _():
            copy.start()
            greet_all()
            rows_cargo.start()
            run.start([0])
            deal.start_near()

        @pl.when(step == 1)
        def _():
            rows_cargo.finish()
            run.start([1])
            deal.start_far()

        @pl.when(step == 2)
        def _():
            run.step(0)

        @pl.when(step == 3)
        def _():
            run.step(1)
    else:
        att_ref, qt_ref, vt_ref = refs
    width = v_ref.shape[1]
    half = width // 2
    length = q_ref.shape[0]
    scale = half ** -0.5 * log2e

    @pl.when(step == 0)
    def _():
        def prepare(index, carry):
            cols = pl.ds(pl.multiple_of(index * block, block), block)
            cosine, sine = cos_ref[:, cols], sin_ref[:, cols]
            qkv = dot(held[cols, :], qkv_ref[...]).T if share else qkv_ref[:, cols]
            query = rotated(qkv[0:width], cosine, sine)
            key = rotated(qkv[width : 2 * width], cosine, sine)
            value = qkv[2 * width : 3 * width]
            qt_ref[:, cols] = query.astype(bf16)
            kt_ref[:, cols] = key.astype(bf16)
            vt_ref[:, cols] = value.astype(bf16)
            q_ref[cols, :] = query.T.astype(bf16)
            k_ref[cols, :] = key.T.astype(bf16)
            v_ref[cols, :] = value.T.astype(bf16)
            return carry

        if share:
            copy.wait()
        lax.fori_loop(0, length // block, prepare, 0)

    own = pl.ds(pl.multiple_of(step * block, block), block)
    queries = qt_ref[:, own]
    key_ids = lax.broadcasted_iota(jnp.int32, (block, block), 0)
    query_ids = lax.broadcasted_iota(jnp.int32, (block, block), 1)

    def visit(index, state, diagonal):
        rows = pl.ds(pl.multiple_of(index * block, block), block)
        values = vt_ref[:, rows]
        out = []
        for part in range(2):
            top, total, acc = state[part]
            lo, hi = part * half, (part + 1) * half
            scores = dot(k_ref[rows, lo:hi], queries[lo:hi]) * scale
            if diagonal:
                scores = jnp.where(key_ids <= query_ids, scores, neg_large)
            new_top = jnp.maximum(top, jnp.max(scores, axis=0, keepdims=True))
            weights = jnp.exp2(scores - new_top)
            fade = jnp.exp2(top - new_top)
            total = total * fade + jnp.sum(weights, axis=0, keepdims=True)
            acc = acc * fade + dot(values, weights.astype(bf16))
            out.append((new_top, total, acc))
        return tuple(out)

    start = tuple(
        (
            jnp.full((1, block), neg_large, f32),
            jnp.zeros((1, block), f32),
            jnp.zeros((width, block), f32),
        )
        for _ in range(2)
    )
    state = lax.fori_loop(0, step, lambda index, now: visit(index, now, False), start)
    state = visit(step, state, True)
    outs = []
    for part, ref in ((0, o1_ref), (1, o2_ref)):
        top, total, acc = state[part]
        result = acc / total
        ref[:, own] = result
        lse_ref[pl.ds(part, 1), own] = top + jnp.log2(total)
        outs.append(result)
    mixed = outs[0] - lam_ref[0] * outs[1]
    factor = lax.rsqrt(jnp.mean(mixed * mixed, axis=0, keepdims=True) + norm_eps)
    attended = mixed * factor * gain_ref[...] * (1.0 - lam_init)
    att_ref[own, :] = attended.T.astype(bf16)
    if share:
        rows, heads = out_ref.shape[0], out_ref.shape[1] // width
        active = is_active(me, heads)

        def part(number, head):
            cols = pl.ds(pl.multiple_of(head * width, width), width)
            return att_ref.at[pl.ds(pl.multiple_of(number * rows, rows), rows)], out_ref.at[:, cols]

        def send(number, head):
            src, dst = part(number, head)
            return remote(src, dst, send_sem.at[number], recv_sem.at[head], number)

        def keep():
            src, dst = part(me, head_of(me, heads))
            return pltpu.make_async_copy(src, dst, local_sem.at[0])

        for j in range(block // rows):
            number = step * (block // rows) + j
            pl.when(active & (number != me))(lambda: send(number, head_of(me, heads)).start())
            pl.when(active & (number == me))(lambda: keep().start())

        @pl.when(step == pl.num_programs(0) - 1)
        def _():
            def sent(number, carry):
                pl.when(active & (number != me))(lambda: send(number, 0).wait_send())
                return carry

            def taken(head, carry):
                pl.when(owner_of(head, heads) != me)(lambda: send(me, head).wait_recv())
                return carry

            lax.fori_loop(0, heads, taken, 0)
            lax.fori_loop(0, group, sent, 0)
            pl.when(active)(lambda: keep().wait())
            run.step(2)
            run.finish()
            deal.finish_near()
            deal.finish_far()


def forward_attention(lam, qkv, cosine, sine, gain, block, weights=(), rows=0, heads=0, columns=0, collective_id=None):
    width, length = gain.shape[0], cosine.shape[1]
    full = lambda shape: pl.BlockSpec(shape, lambda i: (0,) * len(shape))
    outs = [
        ((length, width), bf16),
        ((length, width), bf16),
        ((length, width), bf16),
        ((width, length), bf16),
        ((width, length), f32),
        ((width, length), f32),
        ((8, length), f32),
    ]
    scratch = [pltpu.VMEM((width, length), bf16), pltpu.VMEM((width, length), bf16)]
    out_specs = [full(shape) for shape, _ in outs]
    share = bool(weights)
    if share:
        wide = heads * width
        more = [((rows, wide), bf16), ((wide, 2 * columns), bf16), ((wide, wide), bf16)]
        outs, out_specs = outs + more, out_specs + [ANY] * 3
        scratch += [
            pltpu.VMEM((length, width), bf16), pltpu.VMEM((weights[2].shape[0] // 2, wide), bf16),
            pltpu.VMEM(weights[3].shape, bf16), DMA((group,)), DMA((heads,)), DMA((2,)), DMA((2, 1)),
        ]
        scratch += Gather.scratch(2) + Deal.scratch(2)
    else:
        outs, out_specs = outs + [((length, width), bf16)], out_specs + [full((length, width))]
    return pl.pallas_call(
        functools.partial(forward_kernel, block, share),
        grid=(length // block,),
        in_specs=[SMEM] + [full(a.shape) for a in (qkv, cosine, sine, gain)] + [ANY] * len(weights),
        out_specs=out_specs,
        out_shape=[jax.ShapeDtypeStruct(shape, kind) for shape, kind in outs],
        scratch_shapes=scratch,
        compiler_params=pltpu.CompilerParams(
            dimension_semantics=("arbitrary",), vmem_limit_bytes=56 * 2**20,
            collective_id=collective_id, has_side_effects=share,
        ),
        cost_estimate=busy,
        name="attention_forward",
    )(lam, qkv, cosine, sine, gain, *weights)


def backward_kernel(
    block, share, lam_ref, q_ref, k_ref, v_ref, kt_ref, o1_ref, o2_ref, lse_ref, datt_ref,
    cos_ref, sin_ref, gain_ref, *refs,
):
    if share:
        (left_ref, right_ref, cargo_in, given_ref, rows_ref, normed), refs = refs[:6], refs[6:]
    dqkv_ref, dgain_ref, dlam_ref, *refs = refs
    if share:
        (part_ref, theirs_ref, cargo_out, taken_ref, back_ref, head_ref), refs = refs[:6], refs[6:]
    dmix_ref, dmixt_ref, delta_ref, dqt_ref, *refs = refs
    if share:
        cargo_sem, held_sem, held, part_sum, *refs = refs
        copy = pltpu.make_async_copy(normed, held, held_sem.at[0])
        run, back_sems, refs = Scatter(sum_few_z, *refs[:7]), refs[7:10], refs[10:]
        back = Restore(rows_ref, back_ref, lambda n: n >= 0, natural(rows_ref.shape[1] // 2), *back_sems)
        part_cargo = Cargo([(part_ref, theirs_ref)], [], cargo_sem.at[1])
        cargo = Cargo(
            [(for_partner(cargo_in, cargo_out.shape[0]), cargo_out)], [(given_ref, taken_ref)], cargo_sem.at[0]
        )
    step = pl.program_id(0)
    blocks = pl.num_programs(0)
    width = v_ref.shape[1]
    half = width // 2
    length = q_ref.shape[0]
    scale = half ** -0.5
    lam = lam_ref[0]
    used = lam_ref[1] > 0.0

    @pl.when(step == 0)
    def _():
        if share:
            greet_all()


            def meanwhile():
                run.begin(left_ref, right_ref, 0)
                cargo.start()
                back.start()
                copy.start()

            collect(meanwhile, datt_ref, *refs)
        source = refs[0] if share else datt_ref
        dgain_ref[...] = jnp.zeros_like(dgain_ref)
        dlam_ref[...] = jnp.zeros_like(dlam_ref)
        dqt_ref[...] = jnp.zeros_like(dqt_ref)

        def prepare(index, carry):
            cols = pl.ds(pl.multiple_of(index * block, block), block)
            first, second = o1_ref[:, cols], o2_ref[:, cols]
            mixed = first - lam * second
            factor = lax.rsqrt(jnp.mean(mixed * mixed, axis=0, keepdims=True) + norm_eps)
            upstream = source[cols, :].astype(f32).T * (1.0 - lam_init)
            dgain_ref[...] += jnp.sum(upstream * mixed * factor, axis=1, keepdims=True)
            scaled = upstream * gain_ref[...]
            dmixed = factor * scaled - mixed * (factor * factor * factor) * jnp.mean(
                scaled * mixed, axis=0, keepdims=True
            )
            low = dmixed.astype(bf16)
            back = low.astype(f32)
            dmixt_ref[:, cols] = low
            dmix_ref[cols, :] = back.T.astype(bf16)
            along_second = jnp.sum(back * second, axis=0, keepdims=True)
            delta_ref[0:1, cols] = jnp.sum(back * first, axis=0, keepdims=True)
            delta_ref[1:2, cols] = -lam * along_second
            dlam_ref[...] -= jnp.sum(along_second, axis=1, keepdims=True)
            return carry

        lax.fori_loop(0, length // block, prepare, 0)

    if share:
        for i in range(3):

            @pl.when(step == i + 1)
            def _(i=i):
                run.halve_all(i, part_sum)
                if i == 0:
                    back.middle()
                if i == 2:
                    part_ref[...] = part_sum[...].astype(bf16)
                    part_cargo.start()

    own = pl.ds(pl.multiple_of(step * block, block), block)
    key_ids = lax.broadcasted_iota(jnp.int32, (block, block), 0)
    query_ids = lax.broadcasted_iota(jnp.int32, (block, block), 1)
    keys = k_ref[own, :]
    keys_t = kt_ref[:, own]
    values = v_ref[own, :]

    def visit(index, state, diagonal):
        dkeys, dvalues = state
        cols = pl.ds(pl.multiple_of(index * block, block), block)
        queries = q_ref[cols, :]
        dmix = dmix_ref[cols, :]
        dprob = dot(values, dmixt_ref[:, cols])
        new_keys = []
        blend = None
        for part in range(2):
            lo, hi = part * half, (part + 1) * half
            scores = dot(keys[:, lo:hi], queries[:, lo:hi], 1, 1) * (scale * log2e)
            weights = jnp.exp2(scores - lse_ref[pl.ds(part, 1), cols])
            if diagonal:
                weights = jnp.where(key_ids <= query_ids, weights, 0.0)
            delta = delta_ref[part : part + 1, cols]
            if part == 0:
                blend = weights
                dscore = (weights * (dprob - delta)).astype(bf16)
            else:
                blend = blend - lam * weights
                dscore = (weights * (-lam * dprob - delta)).astype(bf16)
            new_keys.append(dkeys[part] + dot(dscore, queries[:, lo:hi]))
            dqt_ref[lo:hi, cols] += dot(keys_t[lo:hi], dscore)
        dvalues = dvalues + dot(blend.astype(bf16), dmix)
        return tuple(new_keys), dvalues

    start = (
        (jnp.zeros((block, half), f32), jnp.zeros((block, half), f32)),
        jnp.zeros((block, width), f32),
    )
    state = visit(step, start, True)
    dkeys, dvalues = lax.fori_loop(
        step + 1, blocks, lambda index, now: visit(index, now, False), state
    )
    both = jnp.where(used, jnp.concatenate(dkeys, axis=1).T * scale, 0.0)
    dqkv_ref[own, width : 2 * width] = (
        rotated(both, cos_ref[:, own], sin_ref[:, own], True).T.astype(bf16)
    )
    dqkv_ref[own, 2 * width : 3 * width] = jnp.where(used, dvalues, 0.0).astype(bf16)

    dqkv_ref[own, 0:width] = (
        rotated(jnp.where(used, dqt_ref[:, own] * scale, 0.0), cos_ref[:, own], sin_ref[:, own], True).T.astype(bf16)
    )
    if share:

        @pl.when(step == blocks - 1)
        def _():
            copy.wait()
            weight_grads(held, dqkv_ref, head_ref)
            run.finish()
            cargo.finish()
            part_cargo.finish()
            back.finish()


def collect(meanwhile, grad_ref, out_ref, send_sem, recv_sem, local_sem):
    me = place()[0]
    rows = grad_ref.shape[0]
    width = out_ref.shape[1]
    heads = grad_ref.shape[1] // width
    active = is_active(me, heads)

    def move(head, number):
        src = grad_ref.at[:, pl.ds(pl.multiple_of(head * width, width), width)]
        dst = out_ref.at[pl.ds(pl.multiple_of(number * rows, rows), rows)]
        return src, dst

    def send(head, number):
        src, dst = move(head, number)
        return remote(src, dst, send_sem.at[head], recv_sem.at[number], owner_of(head, heads))

    def keep():
        src, dst = move(head_of(me, heads), me)
        return pltpu.make_async_copy(src, dst, local_sem.at[0])

    def begin(head, carry):
        pl.when(owner_of(head, heads) != me)(lambda: send(head, me).start())
        return carry

    def taken(number, carry):
        pl.when(active & (number != me))(lambda: send(0, number).wait_recv())
        return carry

    def sent(head, carry):
        pl.when(owner_of(head, heads) != me)(lambda: send(head, me).wait_send())
        return carry

    lax.fori_loop(0, heads, begin, 0)
    pl.when(active)(lambda: keep().start())
    meanwhile()
    lax.fori_loop(0, group, taken, 0)
    pl.when(active)(lambda: keep().wait())
    lax.fori_loop(0, heads, sent, 0)


def backward_attention(lam, q, k, v, kt, o1, o2, lse, datt, cosine, sine, gain, block, extra=None, collective_id=None):
    length, width = q.shape
    full = lambda shape: pl.BlockSpec(shape, lambda i: (0,) * len(shape))
    arrays = (q, k, v, kt, o1, o2, lse, datt, cosine, sine, gain)
    outs = [((length, 3 * width), bf16), ((width, 1), f32), ((1, 1), f32)]
    share = collective_id is not None
    more, more_out, more_in, more_specs, out_specs = [], [], [], [], []
    if share:
        rows, wide = datt.shape
        grads, part = extra[2], (wide // group, wide)
        more_in, more_specs = list(extra), [full(a.shape) for a in extra[:2]] + [ANY] * 4
        more_out = [
            jax.ShapeDtypeStruct(part, bf16), jax.ShapeDtypeStruct(part, bf16),
            jax.ShapeDtypeStruct((grads.shape[0] // 2, grads.shape[1]), bf16),
            jax.ShapeDtypeStruct((rows, wide), bf16),
            jax.ShapeDtypeStruct((2, part[0], extra[4].shape[1] // 2 * group), bf16),
            jax.ShapeDtypeStruct((wide, 3 * width), bf16),
        ]
        out_specs = [full(part), ANY, ANY, ANY, ANY, full((wide, 3 * width))]
        more = [DMA((2, 2, 2)), DMA((1,)), pltpu.VMEM(extra[5].shape, bf16), pltpu.VMEM(part, f32)] + Scatter.scratch(*part) + Restore.scratch(2) + [
            pltpu.VMEM((length, width), bf16), DMA((wide // width,)), DMA((group,)), DMA((1,)),
        ]
    return pl.pallas_call(
        functools.partial(backward_kernel, block, share),
        grid=(length // block,),
        in_specs=[SMEM] + [full(a.shape) for a in arrays] + more_specs,
        out_specs=[full(shape) for shape, _ in outs] + out_specs,
        out_shape=[jax.ShapeDtypeStruct(shape, kind) for shape, kind in outs] + more_out,
        scratch_shapes=[
            pltpu.VMEM((length, width), bf16),
            pltpu.VMEM((width, length), bf16),
            pltpu.VMEM((8, length), f32),
            pltpu.VMEM((width, length), f32),
        ] + more,
        compiler_params=pltpu.CompilerParams(
            dimension_semantics=("arbitrary",), vmem_limit_bytes=56 * 2**20,
            collective_id=collective_id, has_side_effects=share,
        ),
        cost_estimate=busy,
        name="attention_backward",
    )(lam, *arrays, *more_in)


def rms_parts(value):
    return lax.rsqrt(jnp.mean(value * value, axis=-1, keepdims=True) + norm_eps)


def rms_back(value, factor, gain, upstream):
    scaled = upstream * gain
    mean = jnp.mean(scaled * value, axis=-1, keepdims=True)
    grad = factor * scaled - value * (factor * factor * factor) * mean
    return grad, jnp.sum(upstream * value * factor, axis=0)


def cube_body(
    block_input, positions, needle, cotangent, norm_gain1, w_query, w_key, w_value,
    lam_q1, lam_k1, lam_q2, lam_k2, sub_gain, w_out, norm_gain2, w_gate, w_up, w_down,
):
    rows, width = block_input.shape[1:]
    heads, half = lam_q1.shape
    head_width = sub_gain.shape[0]
    hidden = w_gate.shape[1]
    depth = w_query.shape[0]
    length = rows * group
    columns = hidden // group
    me, cube = place()
    my_head = head_of(me, heads)
    used = is_active(me, heads)
    active = used.astype(f32)
    here = jnp.broadcast_to(positions[0], (1, 8, rows))
    tokens_low, normed_all, places, w_head, w_d = first_exchange(
        block_input[0], here, norm_gain1[None], (w_query, w_key, w_value, w_down),
        heads, head_width, columns, 0,
    )
    tokens = tokens_low.astype(f32)
    factor1 = rms_parts(tokens)
    upstream = cotangent[0].astype(f32) * needle[0].astype(f32)[:, None]
    upstream_low = upstream.astype(bf16)
    places = places[:, 0].reshape(length)

    inv_freq = jnp.exp(-math.log(10000.0) * jnp.arange(half // 2, dtype=f32) / (half // 2))
    angles = inv_freq[:, None] * places.astype(f32)[None, :]
    cosine, sine = jnp.cos(angles), jnp.sin(angles)
    lam_vals, lam_pull = jax.vjp(lambdas, lam_q1, lam_k1, lam_q2, lam_k2)
    lam_mine = jnp.stack([lax.dynamic_index_in_dim(lam_vals, my_head, 0, False), active])
    gain_col = sub_gain[:, None]
    block = 4 * rows

    q, k, v, kt, o1, o2, lse, attended, w_gates, w_o = forward_attention(
        lam_mine, w_head, cosine, sine, gain_col, block,
        (w_gate, w_up, w_out, normed_all), rows, heads, columns, 1,
    )
    resid = tokens + dot(attended, w_o)
    factor2 = rms_parts(resid)
    normed_two = (resid * factor2 * norm_gain2).astype(bf16)
    grad_low, two_all, grad_all = second_exchange(normed_two, upstream_low, 2)

    both = dot(two_all, w_gates)
    gate, upper = both[:, :columns], both[:, columns:]
    grad_inner = dot(grad_all, w_d)
    sigma = jax.nn.sigmoid(gate)
    silu = gate * sigma
    inner = (silu * upper).astype(bf16)
    gate_low = (grad_inner * upper * sigma * (1.0 + gate * (1.0 - sigma))).astype(bf16)
    upper_low = (grad_inner * silu).astype(bf16)
    grad_two, ffn_out, gate_grads, down_grads, gate_theirs = scatter(
        gate_low, upper_low, w_gates, inner, w_d, two_all, grad_all, 3
    )
    output_low = (resid + ffn_out).astype(bf16)

    grad_resid_two, gain_two = rms_back(resid, factor2, norm_gain2, grad_two)
    grad_resid = grad_low.astype(f32) + grad_resid_two
    resid_low = grad_resid.astype(bf16)
    grad_att = dot(resid_low, w_o, 1, 1).astype(bf16)

    def combine(mine, theirs):
        part = theirs.shape[0]
        mine = lax.dynamic_slice_in_dim(mine, cube * part, part, 0)
        return (mine.astype(f32) + theirs.astype(f32)).astype(bf16)

    dqkv, dgain, dlam, out_part, out_theirs, down_theirs, output_back, gate_back, head_grads = backward_attention(
        lam_mine, q, k, v, kt, o1, o2, lse, grad_att, cosine, sine, gain_col, block,
        (attended, resid_low, down_grads, output_low, combine(gate_grads, gate_theirs), normed_all), 4,
    )
    hot = jax.nn.one_hot(my_head, heads, dtype=f32)
    lines = width // head_width
    small = jnp.concatenate([
        jnp.zeros((lines, head_width), f32), gain_two.reshape(lines, head_width),
        jnp.where(used, dgain[:, 0], 0.0)[None],
        jnp.pad(jnp.where(used, hot * dlam[0, 0], 0.0), (0, head_width - heads))[None],
    ])
    small = jnp.pad(small, ((0, -small.shape[0] % 8), (0, 0)))
    out_sum = (out_part.astype(f32) + out_theirs.astype(f32)).astype(bf16)
    down_back, head_back, out_pair, small, input_back = last_exchange(
        (
            dqkv, w_head, tokens_low, norm_gain1[None], grad_resid, head_grads, small,
            combine(down_grads, down_theirs), out_sum,
        ),
        heads, head_width, columns, 5,
    )
    output = output_back[None]
    input_grad = input_back.astype(f32)[None]
    out_grads = jnp.where(me // 8 == cube, out_sum, out_pair).astype(f32)
    grads = [a.astype(f32) for a in (gate_back[0], gate_back[1], down_back[0])]
    grads += [head_back[i].astype(f32) for i in range(3)]
    gain_one = small[:lines].reshape(-1)
    gain_two = small[lines : 2 * lines].reshape(-1)
    sub_grad = small[2 * lines]
    lam_grads = lam_pull(small[2 * lines + 1, :heads])
    squares = sum(jnp.sum(g * g) for g in lam_grads)
    return (
        output, input_grad, gain_one, grads[3], grads[4], grads[5],
        lam_grads[0], lam_grads[1], lam_grads[2], lam_grads[3], sub_grad, out_grads, gain_two,
        grads[0], grads[1], grads[2], jnp.mean(lam_vals), jnp.sqrt(squares),
    )


def gather_rows(value):
    return lax.all_gather(value, "seq", axis=0, tiled=True)


def scatter_sum(value):
    return lax.psum_scatter(value, "seq", scatter_dimension=0, tiled=True)


def exchange(value):
    return lax.all_to_all(value, "seq", split_axis=0, concat_axis=0, tiled=True)


def plain_body(
    devices, block_input, positions, needle, cotangent, norm_gain1, w_query, w_key, w_value,
    lam_q1, lam_k1, lam_q2, lam_k2, sub_gain, w_out, norm_gain2, w_gate, w_up, w_down,
):
    rows, width = block_input.shape[1:]
    heads, half = lam_q1.shape
    head_width = sub_gain.shape[0]
    hidden = w_gate.shape[1]
    depth = w_query.shape[0]
    length = rows * devices
    columns = hidden // devices
    head_of = [d * heads // devices for d in range(devices)]
    owner_of = [max(d for d in range(devices) if head_of[d] == h) for h in range(heads)]
    me = lax.axis_index("seq")
    my_head = me * heads // devices
    active = ((me + 1) * heads // devices > my_head).astype(f32)

    tokens = block_input[0].astype(f32)
    factor1 = rms_parts(tokens)
    normed = (tokens * factor1 * norm_gain1).astype(bf16)
    normed_all = gather_rows(normed)
    places = gather_rows(positions[0])

    by_head = jnp.stack([w.reshape(depth, heads, head_width) for w in (w_query, w_key, w_value)], 2)
    by_head = by_head.reshape(depth, heads, 3 * head_width).transpose(1, 0, 2)
    w_head = exchange(by_head[jnp.array(head_of)]).reshape(width, 3 * head_width)

    w_o = gather_rows(w_out)
    grad_out = cotangent[0].astype(f32) * needle[0].astype(f32)[:, None]
    grad_low = grad_out.astype(bf16)
    grad_all = gather_rows(grad_low)

    ffn = jnp.stack([w.reshape(depth, devices, columns) for w in (w_gate, w_up, w_down)], 2)
    ffn = ffn.reshape(depth, devices, 3 * columns).transpose(1, 0, 2)
    w_ffn = exchange(ffn).reshape(width, 3 * columns)

    inv_freq = jnp.exp(-math.log(10000.0) * jnp.arange(half // 2, dtype=f32) / (half // 2))
    angles = inv_freq[:, None] * places.astype(f32)[None, :]
    cosine, sine = jnp.cos(angles), jnp.sin(angles)
    lam_vals, lam_pull = jax.vjp(lambdas, lam_q1, lam_k1, lam_q2, lam_k2)
    lam_mine = jnp.stack([lax.dynamic_index_in_dim(lam_vals, my_head, 0, False), active])
    gain_col = sub_gain[:, None]
    block = math.gcd(length, 512)

    qkv = dot(w_head, normed_all, 0, 1)
    q, k, v, kt, o1, o2, lse, att = forward_attention(
        lam_mine, qkv, cosine, sine, gain_col, block
    )
    att_rows = exchange(att.reshape(devices, rows, head_width))
    attended = jnp.concatenate([att_rows[d] for d in owner_of], axis=1)
    resid = tokens + dot(attended, w_o)
    factor2 = rms_parts(resid)
    normed_two = (resid * factor2 * norm_gain2).astype(bf16)
    two_all = gather_rows(normed_two)

    both = dot(two_all, w_ffn[:, : 2 * columns])
    gate, upper = both[:, :columns], both[:, columns:]
    grad_inner = dot(grad_all, w_ffn[:, 2 * columns :])
    sigma = jax.nn.sigmoid(gate)
    silu = gate * sigma
    inner = (silu * upper).astype(bf16)
    gate_low = (grad_inner * upper * sigma * (1.0 + gate * (1.0 - sigma))).astype(bf16)
    upper_low = (grad_inner * silu).astype(bf16)
    gates_low = jnp.concatenate([gate_low, upper_low], axis=1)
    grad_two = scatter_sum(dot(gates_low, w_ffn[:, : 2 * columns], 1, 1).astype(bf16)).astype(f32)
    ffn_out = scatter_sum(dot(inner, w_ffn[:, 2 * columns :], 1, 1).astype(bf16)).astype(f32)
    output = (resid + ffn_out).astype(bf16)[None]

    grad_resid_two, gain_two = rms_back(resid, factor2, norm_gain2, grad_two)
    grad_resid = grad_out + grad_resid_two
    resid_low = grad_resid.astype(bf16)
    grad_att = dot(resid_low, w_o, 1, 1).astype(bf16)
    pieces = jnp.stack(
        [grad_att[:, h * head_width : (h + 1) * head_width] for h in head_of], axis=0
    )
    datt = exchange(pieces).reshape(length, head_width)

    dqkv, dgain, dlam = backward_attention(
        lam_mine, q, k, v, kt, o1, o2, lse, datt, cosine, sine, gain_col, block
    )
    partial = (dot(dqkv, w_head, 1, 1) * active).astype(bf16)
    grad_normed = scatter_sum(partial).astype(f32)
    grad_tokens, gain_one = rms_back(tokens, factor1, norm_gain1, grad_normed)
    input_grad = (grad_resid + grad_tokens)[None]

    def settle(value):
        other = lax.ppermute(value, "batch", [(0, 1), (1, 0)])
        return value.astype(f32) + other.astype(f32)

    ffn_grads = jnp.concatenate(
        [dot(two_all, gates_low, 0, 0), dot(grad_all, inner, 0, 0)], axis=1
    ).astype(bf16)
    ffn_grads = settle(exchange(ffn_grads.reshape(devices, depth, 3 * columns)))
    ffn_grads = ffn_grads.reshape(devices, depth, 3, columns).transpose(2, 1, 0, 3)
    ffn_grads = ffn_grads.reshape(3, depth, hidden)

    head_grads = dot(normed_all, dqkv, 0, 0).astype(bf16)
    head_grads = settle(exchange(head_grads.reshape(devices, depth, 3 * head_width)))
    head_grads = jnp.stack([head_grads[d] for d in owner_of], axis=1)
    head_grads = head_grads.reshape(depth, heads, 3, head_width).transpose(2, 0, 1, 3)
    head_grads = head_grads.reshape(3, depth, width)

    out_grads = dot(attended, resid_low, 0, 0).astype(bf16)
    out_grads = settle(scatter_sum(out_grads))

    hot = jax.nn.one_hot(my_head, heads, dtype=f32) * active
    small = lax.psum(
        (gain_one, gain_two, dgain[:, 0] * active, hot * dlam[0, 0]), ("batch", "seq")
    )
    lam_grads = lam_pull(small[3])
    squares = sum(jnp.sum(g * g) for g in lam_grads)
    return (
        output, input_grad, small[0], head_grads[0], head_grads[1], head_grads[2],
        lam_grads[0], lam_grads[1], lam_grads[2], lam_grads[3], small[2], out_grads, small[1],
        ffn_grads[0], ffn_grads[1], ffn_grads[2], jnp.mean(lam_vals), jnp.sqrt(squares),
    )


def solution(mesh):
    rows = P("seq", None)
    in_specs = (
        P("batch", "seq", None), P("batch", "seq"), P("batch", "seq"), P("batch", "seq", None),
        P(), rows, rows, rows, P(), P(), P(), P(), P(), rows, P(), rows, rows, rows,
    )
    out_specs = (
        P("batch", "seq", None), P("batch", "seq", None), P(), rows, rows, rows,
        P(), P(), P(), P(), P(), rows, P(), rows, rows, rows, P(), P(),
    )
    if mesh.shape["seq"] == group and mesh.shape["batch"] == 2:
        body = cube_body
    else:
        body = functools.partial(plain_body, mesh.shape["seq"])
    return jax.shard_map(body, mesh=mesh, in_specs=in_specs, out_specs=out_specs, check_vma=False)
```
